32 devices in a mesh: seq: 16 (over z, y, core), tp: 2 (over x).
Axes of the slice: x: 2, y: 2, z: 4, core: 2. Of those that a mesh axis runs over, the one named last changes fastest.
Arguments:
- state: bfloat16 [2048, 1024], P('seq', 'tp'), may hold values from -16 to 16
- cotangent: float32 [2048, 1024], P('seq', 'tp'), may hold values from -40 to 40
- norm_gain: float32 [1024], replicated, may hold values from 0.5 to 1.5
- w_query: bfloat16 [1024, 1024], P(None, 'tp'), may hold values from -8 to 8
- w_key: bfloat16 [1024, 1024], P(None, 'tp'), may hold values from -1 to 1
- w_value: bfloat16 [1024, 1024], P(None, 'tp'), may hold values from -0.1875 to 0.1875
- w_out: bfloat16 [1024, 1024], P('tp'), may hold values from -1.5 to 1.5
Outputs:
- adjoint: float32 [2048, 1024], P('seq', 'tp')
- residual: float32 [2048, 1024], P('seq', 'tp')
The draws below stay inside these ranges and needn't reach their ends.
All inputs are finite; a program needn't handle non-finite values.
Results may differ from the reference program's by a relative error of at most 0.025.
The reference program's roundings to bfloat16 on the way (of `normed`, `grad_out` and `grad_score`) count: a program that leaves them out, or rounds other values in their place, can miss the bound.
Values may be sent and summed in bfloat16 or wider, within the bound.
No kernel may reach another device: no remote copies, remote signals or barrier semaphores. Data moves between devices by JAX's collectives and lax.ppermute only.
A program may use at most 64 MiB of HBM per device.

```python
import math
import jax
import jax.numpy as jnp
from jax import lax

D = 1024
HEADS = 8
HD = 128
WIN = 1024
SSTEP = 4
TOK_DEV = 128
SEQ = 2048


def key_base(key):
    drawn = jax.random.truncated_normal(jax.random.fold_in(key, 31), -6.0, 6.0, (D, D), jnp.float32)
    return drawn / jnp.sqrt(jnp.float32(D))


def draw_w_key(key, part):
    return jnp.clip(key_base(key), -1.0, 1.0).astype(jnp.bfloat16)


def draw_w_query(key, part):
    drawn = jax.random.truncated_normal(jax.random.fold_in(key, 34), -6.0, 6.0, (D, D), jnp.float32) / jnp.sqrt(jnp.float32(D))
    return jnp.clip(drawn, -8.0, 8.0).astype(jnp.bfloat16)


def draw_state(key, part):
    drawn = jax.random.normal(jax.random.fold_in(key, 41), (SEQ, D), jnp.float32)
    return jnp.clip(drawn, -16.0, 16.0).astype(jnp.bfloat16)


def draw_cotangent(key, part):
    position = jnp.arange(SEQ, dtype=jnp.float32)[:, None] / (SEQ - 1)
    drawn = jax.random.normal(jax.random.fold_in(key, 53), (SEQ, D), jnp.float32) * 3.0 ** position
    return jnp.clip(drawn, -40.0, 40.0)


def shard_levels(stream_key, extent, pieces, least, top_value):
    level = 1.0
    for dim, blocks in pieces:
        draws = jax.random.uniform(jax.random.fold_in(jax.random.fold_in(stream_key, 6), dim), (blocks,), jnp.float32, least / len(pieces), top_value / len(pieces))
        level = level * jnp.repeat(jnp.exp(draws), extent[dim] // blocks).reshape((-1,) + (1,) * (len(extent) - 1 - dim))
    return level


def gaussian(key, dims, spread, reach, shards=(), kind=jnp.bfloat16):
    loudness = shard_levels(key, dims, shards, -0.22, 0.18) if shards else 1.0
    array = jax.random.normal(key, dims, jnp.float32) * spread * loudness
    return jnp.minimum(jnp.maximum(array, -reach), reach).astype(kind)


def setup_inputs(seed: int = 0) -> dict:
    seeds = jax.random.split(jax.random.key(seed), 8)
    return {
        "state": draw_state(jax.random.fold_in(seeds[7], 71), 0),
        "cotangent": draw_cotangent(jax.random.fold_in(seeds[7], 71), 0),
        "norm_gain": jnp.clip(1.0 + 0.1 * jax.random.normal(seeds[2], (D,), jnp.float32), 0.5, 1.5),
        "w_query": draw_w_query(jax.random.fold_in(seeds[7], 71), 0),
        "w_key": draw_w_key(jax.random.fold_in(seeds[7], 71), 0),
        "w_value": gaussian(seeds[5], (D, D), D ** -0.5, 0.1875, ((1, 2),)),
        "w_out": gaussian(seeds[6], (D, D), 16 ** -0.5, 1.5, ((0, 2),)),
    }


EPSILON = 1e-05

def lower_solve(factor, values):
    result = []
    for index_i in range(values.shape[0]):
        running = values[index_i]
        for index_j in range(index_i):
            running = running - factor[index_i, index_j] * result[index_j]
        result.append(running / factor[index_i, index_i])
    return jnp.stack(result)

def upper_solve(factor, values):
    length_n = values.shape[0]
    result = [None] * length_n
    for index_i in range(length_n - 1, -1, -1):
        running = values[index_i]
        for index_j in range(index_i + 1, length_n):
            running = running - factor[index_j, index_i] * result[index_j]
        result[index_i] = running / factor[index_i, index_i]
    return jnp.stack(result)

def combine_coefficients(gram_matrix, right_side):
    factor = jnp.linalg.cholesky(gram_matrix)
    return upper_solve(factor, lower_solve(factor, right_side))

def window_valid(first_row, block_rows):
    query_pos = first_row + jnp.arange(block_rows, dtype=jnp.int32)
    key_pos = first_row - WIN // 2 + jnp.arange(block_rows + WIN, dtype=jnp.int32)
    distance = jnp.abs(key_pos[None, :] - query_pos[:, None])
    return (distance <= WIN // 2) & (key_pos[None, :] >= 0) & (key_pos[None, :] < SEQ)

def window_probs(queries_blk, keys_win, valid):
    scores = jnp.einsum('rhe,khe->hrk', queries_blk.astype(jnp.float32), keys_win.astype(jnp.float32)) * (1.0 / math.sqrt(HD))
    row_peak = lax.optimization_barrier(jnp.max(jnp.where(valid[None], scores, -jnp.inf), axis=2, keepdims=True))
    raw_weights = jnp.where(valid[None], jnp.exp(scores - row_peak), 0.0)
    return raw_weights / lax.optimization_barrier(jnp.sum(raw_weights, axis=2, keepdims=True))

def reference(state, cotangent, norm_gain, w_query, w_key, w_value, w_out):
    half_span = WIN // 2
    block_rows = TOK_DEV
    block_count = SEQ // block_rows
    scale_factor = 1.0 / math.sqrt(HD)
    state_full = state.astype(jnp.float32)
    inverse = lax.rsqrt(lax.optimization_barrier(jnp.mean(state_full * state_full, axis=1, keepdims=True)) + EPSILON)
    normed = (state_full * inverse * norm_gain[None, :]).astype(jnp.bfloat16)
    queries = jnp.dot(normed.astype(jnp.float32), w_query.astype(jnp.float32), preferred_element_type=jnp.float32).astype(jnp.bfloat16).reshape(SEQ, HEADS, HD)
    key_vecs = jnp.dot(normed.astype(jnp.float32), w_key.astype(jnp.float32), preferred_element_type=jnp.float32).astype(jnp.bfloat16).reshape(SEQ, HEADS, HD)
    values = jnp.dot(normed.astype(jnp.float32), w_value.astype(jnp.float32), preferred_element_type=jnp.float32).astype(jnp.bfloat16).reshape(SEQ, HEADS, HD)
    padding = ((half_span, half_span), (0, 0), (0, 0))
    keys_pad = jnp.pad(key_vecs, padding)
    values_pad = jnp.pad(values, padding)
    starts = jnp.arange(block_count, dtype=jnp.int32) * block_rows

    def forward_block(first_row):
        queries_blk = lax.dynamic_slice_in_dim(queries, first_row, block_rows, 0)
        keys_win = lax.dynamic_slice_in_dim(keys_pad, first_row, block_rows + WIN, 0)
        values_win = lax.dynamic_slice_in_dim(values_pad, first_row, block_rows + WIN, 0)
        attn_probs = window_probs(queries_blk, keys_win, window_valid(first_row, block_rows))
        return jnp.einsum('hrk,khe->rhe', attn_probs.astype(jnp.bfloat16).astype(jnp.float32), values_win.astype(jnp.float32))
    attended = lax.map(forward_block, starts).reshape(SEQ, HEADS, HD)

    def cell_vjp(vector):
        grad_out = jnp.dot(vector.astype(jnp.bfloat16).astype(jnp.float32), w_out.T.astype(jnp.float32), preferred_element_type=jnp.float32).astype(jnp.bfloat16).reshape(SEQ, HEADS, HD)
        row_corr = lax.optimization_barrier(jnp.sum(grad_out.astype(jnp.float32) * attended, axis=2))

        def block_step(carry, first_row):
            key_acc, value_acc = carry
            queries_blk = lax.dynamic_slice_in_dim(queries, first_row, block_rows, 0)
            keys_win = lax.dynamic_slice_in_dim(keys_pad, first_row, block_rows + WIN, 0)
            values_win = lax.dynamic_slice_in_dim(values_pad, first_row, block_rows + WIN, 0)
            attn_probs = window_probs(queries_blk, keys_win, window_valid(first_row, block_rows))
            out_blk = lax.dynamic_slice_in_dim(grad_out, first_row, block_rows, 0).astype(jnp.float32)
            corr_blk = lax.dynamic_slice_in_dim(row_corr, first_row, block_rows, 0).T
            grad_prob = jnp.einsum('rhe,khe->hrk', out_blk, values_win.astype(jnp.float32))
            grad_score = (scale_factor * attn_probs * (grad_prob - corr_blk[:, :, None])).astype(jnp.bfloat16).astype(jnp.float32)
            grad_query = jnp.einsum('hrk,khe->rhe', grad_score, keys_win.astype(jnp.float32)).astype(jnp.bfloat16)
            key_part = jnp.einsum('hrk,rhe->khe', grad_score, queries_blk.astype(jnp.float32))
            value_part = jnp.einsum('hrk,rhe->khe', attn_probs.astype(jnp.bfloat16).astype(jnp.float32), out_blk)
            key_acc = lax.dynamic_update_slice_in_dim(key_acc, lax.dynamic_slice_in_dim(key_acc, first_row, block_rows + WIN, 0) + key_part, first_row, 0)
            value_acc = lax.dynamic_update_slice_in_dim(value_acc, lax.dynamic_slice_in_dim(value_acc, first_row, block_rows + WIN, 0) + value_part, first_row, 0)
            return ((key_acc, value_acc), grad_query)
        zeros_pad = jnp.zeros((SEQ + WIN, HEADS, HD), jnp.float32)
        (key_acc, value_acc), grad_query = lax.scan(block_step, (zeros_pad, zeros_pad), starts)
        grad_query = grad_query.reshape(SEQ, D)
        grad_key = key_acc[half_span:half_span + SEQ].astype(jnp.bfloat16).reshape(SEQ, D)
        grad_value = value_acc[half_span:half_span + SEQ].astype(jnp.bfloat16).reshape(SEQ, D)
        summed = jnp.dot(grad_query.astype(jnp.float32), w_query.T.astype(jnp.float32), preferred_element_type=jnp.float32)
        summed = summed + jnp.dot(grad_key.astype(jnp.float32), w_key.T.astype(jnp.float32), preferred_element_type=jnp.float32)
        summed = summed + jnp.dot(grad_value.astype(jnp.float32), w_value.T.astype(jnp.float32), preferred_element_type=jnp.float32)
        return inverse * (norm_gain[None, :] * summed)
    krylov = [cotangent]
    for index_n in range(SSTEP):
        krylov.append(cell_vjp(krylov[-1]))
    differences = [krylov[index_n] - krylov[index_n + 1] for index_n in range(SSTEP)]
    gram_matrix = jnp.stack([jnp.stack([jnp.sum(differences[index_a] * differences[index_b]) for index_b in range(SSTEP)]) for index_a in range(SSTEP)])
    right_side = jnp.stack([jnp.sum(differences[index_a] * cotangent) for index_a in range(SSTEP)])
    coefficients = combine_coefficients(gram_matrix, right_side)
    adjoint = coefficients[0] * krylov[0]
    residual = cotangent - coefficients[0] * differences[0]
    for index_n in range(1, SSTEP):
        adjoint = adjoint + coefficients[index_n] * krylov[index_n]
        residual = residual - coefficients[index_n] * differences[index_n]
    return (adjoint, residual)
```

```python
import functools
import math

import jax
import jax.numpy as jnp
from jax import lax
from jax.experimental import pallas as pl
from jax.experimental.pallas import tpu as pltpu
from jax.sharding import PartitionSpec as P

HD = 128
WIN = 1024
SSTEP = 4
EPSILON = 1e-05
PAD = 16
NEG = -1e30
SCALE = 1.0 / math.sqrt(HD)
NT = (((1,), (1,)), ((), ()))
NN = (((1,), (0,)), ((), ()))
F32 = jnp.float32
BF16 = jnp.bfloat16


def mm(a, b, dims=NN):
    return lax.dot_general(a, b, dims, preferred_element_type=F32)


def col(h):
    return slice(h * HD, (h + 1) * HD)


def kernel_call(body, outs, ins, n_smem=0, scratch=(), flops=10**8, limit=24 << 20):
    in_specs = [pl.BlockSpec(memory_space=pltpu.SMEM)] * n_smem
    in_specs += [pl.BlockSpec(memory_space=pltpu.VMEM)] * (len(ins) - n_smem)
    moved = sum(math.prod(a.shape) * a.dtype.itemsize for a in list(ins) + list(outs))
    return pl.pallas_call(
        body,
        out_shape=[jax.ShapeDtypeStruct(o.shape, o.dtype) for o in outs],
        in_specs=in_specs,
        out_specs=[pl.BlockSpec(memory_space=pltpu.VMEM)] * len(outs),
        scratch_shapes=list(scratch),
        compiler_params=pltpu.CompilerParams(vmem_limit_bytes=limit),
        cost_estimate=pl.CostEstimate(flops=flops, bytes_accessed=moved, transcendentals=0),
    )(*ins)


def sds(*shape, dtype=F32):
    return jax.ShapeDtypeStruct(shape, dtype)


def parts_of(x):
    hi = x.astype(BF16).astype(F32)
    rest = x - hi
    mid = rest.astype(BF16).astype(F32)
    low = (rest - mid).astype(BF16).astype(F32)
    return [hi, mid, low]


def pack_rows(out_ref, rows, heads, columns):
    lane = lax.broadcasted_iota(jnp.int32, (rows, HD), 1)
    mat = jnp.zeros((rows, HD), F32)
    for i, c in enumerate(columns):
        mat = jnp.where(lane == i, c, mat)
    pieces = parts_of(mat.T)
    sub = lax.broadcasted_iota(jnp.int32, (PAD, rows), 0)
    for h in range(heads):
        tile = jnp.zeros((PAD, rows), F32)
        for kind in range(len(columns) // heads):
            r = kind * heads + h
            for i, piece in enumerate(pieces):
                tile = jnp.where(sub == 3 * kind + i, piece[r : r + 1, :], tile)
        out_ref[rows : rows + PAD, col(h)] = tile.astype(BF16)


def unpack_row(slots, rows, h, kind):
    pieces = []
    for s in slots:
        t = s[rows : rows + PAD, col(h)].astype(F32)
        k = 3 * kind
        pieces.append(t[k : k + 1] + t[k + 1 : k + 2] + t[k + 2 : k + 3])
    return jnp.concatenate(pieces, axis=1)


def project_body(x_ref, gain_ref, wq_ref, wk_ref, wv_ref, wo_ref, q_ref, kv_ref, go_ref, inv_ref):
    tps, _, rows, cols = x_ref.shape
    width = wq_ref.shape[1]
    xs = [x_ref[t, 0].astype(F32) for t in range(tps)]
    total = jnp.zeros((rows, 1), F32)
    for x in xs:
        total = total + jnp.sum(x * x, axis=1, keepdims=True)
    inverse = lax.rsqrt(total / (tps * cols) + EPSILON)
    inv_ref[...] = jnp.broadcast_to(inverse, inv_ref.shape)
    normed = jnp.concatenate(
        [
            (x * inverse * gain_ref[:, t * cols : (t + 1) * cols]).astype(BF16)
            for t, x in enumerate(xs)
        ],
        axis=1,
    )
    kv_ref[:, :width] = mm(normed, wk_ref[...]).astype(BF16)
    kv_ref[:, width:] = mm(normed, wv_ref[...]).astype(BF16)
    q_ref[...] = mm(normed, wq_ref[...]).astype(BF16)
    cot = jnp.concatenate([x_ref[t, 1] for t in range(tps)], axis=1)
    go_ref[...] = mm(cot, wo_ref[...], NT).astype(BF16)


def mask_of(start_ref, rows, slots, half):
    own = start_ref[0] + lax.broadcasted_iota(jnp.int32, (rows, rows), 0)
    lane = lax.broadcasted_iota(jnp.int32, (rows, rows), 1)
    pieces = []
    for b in range(slots):
        pieces.append(jnp.abs(start_ref[b] + lane - own) <= half)
    return pieces


def stats_body(slots, half, start_ref, *refs):
    kv = refs[:slots]
    q_ref, go_ref = refs[slots : slots + 2]
    p_ref, att_ref, packed_ref, kw_ref, vw_ref = refs[slots + 2 :]
    rows, width = q_ref.shape
    heads = width // HD
    for b in range(slots):
        kw_ref[b * rows : (b + 1) * rows, :] = kv[b][:, :width]
        vw_ref[b * rows : (b + 1) * rows, :] = kv[b][:, width:]
    masks = mask_of(start_ref, rows, slots, half)
    packed_ref[:rows, :] = go_ref[...]
    lse, corr = [], []
    for h in range(heads):
        s = mm(q_ref[:, col(h)], kw_ref[:, col(h)], NT) * SCALE
        s = jnp.concatenate(
            [
                jnp.where(masks[b], s[:, b * rows : (b + 1) * rows], NEG)
                for b in range(slots)
            ],
            axis=1,
        )
        peak = jnp.max(s, axis=1, keepdims=True)
        raw = jnp.exp(s - peak)
        total = jnp.sum(raw, axis=1, keepdims=True)
        probs = raw / total
        p_ref[h] = probs
        att = mm(probs.astype(BF16), vw_ref[:, col(h)])
        att_ref[:, col(h)] = att
        lse.append(peak + jnp.log(total))
        corr.append(jnp.sum(go_ref[:, col(h)].astype(F32) * att, axis=1, keepdims=True))
    pack_rows(packed_ref, rows, heads, corr + lse)


def scores_t_body(slots, half, start_ref, *refs):
    qs = refs[:slots]
    kv_ref = refs[slots]
    st_ref, qw_ref = refs[slots + 1 :]
    rows, width = qs[0].shape
    for b in range(slots):
        qw_ref[b * rows : (b + 1) * rows, :] = qs[b][...]
    masks = mask_of(start_ref, rows, slots, half)
    for h in range(width // HD):
        s = mm(kv_ref[:, col(h)], qw_ref[:, col(h)], NT) * SCALE
        for b in range(slots):
            st_ref[h, :, b * rows : (b + 1) * rows] = jnp.where(
                masks[b], s[:, b * rows : (b + 1) * rows], NEG
            )


def query_body(packed_ref, att_ref, p_ref, kw_ref, vw_ref, wq_ref, part_ref):
    rows, width = att_ref.shape
    grads = []
    for h in range(width // HD):
        go = packed_ref[:rows, col(h)]
        corr = jnp.sum(go.astype(F32) * att_ref[:, col(h)], axis=1, keepdims=True)
        gp = mm(go, vw_ref[:, col(h)], NT)
        gs = (SCALE * p_ref[h] * (gp - corr)).astype(BF16)
        grads.append(mm(gs, kw_ref[:, col(h)]).astype(BF16))
    part_ref[...] = mm(jnp.concatenate(grads, axis=1), wq_ref[...], NT)


def key_body(slots, first, *refs):
    got = refs[:slots]
    pt_in, kv_ref, qw_ref, wk_ref, wv_ref, partq_ref = refs[slots : slots + 6]
    if first:
        part_ref, send_ref, pt_ref, gow_ref = refs[slots + 6 :]
    else:
        part_ref, send_ref, gow_ref = refs[slots + 6 :]
        pt_ref = pt_in
    rows = kv_ref.shape[0]
    width = qw_ref.shape[1]
    for b in range(slots):
        gow_ref[b * rows : (b + 1) * rows, :] = got[b][:rows, :]
    gks, gvs = [], []
    for h in range(width // HD):
        corr = unpack_row(got, rows, h, 0)
        if first:
            pt = jnp.exp(pt_in[h] - unpack_row(got, rows, h, 1))
            pt_ref[h] = pt
        else:
            pt = pt_ref[h]
        go = gow_ref[:, col(h)]
        gp = mm(kv_ref[:, width + h * HD : width + (h + 1) * HD], go, NT)
        gs = (SCALE * pt * (gp - corr)).astype(BF16)
        gks.append(mm(gs, qw_ref[:, col(h)]).astype(BF16))
        gvs.append(mm(pt.astype(BF16), go).astype(BF16))
    part = partq_ref[...] + mm(jnp.concatenate(gks, axis=1), wk_ref[...], NT)
    part = part + mm(jnp.concatenate(gvs, axis=1), wv_ref[...], NT)
    part_ref[...] = part
    send_ref[...] = part.astype(BF16)


def combine_body(where_ref, part_ref, recv_ref, inv_ref, gain_ref, wo_ref, att_ref, *refs):
    kry_ref, packed_ref, vec_ref = refs
    rows, width = att_ref.shape
    cols = kry_ref.shape[1]
    inverse = inv_ref[:, :1]
    vec = inverse * (gain_ref[...] * (part_ref[...] + recv_ref[...].astype(F32)))
    vec_ref[...] = vec
    off = pl.multiple_of(where_ref[0], HD)
    kry_ref[...] = vec_ref[:, pl.ds(off, cols)]
    go = mm(vec.astype(BF16), wo_ref[...], NT).astype(BF16)
    packed_ref[:rows, :] = go
    corr = [
        jnp.sum(go[:, col(h)].astype(F32) * att_ref[:, col(h)], axis=1, keepdims=True)
        for h in range(width // HD)
    ]
    pack_rows(packed_ref, rows, width // HD, corr)


def gram_body(where_ref, part_ref, recv_ref, inv_ref, gain_ref, *refs):
    kry = refs[:SSTEP]
    last_ref, sums_ref, vec_ref = refs[SSTEP:]
    rows, cols = last_ref.shape
    inverse = inv_ref[:, :1]
    vec_ref[...] = inverse * (gain_ref[...] * (part_ref[...] + recv_ref[...].astype(F32)))
    off = pl.multiple_of(where_ref[0], HD)
    last_ref[...] = vec_ref[:, pl.ds(off, cols)]
    all_k = list(kry) + [last_ref]
    count = SSTEP * (SSTEP + 1) // 2 + SSTEP
    acc = [jnp.zeros((8, HD), F32) for _ in range(count)]
    for r in range(0, rows, 8):
        for c in range(0, cols, HD):
            ks = [k[r : r + 8, c : c + HD] for k in all_k]
            ds = [ks[i] - ks[i + 1] for i in range(SSTEP)]
            i = 0
            for a in range(SSTEP):
                for b in range(a + 1):
                    acc[i] = acc[i] + ds[a] * ds[b]
                    i += 1
            for a in range(SSTEP):
                acc[i] = acc[i] + ds[a] * ks[0]
                i += 1
    sub = lax.broadcasted_iota(jnp.int32, sums_ref.shape, 0)
    out = jnp.zeros(sums_ref.shape, F32)
    for i in range(count):
        out = jnp.where(sub == i, jnp.sum(acc[i], axis=0, keepdims=True), out)
    sums_ref[...] = out


def solve(gram, right):
    n = len(right)
    low = [[None] * n for _ in range(n)]
    for i in range(n):
        for j in range(i + 1):
            run = gram[i][j]
            for k in range(j):
                run = run - low[i][k] * low[j][k]
            low[i][j] = jnp.sqrt(run) if i == j else run / low[j][j]
    mid = []
    for i in range(n):
        run = right[i]
        for j in range(i):
            run = run - low[i][j] * mid[j]
        mid.append(run / low[i][i])
    out = [None] * n
    for i in range(n - 1, -1, -1):
        run = mid[i]
        for j in range(i + 1, n):
            run = run - low[j][i] * out[j]
        out[i] = run / low[i][i]
    return out


def finish_body(sums_ref, *refs):
    kry = refs[: SSTEP + 1]
    adj_ref, res_ref = refs[SSTEP + 1 :]
    total = jnp.sum(sums_ref[...], axis=0)
    vals = jnp.sum(total, axis=1, keepdims=True)
    idx = 0
    gram = [[None] * SSTEP for _ in range(SSTEP)]
    for a in range(SSTEP):
        for b in range(a + 1):
            gram[a][b] = vals[idx : idx + 1, :]
            idx += 1
    right = [vals[idx + a : idx + a + 1, :] for a in range(SSTEP)]
    coef = solve(gram, right)
    ks = [k[...] for k in kry]
    adj = coef[0] * ks[0]
    res = ks[0] - coef[0] * (ks[0] - ks[1])
    for i in range(1, SSTEP):
        adj = adj + coef[i] * ks[i]
        res = res - coef[i] * (ks[i] - ks[i + 1])
    adj_ref[...] = adj
    res_ref[...] = res


def swap_partner(c, d, odd):
    return c + d if (c // d) % 2 == odd else c - d


def on_device(state, cotangent, norm_gain, w_query, w_key, w_value, w_out):
    rows, cols = state.shape
    width = w_query.shape[1]
    heads = width // HD
    half = WIN // 2
    seq = lax.axis_size("seq")
    tps = lax.axis_size("tp")
    chips = seq // 2
    reach = (half + rows - 1) // rows
    chip_reach = (reach + 1) // 2
    me = lax.axis_index("seq")
    chip, core = me // 2, me % 2
    hops = [(d, odd) for d in range(1, chip_reach + 1) for odd in (1, 0)]
    ids = [chip]
    for d, odd in hops:
        ids.append(jnp.where((chip // d) % 2 == odd, chip + d, chip - d))
    starts = []
    for k in (core, 1 - core):
        for q in ids:
            starts.append(
                jnp.where((q >= 0) & (q < chips), (2 * q + k) * rows, -(1 << 24))
            )
    starts = jnp.stack(starts).astype(jnp.int32)
    slots = 2 * len(ids)
    nwin = slots * rows
    gain = norm_gain[None, :]
    where = (lax.axis_index("tp") * cols).astype(jnp.int32)[None]

    def swap_core(x):
        return lax.ppermute(x, "seq", [(i, i ^ 1) for i in range(seq)])

    def fetch(x):
        got = []
        for d, odd in hops:
            pairs = []
            for c in range(chips):
                q = swap_partner(c, d, odd)
                if 0 <= q < chips:
                    pairs += [(2 * c, 2 * q), (2 * c + 1, 2 * q + 1)]
            got.append(lax.ppermute(x, "seq", pairs))
        mine = [x] + got
        return mine + [swap_core(y) for y in mine]

    both = jnp.stack([state, cotangent.astype(BF16)])
    both = lax.all_gather(both, "tp", axis=0, tiled=False)
    q_own, kv_own, go0, inv = kernel_call(
        project_body,
        [
            sds(rows, width, dtype=BF16),
            sds(rows, 2 * width, dtype=BF16),
            sds(rows, width, dtype=BF16),
            sds(rows, HD),
        ],
        [both, gain, w_query, w_key, w_value, w_out],
    )
    kv_slots = fetch(kv_own)
    q_slots = fetch(q_own)
    probs, att, packed, k_win, v_win = kernel_call(
        functools.partial(stats_body, slots, half),
        [
            sds(heads, rows, nwin),
            sds(rows, width),
            sds(rows + PAD, width, dtype=BF16),
            sds(nwin, width, dtype=BF16),
            sds(nwin, width, dtype=BF16),
        ],
        [starts] + kv_slots + [q_own, go0],
        n_smem=1,
    )
    probs_t, q_win = kernel_call(
        functools.partial(scores_t_body, slots, half),
        [sds(heads, rows, nwin), sds(nwin, width, dtype=BF16)],
        [starts] + q_slots + [kv_own],
        n_smem=1,
    )
    krylov = [cotangent]
    for n in range(SSTEP):
        got = fetch(packed)
        (part_q,) = kernel_call(
            query_body,
            [sds(rows, tps * cols)],
            [packed, att, probs, k_win, v_win, w_query],
        )
        outs = [sds(rows, tps * cols), sds(rows, tps * cols, dtype=BF16)]
        if n == 0:
            outs.append(sds(heads, rows, nwin))
        res = kernel_call(
            functools.partial(key_body, slots, n == 0),
            outs,
            got + [probs_t, kv_own, q_win, w_key, w_value, part_q],
            scratch=[pltpu.VMEM((nwin, width), BF16)],
        )
        part, send = res[:2]
        if n == 0:
            probs_t = res[2]
        k = 1
        while True:
            recv = lax.ppermute(send, "tp", [(i, i ^ k) for i in range(tps)])
            k *= 2
            if k >= tps:
                break
            part = part + recv.astype(F32)
            send = part.astype(BF16)
        if n < SSTEP - 1:
            kry, packed = kernel_call(
                combine_body,
                [sds(rows, cols), sds(rows + PAD, width, dtype=BF16)],
                [where, part, recv, inv, gain, w_out, att],
                n_smem=1,
                scratch=[pltpu.VMEM((rows, tps * cols), F32)],
            )
            krylov.append(kry)
        else:
            last, sums = kernel_call(
                gram_body,
                [sds(rows, cols), sds(PAD, HD)],
                [where, part, recv, inv, gain] + krylov,
                n_smem=1,
                scratch=[pltpu.VMEM((rows, tps * cols), F32)],
            )
            krylov.append(last)
    ranks = seq * tps
    sums = lax.all_to_all(
        jnp.broadcast_to(sums[None], (ranks,) + sums.shape), ("seq", "tp"), 0, 0
    )
    adjoint, residual = kernel_call(
        finish_body,
        [sds(rows, cols), sds(rows, cols)],
        [sums] + krylov,
    )
    return (adjoint, residual)


def solution(mesh):
    in_specs = (
        P("seq", "tp"),
        P("seq", "tp"),
        P(),
        P(None, "tp"),
        P(None, "tp"),
        P(None, "tp"),
        P("tp", None),
    )
    out_specs = (P("seq", "tp"), P("seq", "tp"))
    return jax.shard_map(
        on_device, mesh=mesh, in_specs=in_specs, out_specs=out_specs, check_vma=False
    )
```

```python
import functools
import math

import jax
import jax.numpy as jnp
from jax import lax
from jax.experimental import pallas as pl
from jax.experimental.pallas import tpu as pltpu
from jax.sharding import PartitionSpec as P

HD = 128
WIN = 1024
SSTEP = 4
EPSILON = 1e-05
PAD = 16
NEG = -1e30
SCALE = 1.0 / math.sqrt(HD)
NT = (((1,), (1,)), ((), ()))
NN = (((1,), (0,)), ((), ()))
F32 = jnp.float32
BF16 = jnp.bfloat16


def mm(a, b, dims=NN):
    return lax.dot_general(a, b, dims, preferred_element_type=F32)


def col(h):
    return slice(h * HD, (h + 1) * HD)


def kernel_call(body, outs, ins, scratch=(), flops=10**8, limit=12 << 20):
    in_specs = [pl.BlockSpec(memory_space=pltpu.VMEM)] * len(ins)
    moved = sum(math.prod(a.shape) * a.dtype.itemsize for a in list(ins) + list(outs))
    return pl.pallas_call(
        body,
        out_shape=[jax.ShapeDtypeStruct(o.shape, o.dtype) for o in outs],
        in_specs=in_specs,
        out_specs=[pl.BlockSpec(memory_space=pltpu.VMEM)] * len(outs),
        scratch_shapes=list(scratch),
        compiler_params=pltpu.CompilerParams(vmem_limit_bytes=limit),
        cost_estimate=pl.CostEstimate(flops=flops, bytes_accessed=moved, transcendentals=0),
    )(*ins)


def sds(*shape, dtype=F32):
    return jax.ShapeDtypeStruct(shape, dtype)


def parts_of(x):
    hi = x.astype(BF16).astype(F32)
    rest = x - hi
    mid = rest.astype(BF16).astype(F32)
    low = (rest - mid).astype(BF16).astype(F32)
    return [hi, mid, low]


def pack_rows(out_ref, rows, heads, columns):
    lane = lax.broadcasted_iota(jnp.int32, (rows, HD), 1)
    mat = jnp.zeros((rows, HD), F32)
    for i, c in enumerate(columns):
        mat = jnp.where(lane == i, c, mat)
    pieces = parts_of(mat.T)
    sub = lax.broadcasted_iota(jnp.int32, (PAD, rows), 0)
    for h in range(heads):
        tile = jnp.zeros((PAD, rows), F32)
        for kind in range(len(columns) // heads):
            r = kind * heads + h
            for i, piece in enumerate(pieces):
                tile = jnp.where(sub == 3 * kind + i, piece[r : r + 1, :], tile)
        out_ref[rows : rows + PAD, col(h)] = tile.astype(BF16)


def unpack_row(slots, rows, h, kind):
    pieces = []
    for s in slots:
        t = s[rows : rows + PAD, col(h)].astype(F32)
        k = 3 * kind
        pieces.append(t[k : k + 1] + t[k + 1 : k + 2] + t[k + 2 : k + 3])
    return jnp.concatenate(pieces, axis=1)


def slot_starts(half, rows):
    me, seq = lax.axis_index("seq"), lax.axis_size("seq")
    chip, core = me // 2, me % 2
    ids = [chip]
    for d, odd in hops_of(half, rows):
        ids.append(jnp.where((chip // d) % 2 == odd, chip + d, chip - d))
    out = []
    for k in (core, 1 - core):
        for q in ids:
            inside = (q >= 0) & (q < seq // 2)
            out.append(jnp.where(inside, (2 * q + k) * rows, -(1 << 24)))
    return out


def hops_of(half, rows):
    reach = (half + rows - 1) // rows
    return [(d, odd) for d in range(1, (reach + 1) // 2 + 1) for odd in (1, 0)]


def masks_of(half, rows):
    starts = slot_starts(half, rows)
    sub = lax.broadcasted_iota(jnp.int32, (rows, rows), 0)
    lane = lax.broadcasted_iota(jnp.int32, (rows, rows), 1)
    return [jnp.abs(lane - sub + (st - starts[0])) <= half for st in starts]


def masked(s, masks):
    rows = s.shape[0]
    pieces = [
        jnp.where(m, s[:, b * rows : (b + 1) * rows], NEG) for b, m in enumerate(masks)
    ]
    return jnp.concatenate(pieces, axis=1)


def feature_slices(tps, cols):
    me = lax.axis_index("tp")
    return [pl.ds(pl.multiple_of(((me + k) % tps) * cols, HD), cols) for k in range(tps)]


def round_body(x_ref, o_ref):
    o_ref[...] = x_ref[...].astype(o_ref.dtype)


def norm_body(tps, *refs):
    xs = refs[:tps]
    gain_ref, normed_ref, inv_ref = refs[tps:]
    rows, cols = xs[0].shape
    vals = [x[...].astype(F32) for x in xs]
    total = jnp.zeros((rows, 1), F32)
    for x in vals:
        total = total + jnp.sum(x * x, axis=1, keepdims=True)
    inverse = lax.rsqrt(total / (tps * cols) + EPSILON)
    inv_ref[...] = jnp.broadcast_to(inverse, inv_ref.shape)
    for x, at in zip(vals, feature_slices(tps, cols)):
        normed_ref[:, at] = (x * inverse * gain_ref[:, at]).astype(BF16)


def kv_body(blocks, *refs):
    xs = refs[:blocks]
    wk_ref, wv_ref, kv_ref = refs[blocks:]
    rows = xs[0].shape[0]
    width = wk_ref.shape[1]
    x = jnp.concatenate([r[...] for r in xs], axis=0)
    kv_ref[:, :width] = mm(x, wk_ref[...]).astype(BF16)
    kv_ref[:, width:] = mm(x, wv_ref[...]).astype(BF16)


def q_body(blocks, tps, *refs):
    xs = refs[:blocks]
    cots = refs[blocks : blocks + tps]
    wq_ref, wo_ref, q_ref, go_ref, cot_ref = refs[blocks + tps :]
    x = jnp.concatenate([r[...] for r in xs], axis=0)
    q_ref[...] = mm(x, wq_ref[...]).astype(BF16)
    for c, at in zip(cots, feature_slices(tps, cots[0].shape[1])):
        cot_ref[:, at] = c[...]
    go_ref[...] = mm(cot_ref[...], wo_ref[...], NT).astype(BF16)


def stats_body(half, kvm_ref, kvo_ref, q_ref, go_ref, p_ref, att_ref, packed_ref):
    rows, width = go_ref.shape
    heads = width // HD
    near = kvm_ref.shape[0]
    masks = masks_of(half, rows)
    packed_ref[:rows, :] = go_ref[...]
    lse, corr = [], []
    for h in range(heads):
        q = q_ref[:rows, col(h)]
        s = jnp.concatenate(
            [mm(q, kvm_ref[:, col(h)], NT), mm(q, kvo_ref[:, col(h)], NT)], axis=1
        )
        s = masked(s * SCALE, masks)
        peak = jnp.max(s, axis=1, keepdims=True)
        raw = jnp.exp(s - peak)
        total = jnp.sum(raw, axis=1, keepdims=True)
        probs = raw / total
        p_ref[h] = probs
        low = probs.astype(BF16)
        att = mm(low[:, :near], kvm_ref[:, col(heads + h)])
        att = att + mm(low[:, near:], kvo_ref[:, col(heads + h)])
        att_ref[:, col(h)] = att
        lse.append(peak + jnp.log(total))
        corr.append(jnp.sum(go_ref[:, col(h)].astype(F32) * att, axis=1, keepdims=True))
    pack_rows(packed_ref, rows, heads, corr + lse)


def scores_t_body(half, qm_ref, qo_ref, kv_ref, st_ref):
    rows = st_ref.shape[1]
    masks = masks_of(half, rows)
    for h in range(st_ref.shape[0]):
        k = kv_ref[:rows, col(h)]
        s = jnp.concatenate(
            [mm(k, qm_ref[:, col(h)], NT), mm(k, qo_ref[:, col(h)], NT)], axis=1
        )
        st_ref[h] = masked(s * SCALE, masks)


def query_body(packed_ref, att_ref, p_ref, kvm_ref, kvo_ref, wq_ref, part_ref):
    rows, width = att_ref.shape
    heads = width // HD
    near = kvm_ref.shape[0]
    grads = []
    for h in range(heads):
        go = packed_ref[:rows, col(h)]
        corr = jnp.sum(go.astype(F32) * att_ref[:, col(h)], axis=1, keepdims=True)
        v = col(heads + h)
        gp = jnp.concatenate([mm(go, kvm_ref[:, v], NT), mm(go, kvo_ref[:, v], NT)], axis=1)
        gs = (SCALE * p_ref[h] * (gp - corr)).astype(BF16)
        gq = mm(gs[:, :near], kvm_ref[:, col(h)]) + mm(gs[:, near:], kvo_ref[:, col(h)])
        grads.append(gq.astype(BF16))
    part_ref[...] = mm(jnp.concatenate(grads, axis=1), wq_ref[...], NT)


def key_body(slots, first, *refs):
    got = refs[:slots]
    pt_in, kv_ref, qm_ref, qo_ref, wk_ref, wv_ref, partq_ref = refs[slots : slots + 7]
    if first:
        part_ref, send_ref, pt_ref, gow_ref = refs[slots + 7 :]
    else:
        part_ref, send_ref, gow_ref = refs[slots + 7 :]
        pt_ref = pt_in
    rows, width = got[0].shape[0] - PAD, got[0].shape[1]
    heads = width // HD
    near = qm_ref.shape[0]
    for b in range(slots):
        gow_ref[b * rows : (b + 1) * rows, :] = got[b][:rows, :]
    gks, gvs = [], []
    for h in range(heads):
        corr = unpack_row(got, rows, h, 0)
        if first:
            pt = jnp.exp(pt_in[h] - unpack_row(got, rows, h, 1))
            pt_ref[h] = pt
        else:
            pt = pt_ref[h]
        go = gow_ref[:, col(h)]
        gp = mm(kv_ref[:rows, col(heads + h)], go, NT)
        gs = (SCALE * pt * (gp - corr)).astype(BF16)
        gk = mm(gs[:, :near], qm_ref[:, col(h)]) + mm(gs[:, near:], qo_ref[:, col(h)])
        gks.append(gk.astype(BF16))
        gvs.append(mm(pt.astype(BF16), go).astype(BF16))
    part = partq_ref[...] + mm(jnp.concatenate(gks, axis=1), wk_ref[...], NT)
    part = part + mm(jnp.concatenate(gvs, axis=1), wv_ref[...], NT)
    part_ref[...] = part
    send_ref[...] = part.astype(BF16)


def combine_body(part_ref, recv_ref, inv_ref, gain_ref, wo_ref, att_ref, *refs):
    kry_ref, packed_ref, vec_ref = refs
    rows, width = att_ref.shape
    cols = kry_ref.shape[1]
    inverse = inv_ref[:, :1]
    vec = inverse * (gain_ref[...] * (part_ref[...] + recv_ref[...].astype(F32)))
    vec_ref[...] = vec
    off = pl.multiple_of(lax.axis_index("tp") * cols, HD)
    kry_ref[...] = vec_ref[:, pl.ds(off, cols)]
    go = mm(vec.astype(BF16), wo_ref[...], NT).astype(BF16)
    packed_ref[:rows, :] = go
    corr = [
        jnp.sum(go[:, col(h)].astype(F32) * att_ref[:, col(h)], axis=1, keepdims=True)
        for h in range(width // HD)
    ]
    pack_rows(packed_ref, rows, width // HD, corr)


def gram_body(part_ref, recv_ref, inv_ref, gain_ref, *refs):
    kry = refs[:SSTEP]
    last_ref, sums_ref, vec_ref = refs[SSTEP:]
    rows, cols = last_ref.shape
    inverse = inv_ref[:, :1]
    vec_ref[...] = inverse * (gain_ref[...] * (part_ref[...] + recv_ref[...].astype(F32)))
    off = pl.multiple_of(lax.axis_index("tp") * cols, HD)
    last_ref[...] = vec_ref[:, pl.ds(off, cols)]
    all_k = list(kry) + [last_ref]
    count = SSTEP * (SSTEP + 1) // 2 + SSTEP
    acc = [jnp.zeros((8, HD), F32) for _ in range(count)]
    for r in range(0, rows, 8):
        for c in range(0, cols, HD):
            ks = [k[r : r + 8, c : c + HD] for k in all_k]
            ds = [ks[i] - ks[i + 1] for i in range(SSTEP)]
            i = 0
            for a in range(SSTEP):
                for b in range(a + 1):
                    acc[i] = acc[i] + ds[a] * ds[b]
                    i += 1
            for a in range(SSTEP):
                acc[i] = acc[i] + ds[a] * ks[0]
                i += 1
    sub = lax.broadcasted_iota(jnp.int32, (PAD, HD), 0)
    out = jnp.zeros((PAD, HD), F32)
    for i in range(count):
        out = jnp.where(sub == i, jnp.sum(acc[i], axis=0, keepdims=True), out)
    for r in range(sums_ref.shape[0]):
        sums_ref[r] = out


def solve(gram, right):
    n = len(right)
    low = [[None] * n for _ in range(n)]
    for i in range(n):
        for j in range(i + 1):
            run = gram[i][j]
            for k in range(j):
                run = run - low[i][k] * low[j][k]
            low[i][j] = jnp.sqrt(run) if i == j else run / low[j][j]
    mid = []
    for i in range(n):
        run = right[i]
        for j in range(i):
            run = run - low[i][j] * mid[j]
        mid.append(run / low[i][i])
    out = [None] * n
    for i in range(n - 1, -1, -1):
        run = mid[i]
        for j in range(i + 1, n):
            run = run - low[j][i] * out[j]
        out[i] = run / low[i][i]
    return out


def finish_body(sums_ref, *refs):
    kry = refs[: SSTEP + 1]
    adj_ref, res_ref = refs[SSTEP + 1 :]
    total = jnp.sum(sums_ref[...], axis=0)
    vals = jnp.sum(total, axis=1, keepdims=True)
    idx = 0
    gram = [[None] * SSTEP for _ in range(SSTEP)]
    for a in range(SSTEP):
        for b in range(a + 1):
            gram[a][b] = vals[idx : idx + 1, :]
            idx += 1
    right = [vals[idx + a : idx + a + 1, :] for a in range(SSTEP)]
    coef = solve(gram, right)
    ks = [k[...] for k in kry]
    adj = coef[0] * ks[0]
    res = ks[0] - coef[0] * (ks[0] - ks[1])
    for i in range(1, SSTEP):
        adj = adj + coef[i] * ks[i]
        res = res - coef[i] * (ks[i] - ks[i + 1])
    adj_ref[...] = adj
    res_ref[...] = res


def swap_partner(c, d, odd):
    return c + d if (c // d) % 2 == odd else c - d


def on_device(state, cotangent, norm_gain, w_query, w_key, w_value, w_out):
    rows, cols = state.shape
    width = w_query.shape[1]
    heads = width // HD
    half = WIN // 2
    seq = lax.axis_size("seq")
    tps = lax.axis_size("tp")
    chips = seq // 2
    hops = hops_of(half, rows)
    blocks = 1 + len(hops)
    slots = 2 * blocks
    nwin = slots * rows
    gain = norm_gain[None, :]

    def swap_core(x):
        return lax.ppermute(x, "seq", [(i, i ^ 1) for i in range(seq)])

    def tp_blocks(x):
        return [x] + [
            lax.ppermute(x, "tp", [((i + k) % tps, i) for i in range(tps)]) for k in range(1, tps)
        ]

    def fetch(x):
        got = [x]
        for d, odd in hops:
            pairs = []
            for c in range(chips):
                q = swap_partner(c, d, odd)
                if 0 <= q < chips:
                    pairs += [(2 * c, 2 * q), (2 * c + 1, 2 * q + 1)]
            got.append(lax.ppermute(x, "seq", pairs))
        return got

    states = tp_blocks(state)
    (cot_low,) = kernel_call(round_body, [sds(rows, cols, dtype=BF16)], [cotangent])
    cots = tp_blocks(cot_low)
    normed, inv = kernel_call(
        functools.partial(norm_body, tps),
        [sds(rows, tps * cols, dtype=BF16), sds(rows, HD)],
        states + [gain],
    )
    near = fetch(normed)
    (kv_mine,) = kernel_call(
        functools.partial(kv_body, blocks),
        [sds(blocks * rows, 2 * width, dtype=BF16)],
        near + [w_key, w_value],
    )
    kv_other = swap_core(kv_mine)
    q_mine, go0 = kernel_call(
        functools.partial(q_body, blocks, tps),
        [sds(blocks * rows, width, dtype=BF16), sds(rows, width, dtype=BF16)],
        near + cots + [w_query, w_out],
        scratch=[pltpu.VMEM((rows, tps * cols), BF16)],
    )
    q_other = swap_core(q_mine)
    probs, att, packed = kernel_call(
        functools.partial(stats_body, half),
        [
            sds(heads, rows, nwin),
            sds(rows, width),
            sds(rows + PAD, width, dtype=BF16),
        ],
        [kv_mine, kv_other, q_mine, go0],
    )
    (probs_t,) = kernel_call(
        functools.partial(scores_t_body, half),
        [sds(heads, rows, nwin)],
        [q_mine, q_other, kv_mine],
    )
    krylov = [cotangent]
    ranks = seq * tps
    for n in range(SSTEP):
        got = fetch(packed)
        got = got + [swap_core(x) for x in got]
        (part_q,) = kernel_call(
            query_body,
            [sds(rows, tps * cols)],
            [packed, att, probs, kv_mine, kv_other, w_query],
        )
        outs = [sds(rows, tps * cols), sds(rows, tps * cols, dtype=BF16)]
        if n == 0:
            outs.append(sds(heads, rows, nwin))
        res = kernel_call(
            functools.partial(key_body, slots, n == 0),
            outs,
            got + [probs_t, kv_mine, q_mine, q_other, w_key, w_value, part_q],
            scratch=[pltpu.VMEM((nwin, width), BF16)],
        )
        part, send = res[:2]
        if n == 0:
            probs_t = res[2]
        k = 1
        while True:
            recv = lax.ppermute(send, "tp", [(i, i ^ k) for i in range(tps)])
            k *= 2
            if k >= tps:
                break
            part = part + recv.astype(F32)
            send = part.astype(BF16)
        if n < SSTEP - 1:
            kry, packed = kernel_call(
                combine_body,
                [sds(rows, cols), sds(rows + PAD, width, dtype=BF16)],
                [part, recv, inv, gain, w_out, att],
                scratch=[pltpu.VMEM((rows, tps * cols), F32)],
            )
            krylov.append(kry)
        else:
            last, sums = kernel_call(
                gram_body,
                [sds(rows, cols), sds(ranks, PAD, HD)],
                [part, recv, inv, gain] + krylov,
                scratch=[pltpu.VMEM((rows, tps * cols), F32)],
            )
            krylov.append(last)
    sums = lax.all_to_all(sums, ("seq", "tp"), 0, 0)
    adjoint, residual = kernel_call(
        finish_body,
        [sds(rows, cols), sds(rows, cols)],
        [sums] + krylov,
    )
    return (adjoint, residual)


def solution(mesh):
    in_specs = (
        P("seq", "tp"),
        P("seq", "tp"),
        P(),
        P(None, "tp"),
        P(None, "tp"),
        P(None, "tp"),
        P("tp", None),
    )
    out_specs = (P("seq", "tp"), P("seq", "tp"))
    return jax.shard_map(
        on_device, mesh=mesh, in_specs=in_specs, out_specs=out_specs, check_vma=False
    )
```

```python
import functools
import math

import jax
import jax.numpy as jnp
from jax import lax
from jax.experimental import pallas as pl
from jax.experimental.pallas import tpu as pltpu
from jax.sharding import PartitionSpec as P


HD = 128
WIN = 1024
SSTEP = 4
EPSILON = 1e-05
PAD = 16
NEG = -1e30
SCALE = 1.0 / math.sqrt(HD)
NT = (((1,), (1,)), ((), ()))
NN = (((1,), (0,)), ((), ()))
F32 = jnp.float32
BF16 = jnp.bfloat16


def mm(a, b, dims=NN):
    return lax.dot_general(a, b, dims, preferred_element_type=F32)


def col(h):
    return slice(h * HD, (h + 1) * HD)


def kernel_call(body, outs, ins, scratch=(), hbm=0, flops=10**8, limit=12 << 20):
    in_specs = [pl.BlockSpec(memory_space=pltpu.HBM)] * hbm
    in_specs += [pl.BlockSpec(memory_space=pltpu.VMEM)] * (len(ins) - hbm)
    moved = sum(math.prod(a.shape) * a.dtype.itemsize for a in list(ins) + list(outs))
    return pl.pallas_call(
        body,
        out_shape=[jax.ShapeDtypeStruct(o.shape, o.dtype) for o in outs],
        in_specs=in_specs,
        out_specs=[pl.BlockSpec(memory_space=pltpu.VMEM)] * len(outs),
        scratch_shapes=list(scratch),
        compiler_params=pltpu.CompilerParams(vmem_limit_bytes=limit),
        cost_estimate=pl.CostEstimate(flops=flops, bytes_accessed=moved, transcendentals=0),
    )(*ins)


def sds(*shape, dtype=F32):
    return jax.ShapeDtypeStruct(shape, dtype)


def parts_of(x):
    hi = x.astype(BF16).astype(F32)
    rest = x - hi
    mid = rest.astype(BF16).astype(F32)
    low = (rest - mid).astype(BF16).astype(F32)
    return [hi, mid, low]


def pack_rows(out_ref, rows, heads, columns):
    lane = lax.broadcasted_iota(jnp.int32, (rows, HD), 1)
    mat = jnp.zeros((rows, HD), F32)
    for i, c in enumerate(columns):
        mat = jnp.where(lane == i, c, mat)
    pieces = parts_of(mat.T)
    sub = lax.broadcasted_iota(jnp.int32, (PAD, rows), 0)
    for h in range(heads):
        tile = jnp.zeros((PAD, rows), F32)
        for kind in range(len(columns) // heads):
            r = kind * heads + h
            for i, piece in enumerate(pieces):
                tile = jnp.where(sub == 3 * kind + i, piece[r : r + 1, :], tile)
        out_ref[rows : rows + PAD, col(h)] = tile.astype(BF16)


def unpack_row(slots, rows, h, kind):
    pieces = []
    for s in slots:
        t = s[rows : rows + PAD, col(h)].astype(F32)
        k = 3 * kind
        pieces.append(t[k : k + 1] + t[k + 1 : k + 2] + t[k + 2 : k + 3])
    return jnp.concatenate(pieces, axis=1)


def slot_starts(half, rows):
    me, seq = lax.axis_index("seq"), lax.axis_size("seq")
    chip, core = me // 2, me % 2
    ids = [chip]
    for d, odd in hops_of(half, rows):
        ids.append(jnp.where((chip // d) % 2 == odd, chip + d, chip - d))
    out = []
    for k in (core, 1 - core):
        for q in ids:
            inside = (q >= 0) & (q < seq // 2)
            out.append(jnp.where(inside, (2 * q + k) * rows, -(1 << 24)))
    return out


def hops_of(half, rows):
    reach = (half + rows - 1) // rows
    return [(d, odd) for odd in (1, 0) for d in range(1, (reach + 1) // 2 + 1)]


def masks_of(half, rows):
    starts = slot_starts(half, rows)
    sub = lax.broadcasted_iota(jnp.int32, (rows, rows), 0)
    lane = lax.broadcasted_iota(jnp.int32, (rows, rows), 1)
    return [jnp.abs(lane - sub + (st - starts[0])) <= half for st in starts]


def masked(s, masks):
    rows = s.shape[0]
    pieces = [
        jnp.where(m, s[:, b * rows : (b + 1) * rows], NEG) for b, m in enumerate(masks)
    ]
    return jnp.concatenate(pieces, axis=1)


def feature_slices(tps, cols):
    me = lax.axis_index("tp")
    return [pl.ds(pl.multiple_of(((me + k) % tps) * cols, HD), cols) for k in range(tps)]


def prep_body(cot_in, state_in, gain_in, wq_in, wk_in, wv_in, wo_in, *refs):
    cot_low, outs, cot_ref, sems = refs[0], refs[1:7], refs[7], refs[8]
    sources = [state_in, gain_in, wq_in, wk_in, wv_in, wo_in]
    copies = [pltpu.make_async_copy(cot_in, cot_ref, sems.at[0])]
    for i, (src, dst) in enumerate(zip(sources, outs)):
        copies.append(pltpu.make_async_copy(src, dst, sems.at[i + 1]))
    for c in copies:
        c.start()
    copies[0].wait()
    cot_low[...] = cot_ref[...].astype(BF16)
    for c in copies[1:]:
        c.wait()


def kv_body(blocks, tps, *refs):
    xs = refs[: blocks * tps]
    gain_ref, wk_ref, wv_ref, kv_ref, normed_ref, inv_ref = refs[blocks * tps :]
    rows, cols = xs[0].shape
    width = wk_ref.shape[1]
    at = feature_slices(tps, cols)
    for b in range(blocks):
        vals = [x[...].astype(F32) for x in xs[b * tps : (b + 1) * tps]]
        total = jnp.zeros((rows, 1), F32)
        for x in vals:
            total = total + jnp.sum(x * x, axis=1, keepdims=True)
        inverse = lax.rsqrt(total / (tps * cols) + EPSILON)
        if b == 0:
            inv_ref[...] = jnp.broadcast_to(inverse, inv_ref.shape)
        for x, sl in zip(vals, at):
            normed_ref[b * rows : (b + 1) * rows, sl] = (x * inverse * gain_ref[:, sl]).astype(
                BF16
            )
    x = normed_ref[...]
    kv_ref[:, :width] = mm(x, wk_ref[...]).astype(BF16)
    kv_ref[:, width:] = mm(x, wv_ref[...]).astype(BF16)


def q_body(tps, *refs):
    cots = refs[:tps]
    normed_ref, wq_ref, wo_ref, q_ref, go_ref, cot_ref = refs[tps:]
    q_ref[...] = mm(normed_ref[...], wq_ref[...]).astype(BF16)
    for c, at in zip(cots, feature_slices(tps, cots[0].shape[1])):
        cot_ref[:, at] = c[...]
    go_ref[...] = mm(cot_ref[...], wo_ref[...], NT).astype(BF16)


def stats_body(half, kvm_ref, kvo_ref, q_ref, go_ref, p_ref, att_ref, packed_ref):
    rows, width = go_ref.shape
    heads = width // HD
    near = kvm_ref.shape[0]
    masks = masks_of(half, rows)
    packed_ref[:rows, :] = go_ref[...]
    lse, corr = [], []
    for h in range(heads):
        q = q_ref[:rows, col(h)]
        s = jnp.concatenate(
            [mm(q, kvm_ref[:, col(h)], NT), mm(q, kvo_ref[:, col(h)], NT)], axis=1
        )
        s = masked(s * SCALE, masks)
        peak = jnp.max(s, axis=1, keepdims=True)
        raw = jnp.exp(s - peak)
        total = jnp.sum(raw, axis=1, keepdims=True)
        probs = raw / total
        p_ref[h] = probs
        low = probs.astype(BF16)
        att = mm(low[:, :near], kvm_ref[:, col(heads + h)])
        att = att + mm(low[:, near:], kvo_ref[:, col(heads + h)])
        att_ref[:, col(h)] = att
        lse.append(peak + jnp.log(total))
        corr.append(jnp.sum(go_ref[:, col(h)].astype(F32) * att, axis=1, keepdims=True))
    pack_rows(packed_ref, rows, heads, corr + lse)


def split_slots(blocks):
    early = list(range(blocks - 1)) + list(range(blocks, 2 * blocks - 1))
    return early, [blocks - 1, 2 * blocks - 1]


def scores_t_body(half, qm_ref, qo_ref, kv_ref, early_ref, late_ref):
    rows = early_ref.shape[1]
    masks = masks_of(half, rows)
    cut = qm_ref.shape[0] - rows
    groups = split_slots(len(masks) // 2)
    for h in range(early_ref.shape[0]):
        k = kv_ref[:rows, col(h)]
        for ref, slots, part in zip(
            (early_ref, late_ref), groups, (slice(0, cut), slice(cut, cut + rows))
        ):
            s = jnp.concatenate(
                [mm(k, qm_ref[part, col(h)], NT), mm(k, qo_ref[part, col(h)], NT)], axis=1
            )
            ref[h] = masked(s * SCALE, [masks[i] for i in slots])


def query_body(packed_ref, att_ref, p_ref, kvm_ref, kvo_ref, wq_ref, part_ref):
    rows, width = att_ref.shape
    heads = width // HD
    near = kvm_ref.shape[0]
    grads = []
    for h in range(heads):
        go = packed_ref[:rows, col(h)]
        corr = jnp.sum(go.astype(F32) * att_ref[:, col(h)], axis=1, keepdims=True)
        v = col(heads + h)
        gp = jnp.concatenate([mm(go, kvm_ref[:, v], NT), mm(go, kvo_ref[:, v], NT)], axis=1)
        gs = (SCALE * p_ref[h] * (gp - corr)).astype(BF16)
        gq = mm(gs[:, :near], kvm_ref[:, col(h)]) + mm(gs[:, near:], kvo_ref[:, col(h)])
        grads.append(gq.astype(BF16))
    part_ref[...] = mm(jnp.concatenate(grads, axis=1), wq_ref[...], NT)


def key_terms(got, part, first, pt_in, pt_ref, kv_ref, qm_ref, qo_ref, gow_ref, h):
    rows, width = got[0].shape[0] - PAD, got[0].shape[1]
    near = part.stop - part.start
    corr = unpack_row(got, rows, h, 0)
    if first:
        pt = jnp.exp(pt_in[h] - unpack_row(got, rows, h, 1))
        pt_ref[h] = pt
    else:
        pt = pt_in[h]
    go = gow_ref[:, col(h)]
    gp = mm(kv_ref[:rows, col(width // HD + h)], go, NT)
    gs = (SCALE * pt * (gp - corr)).astype(BF16)
    gk = mm(gs[:, :near], qm_ref[part, col(h)]) + mm(gs[:, near:], qo_ref[part, col(h)])
    return gk, mm(pt.astype(BF16), go)


def key_early_body(slots, first, *refs):
    got = refs[:slots]
    pt_in, kv_ref, qm_ref, qo_ref = refs[slots : slots + 4]
    gk_ref, gv_ref = refs[slots + 4 : slots + 6]
    pt_ref = refs[slots + 6] if first else None
    gow_ref = refs[-1]
    rows = got[0].shape[0] - PAD
    for b in range(slots):
        gow_ref[b * rows : (b + 1) * rows, :] = got[b][:rows, :]
    part = slice(0, slots // 2 * rows)
    for h in range(pt_in.shape[0]):
        gk, gv = key_terms(got, part, first, pt_in, pt_ref, kv_ref, qm_ref, qo_ref, gow_ref, h)
        gk_ref[:, col(h)] = gk
        gv_ref[:, col(h)] = gv


def key_late_body(first, halved, *refs):
    got = refs[:2]
    pt_in, kv_ref, qm_ref, qo_ref, gk_ref, gv_ref, wk_ref, wv_ref, partq_ref = refs[2:11]
    part_ref, send_ref = refs[11:13]
    pt_ref = refs[13] if first else None
    gow_ref, sum_ref = refs[-2:]
    rows = got[0].shape[0] - PAD
    for b in range(2):
        gow_ref[b * rows : (b + 1) * rows, :] = got[b][:rows, :]
    total = qm_ref.shape[0]
    part = slice(total - rows, total)
    gks, gvs = [], []
    for h in range(pt_in.shape[0]):
        gk, gv = key_terms(got, part, first, pt_in, pt_ref, kv_ref, qm_ref, qo_ref, gow_ref, h)
        gks.append((gk_ref[:, col(h)] + gk).astype(BF16))
        gvs.append((gv_ref[:, col(h)] + gv).astype(BF16))
    acc = partq_ref[...] + mm(jnp.concatenate(gks, axis=1), wk_ref[...], NT)
    acc = acc + mm(jnp.concatenate(gvs, axis=1), wv_ref[...], NT)
    if halved:
        cols = part_ref.shape[1]
        sum_ref[...] = acc
        mine, other = feature_slices(2, cols)
        part_ref[...] = sum_ref[:, mine]
        send_ref[...] = sum_ref[:, other].astype(BF16)
    else:
        part_ref[...] = acc
        send_ref[...] = acc.astype(BF16)


def combine_body(part_ref, recv_ref, inv_ref, gain_ref, wo_ref, att_ref, *refs):
    kry_ref, packed_ref, vec_ref = refs
    rows, width = att_ref.shape
    cols = kry_ref.shape[1]
    inverse = inv_ref[:, :1]
    vec = inverse * (gain_ref[...] * (part_ref[...] + recv_ref[...].astype(F32)))
    vec_ref[...] = vec
    off = pl.multiple_of(lax.axis_index("tp") * cols, HD)
    kry_ref[...] = vec_ref[:, pl.ds(off, cols)]
    go = mm(vec.astype(BF16), wo_ref[...], NT).astype(BF16)
    packed_ref[:rows, :] = go
    corr = [
        jnp.sum(go[:, col(h)].astype(F32) * att_ref[:, col(h)], axis=1, keepdims=True)
        for h in range(width // HD)
    ]
    pack_rows(packed_ref, rows, width // HD, corr)


def gram_body(part_ref, recv_ref, inv_ref, gain_ref, *refs):
    kry = refs[:SSTEP]
    last_ref, sums_ref, vec_ref = refs[SSTEP:]
    rows, cols = last_ref.shape
    inverse = inv_ref[:, :1]
    own = pl.ds(pl.multiple_of(lax.axis_index("tp") * cols, HD), cols)
    vec = part_ref[...] + recv_ref[...].astype(F32)
    if part_ref.shape[1] != cols:
        vec_ref[...] = vec
        vec = vec_ref[:, own]
    last_ref[...] = inverse * (gain_ref[:, own] * vec)
    all_k = list(kry) + [last_ref]
    count = SSTEP * (SSTEP + 1) // 2 + SSTEP
    acc = [jnp.zeros((8, HD), F32) for _ in range(count)]
    for r in range(0, rows, 8):
        for c in range(0, cols, HD):
            ks = [k[r : r + 8, c : c + HD] for k in all_k]
            ds = [ks[i] - ks[i + 1] for i in range(SSTEP)]
            i = 0
            for a in range(SSTEP):
                for b in range(a + 1):
                    acc[i] = acc[i] + ds[a] * ds[b]
                    i += 1
            for a in range(SSTEP):
                acc[i] = acc[i] + ds[a] * ks[0]
                i += 1
    sub = lax.broadcasted_iota(jnp.int32, (PAD, HD), 0)
    out = jnp.zeros((PAD, HD), F32)
    for i in range(count):
        out = jnp.where(sub == i, jnp.sum(acc[i], axis=0, keepdims=True), out)
    for r in range(sums_ref.shape[0]):
        sums_ref[r] = out


def solve(gram, right):
    n = len(right)
    low = [[None] * n for _ in range(n)]
    for i in range(n):
        for j in range(i + 1):
            run = gram[i][j]
            for k in range(j):
                run = run - low[i][k] * low[j][k]
            low[i][j] = jnp.sqrt(run) if i == j else run / low[j][j]
    mid = []
    for i in range(n):
        run = right[i]
        for j in range(i):
            run = run - low[i][j] * mid[j]
        mid.append(run / low[i][i])
    out = [None] * n
    for i in range(n - 1, -1, -1):
        run = mid[i]
        for j in range(i + 1, n):
            run = run - low[j][i] * out[j]
        out[i] = run / low[i][i]
    return out


def finish_body(sums_ref, *refs):
    kry = refs[: SSTEP + 1]
    adj_ref, res_ref = refs[SSTEP + 1 :]
    total = jnp.sum(sums_ref[...], axis=0)
    vals = jnp.sum(total, axis=1, keepdims=True)
    idx = 0
    gram = [[None] * SSTEP for _ in range(SSTEP)]
    for a in range(SSTEP):
        for b in range(a + 1):
            gram[a][b] = vals[idx : idx + 1, :]
            idx += 1
    right = [vals[idx + a : idx + a + 1, :] for a in range(SSTEP)]
    coef = solve(gram, right)
    ks = [k[...] for k in kry]
    adj = coef[0] * ks[0]
    res = ks[0] - coef[0] * (ks[0] - ks[1])
    for i in range(1, SSTEP):
        adj = adj + coef[i] * ks[i]
        res = res - coef[i] * (ks[i] - ks[i + 1])
    adj_ref[...] = adj
    res_ref[...] = res


def swap_partner(c, d, odd):
    return c + d if (c // d) % 2 == odd else c - d


def on_device(state, cotangent, norm_gain, w_query, w_key, w_value, w_out):
    rows, cols = state.shape
    width = w_query.shape[1]
    heads = width // HD
    half = WIN // 2
    seq = lax.axis_size("seq")
    tps = lax.axis_size("tp")
    chips = seq // 2
    hops = hops_of(half, rows)
    blocks = 1 + len(hops)
    early, late = split_slots(blocks)
    ranks = seq * tps
    full = tps * cols

    def swap_core(x):
        return lax.ppermute(x, "seq", [(i, i ^ 1) for i in range(seq)])

    def tp_blocks(x):
        out = [x]
        for k in range(1, tps):
            out.append(lax.ppermute(x, "tp", [((i + k) % tps, i) for i in range(tps)]))
        return out

    def fetch(x):
        got = [x]
        for d, odd in hops:
            pairs = []
            for c in range(chips):
                q = swap_partner(c, d, odd)
                if 0 <= q < chips:
                    pairs += [(2 * c, 2 * q), (2 * c + 1, 2 * q + 1)]
                else:
                    pairs += [(2 * c, 2 * c + 1), (2 * c + 1, 2 * c)]
            got.append(lax.ppermute(x, "seq", pairs))
        return got

    raw = fetch(state)
    cot_low, state_v, gain, w_query, w_key, w_value, w_out = kernel_call(
        prep_body,
        [sds(rows, cols, dtype=BF16), state, sds(1, full)]
        + [w_query, w_key, w_value, w_out],
        [cotangent, state, norm_gain[None, :], w_query, w_key, w_value, w_out],
        scratch=[pltpu.VMEM((rows, cols), F32), pltpu.SemaphoreType.DMA((7,))],
        hbm=7,
        limit=49 << 20,
    )
    pieces = []
    for x in raw:
        pieces += tp_blocks(x)
    pieces[0] = state_v
    cots = tp_blocks(cot_low)
    kv_mine, normed, inv = kernel_call(
        functools.partial(kv_body, blocks, tps),
        [
            sds(blocks * rows, 2 * width, dtype=BF16),
            sds(blocks * rows, full, dtype=BF16),
            sds(rows, HD),
        ],
        pieces + [gain, w_key, w_value],
    )
    kv_other = swap_core(kv_mine)
    q_mine, go0 = kernel_call(
        functools.partial(q_body, tps),
        [sds(blocks * rows, width, dtype=BF16), sds(rows, width, dtype=BF16)],
        cots + [normed, w_query, w_out],
        scratch=[pltpu.VMEM((rows, full), BF16)],
    )
    q_other = swap_core(q_mine)
    probs, att, packed = kernel_call(
        functools.partial(stats_body, half),
        [sds(heads, rows, 2 * blocks * rows), sds(rows, width), sds(rows + PAD, width, dtype=BF16)],
        [kv_mine, kv_other, q_mine, go0],
    )
    krylov = [cotangent]
    for n in range(SSTEP):
        first, last = n == 0, n == SSTEP - 1
        if first:
            pt_early, pt_late = kernel_call(
                functools.partial(scores_t_body, half),
                [sds(heads, rows, len(early) * rows), sds(heads, rows, 2 * rows)],
                [q_mine, q_other, kv_mine],
            )
        got = fetch(packed)
        got = got + [swap_core(x) for x in got]
        (part_q,) = kernel_call(
            query_body,
            [sds(rows, full)],
            [packed, att, probs, kv_mine, kv_other, w_query],
        )
        res = kernel_call(
            functools.partial(key_early_body, len(early), first),
            [sds(rows, width), sds(rows, width)]
            + ([sds(heads, rows, len(early) * rows)] if first else []),
            [got[i] for i in early] + [pt_early, kv_mine, q_mine, q_other],
            scratch=[pltpu.VMEM((len(early) * rows, width), BF16)],
        )
        gk, gv = res[:2]
        if first:
            pt_early = res[2]
        halved = last and tps == 2
        span = cols if halved else full
        res = kernel_call(
            functools.partial(key_late_body, first, halved),
            [sds(rows, span), sds(rows, span, dtype=BF16)]
            + ([sds(heads, rows, 2 * rows)] if first else []),
            [got[i] for i in late]
            + [pt_late, kv_mine, q_mine, q_other, gk, gv, w_key, w_value, part_q],
            scratch=[pltpu.VMEM((2 * rows, width), BF16), pltpu.VMEM((rows, full), F32)],
        )
        part, send = res[:2]
        if first:
            pt_late = res[2]
        k = 1
        while True:
            recv = lax.ppermute(send, "tp", [(i, i ^ k) for i in range(tps)])
            k *= 2
            if k >= tps:
                break
            part = part + recv.astype(F32)
            send = part.astype(BF16)
        if not last:
            kry, packed = kernel_call(
                combine_body,
                [sds(rows, cols), sds(rows + PAD, width, dtype=BF16)],
                [part, recv, inv, gain, w_out, att],
                scratch=[pltpu.VMEM((rows, full), F32)],
            )
        else:
            kry, sums = kernel_call(
                gram_body,
                [sds(rows, cols), sds(ranks, PAD, HD)],
                [part, recv, inv, gain] + krylov,
                scratch=[pltpu.VMEM((rows, full), F32)],
            )
        krylov.append(kry)
    sums = lax.all_to_all(sums, ("seq", "tp"), 0, 0)
    adjoint, residual = kernel_call(
        finish_body,
        [sds(rows, cols), sds(rows, cols)],
        [sums] + krylov,
    )
    return (adjoint, residual)


def solution(mesh):
    in_specs = (
        P("seq", "tp"),
        P("seq", "tp"),
        P(),
        P(None, "tp"),
        P(None, "tp"),
        P(None, "tp"),
        P("tp", None),
    )
    out_specs = (P("seq", "tp"), P("seq", "tp"))
    return jax.shard_map(
        on_device, mesh=mesh, in_specs=in_specs, out_specs=out_specs, check_vma=False
    )
```

```python
import functools
import math

import jax
import jax.numpy as jnp
from jax import lax
from jax.experimental import pallas as pl
from jax.experimental.pallas import tpu as pltpu
from jax.sharding import PartitionSpec as P


HD = 128
WIN = 1024
SSTEP = 4
EPSILON = 1e-05
PAD = 16
NEG = -1e30
SCALE = 1.0 / math.sqrt(HD)
NT = (((1,), (1,)), ((), ()))
NN = (((1,), (0,)), ((), ()))
F32 = jnp.float32
BF16 = jnp.bfloat16


def mm(a, b, dims=NN):
    return lax.dot_general(a, b, dims, preferred_element_type=F32)


def col(h):
    return slice(h * HD, (h + 1) * HD)


def kernel_call(body, outs, ins, scratch=(), hbm=0, flops=10**8, limit=12 << 20):
    in_specs = [pl.BlockSpec(memory_space=pltpu.HBM)] * hbm
    in_specs += [pl.BlockSpec(memory_space=pltpu.VMEM)] * (len(ins) - hbm)
    moved = sum(math.prod(a.shape) * a.dtype.itemsize for a in list(ins) + list(outs))
    return pl.pallas_call(
        body,
        out_shape=[jax.ShapeDtypeStruct(o.shape, o.dtype) for o in outs],
        in_specs=in_specs,
        out_specs=[pl.BlockSpec(memory_space=pltpu.VMEM)] * len(outs),
        scratch_shapes=list(scratch),
        compiler_params=pltpu.CompilerParams(vmem_limit_bytes=limit),
        cost_estimate=pl.CostEstimate(flops=flops, bytes_accessed=moved, transcendentals=0),
    )(*ins)


def sds(*shape, dtype=F32):
    return jax.ShapeDtypeStruct(shape, dtype)


def parts_of(x):
    hi = x.astype(BF16).astype(F32)
    rest = x - hi
    mid = rest.astype(BF16).astype(F32)
    low = (rest - mid).astype(BF16).astype(F32)
    return [hi, mid, low]


def pack_rows(out_ref, rows, heads, columns):
    lane = lax.broadcasted_iota(jnp.int32, (rows, HD), 1)
    mat = jnp.zeros((rows, HD), F32)
    for i, c in enumerate(columns):
        mat = jnp.where(lane == i, c, mat)
    pieces = parts_of(mat.T)
    sub = lax.broadcasted_iota(jnp.int32, (PAD, rows), 0)
    for h in range(heads):
        tile = jnp.zeros((PAD, rows), F32)
        for kind in range(len(columns) // heads):
            r = kind * heads + h
            for i, piece in enumerate(pieces):
                tile = jnp.where(sub == 3 * kind + i, piece[r : r + 1, :], tile)
        out_ref[rows : rows + PAD, col(h)] = tile.astype(BF16)


def unpack_row(slots, rows, h, kind):
    pieces = []
    for s in slots:
        t = s[rows : rows + PAD, col(h)].astype(F32)
        k = 3 * kind
        pieces.append(t[k : k + 1] + t[k + 1 : k + 2] + t[k + 2 : k + 3])
    return jnp.concatenate(pieces, axis=1)


def slot_starts(half, rows):
    me, seq = lax.axis_index("seq"), lax.axis_size("seq")
    chip, core = me // 2, me % 2
    ids = [chip]
    for d, odd in hops_of(half, rows):
        ids.append(jnp.where((chip // d) % 2 == odd, chip + d, chip - d))
    out = []
    for k in (core, 1 - core):
        for q in ids:
            inside = (q >= 0) & (q < seq // 2)
            out.append(jnp.where(inside, (2 * q + k) * rows, -(1 << 24)))
    return out


def hops_of(half, rows):
    reach = (half + rows - 1) // rows
    return [(d, odd) for odd in (1, 0) for d in range(1, (reach + 1) // 2 + 1)]


def masks_of(half, rows):
    starts = slot_starts(half, rows)
    sub = lax.broadcasted_iota(jnp.int32, (rows, rows), 0)
    lane = lax.broadcasted_iota(jnp.int32, (rows, rows), 1)
    return [jnp.abs(lane - sub + (st - starts[0])) <= half for st in starts]


def masked(s, masks):
    rows = s.shape[0]
    pieces = [
        jnp.where(m, s[:, b * rows : (b + 1) * rows], NEG) for b, m in enumerate(masks)
    ]
    return jnp.concatenate(pieces, axis=1)


def feature_slices(tps, cols):
    me = lax.axis_index("tp")
    return [pl.ds(pl.multiple_of(((me + k) % tps) * cols, HD), cols) for k in range(tps)]


def round_body(x_ref, o_ref):
    o_ref[...] = x_ref[...].astype(o_ref.dtype)


def prep_body(*refs):
    count = len(refs) // 2
    sources, outs, sems = refs[:count], refs[count : 2 * count], refs[-1]
    copies = [
        pltpu.make_async_copy(src, dst, sems.at[i])
        for i, (src, dst) in enumerate(zip(sources, outs))
    ]
    for c in copies:
        c.start()
    for c in copies:
        c.wait()


def norm_block(xs, gain_ref, at):
    total = jnp.zeros((xs[0].shape[0], 1), F32)
    vals = [x[...].astype(F32) for x in xs]
    for x in vals:
        total = total + jnp.sum(x * x, axis=1, keepdims=True)
    inverse = lax.rsqrt(total / (len(xs) * xs[0].shape[1]) + EPSILON)
    return inverse, [(x * inverse * gain_ref[:, sl]).astype(BF16) for x, sl in zip(vals, at)]


def norm_body(tps, *refs):
    xs = refs[:tps]
    gain_ref, normed_ref, inv_ref = refs[tps:]
    at = feature_slices(tps, xs[0].shape[1])
    inverse, pieces = norm_block(xs, gain_ref, at)
    inv_ref[...] = jnp.broadcast_to(inverse, inv_ref.shape)
    for sl, piece in zip(at, pieces):
        normed_ref[:, sl] = piece


def kv_body(raw, done, tps, *refs):
    xs = refs[: raw * tps]
    full = refs[raw * tps : raw * tps + done]
    gain_ref, wk_ref, wv_ref, kv_ref, normed_ref = refs[raw * tps + done :]
    rows = full[0].shape[0]
    width = wk_ref.shape[1]
    at = feature_slices(tps, full[0].shape[1] // tps)
    for b in range(raw):
        _, pieces = norm_block(xs[b * tps : (b + 1) * tps], gain_ref, at)
        for sl, piece in zip(at, pieces):
            normed_ref[(b + 1) * rows : (b + 2) * rows, sl] = piece
    for i, x in enumerate(full):
        b = i if i == 0 else i + raw
        normed_ref[b * rows : (b + 1) * rows, :] = x[...]
    x = normed_ref[...]
    kv_ref[:, :width] = mm(x, wk_ref[...]).astype(BF16)
    kv_ref[:, width:] = mm(x, wv_ref[...]).astype(BF16)


def q_body(tps, *refs):
    cots = refs[:tps]
    normed_ref, wq_ref, wo_ref, q_ref, go_ref, cot_ref = refs[tps:]
    q_ref[...] = mm(normed_ref[...], wq_ref[...]).astype(BF16)
    for c, at in zip(cots, feature_slices(tps, cots[0].shape[1])):
        cot_ref[:, at] = c[...]
    go_ref[...] = mm(cot_ref[...], wo_ref[...], NT).astype(BF16)


def stats_body(half, kvm_ref, kvo_ref, q_ref, go_ref, p_ref, att_ref, packed_ref):
    rows, width = go_ref.shape
    heads = width // HD
    near = kvm_ref.shape[0]
    masks = masks_of(half, rows)
    packed_ref[:rows, :] = go_ref[...]
    lse, corr = [], []
    for h in range(heads):
        q = q_ref[:rows, col(h)]
        s = jnp.concatenate(
            [mm(q, kvm_ref[:, col(h)], NT), mm(q, kvo_ref[:, col(h)], NT)], axis=1
        )
        s = masked(s * SCALE, masks)
        peak = jnp.max(s, axis=1, keepdims=True)
        raw = jnp.exp(s - peak)
        total = jnp.sum(raw, axis=1, keepdims=True)
        probs = raw / total
        p_ref[h] = probs
        low = probs.astype(BF16)
        att = mm(low[:, :near], kvm_ref[:, col(heads + h)])
        att = att + mm(low[:, near:], kvo_ref[:, col(heads + h)])
        att_ref[:, col(h)] = att
        lse.append(peak + jnp.log(total))
        corr.append(jnp.sum(go_ref[:, col(h)].astype(F32) * att, axis=1, keepdims=True))
    pack_rows(packed_ref, rows, heads, corr + lse)


def split_slots(blocks):
    early = list(range(blocks - 1)) + list(range(blocks, 2 * blocks - 1))
    return early, [blocks - 1, 2 * blocks - 1]


def scores_t_body(half, qm_ref, qo_ref, kv_ref, early_ref, late_ref):
    rows = early_ref.shape[1]
    masks = masks_of(half, rows)
    cut = qm_ref.shape[0] - rows
    groups = split_slots(len(masks) // 2)
    for h in range(early_ref.shape[0]):
        k = kv_ref[:rows, col(h)]
        for ref, slots, part in zip(
            (early_ref, late_ref), groups, (slice(0, cut), slice(cut, cut + rows))
        ):
            s = jnp.concatenate(
                [mm(k, qm_ref[part, col(h)], NT), mm(k, qo_ref[part, col(h)], NT)], axis=1
            )
            ref[h] = masked(s * SCALE, [masks[i] for i in slots])


def query_body(packed_ref, att_ref, p_ref, kvm_ref, kvo_ref, wq_ref, part_ref):
    rows, width = att_ref.shape
    heads = width // HD
    near = kvm_ref.shape[0]
    grads = []
    for h in range(heads):
        go = packed_ref[:rows, col(h)]
        corr = jnp.sum(go.astype(F32) * att_ref[:, col(h)], axis=1, keepdims=True)
        v = col(heads + h)
        gp = jnp.concatenate([mm(go, kvm_ref[:, v], NT), mm(go, kvo_ref[:, v], NT)], axis=1)
        gs = (SCALE * p_ref[h] * (gp - corr)).astype(BF16)
        gq = mm(gs[:, :near], kvm_ref[:, col(h)]) + mm(gs[:, near:], kvo_ref[:, col(h)])
        grads.append(gq.astype(BF16))
    part_ref[...] = mm(jnp.concatenate(grads, axis=1), wq_ref[...], NT)


def key_terms(got, part, first, pt_in, pt_ref, kv_ref, qm_ref, qo_ref, gow_ref, h):
    rows, width = got[0].shape[0] - PAD, got[0].shape[1]
    near = part.stop - part.start
    corr = unpack_row(got, rows, h, 0)
    if first:
        pt = jnp.exp(pt_in[h] - unpack_row(got, rows, h, 1))
        pt_ref[h] = pt
    else:
        pt = pt_in[h]
    go = gow_ref[:, col(h)]
    gp = mm(kv_ref[:rows, col(width // HD + h)], go, NT)
    gs = (SCALE * pt * (gp - corr)).astype(BF16)
    gk = mm(gs[:, :near], qm_ref[part, col(h)]) + mm(gs[:, near:], qo_ref[part, col(h)])
    return gk, mm(pt.astype(BF16), go)


def key_early_body(slots, first, *refs):
    got = refs[:slots]
    pt_in, kv_ref, qm_ref, qo_ref = refs[slots : slots + 4]
    gk_ref, gv_ref = refs[slots + 4 : slots + 6]
    pt_ref = refs[slots + 6] if first else None
    gow_ref = refs[-1]
    rows = got[0].shape[0] - PAD
    for b in range(slots):
        gow_ref[b * rows : (b + 1) * rows, :] = got[b][:rows, :]
    part = slice(0, slots // 2 * rows)
    for h in range(pt_in.shape[0]):
        gk, gv = key_terms(got, part, first, pt_in, pt_ref, kv_ref, qm_ref, qo_ref, gow_ref, h)
        gk_ref[:, col(h)] = gk
        gv_ref[:, col(h)] = gv


def key_late_body(first, halved, *refs):
    got = refs[:2]
    pt_in, kv_ref, qm_ref, qo_ref, gk_ref, gv_ref, wk_ref, wv_ref, partq_ref = refs[2:11]
    part_ref, send_ref = refs[11:13]
    pt_ref = refs[13] if first else None
    gow_ref, sum_ref = refs[-2:]
    rows = got[0].shape[0] - PAD
    for b in range(2):
        gow_ref[b * rows : (b + 1) * rows, :] = got[b][:rows, :]
    total = qm_ref.shape[0]
    part = slice(total - rows, total)
    gks, gvs = [], []
    for h in range(pt_in.shape[0]):
        gk, gv = key_terms(got, part, first, pt_in, pt_ref, kv_ref, qm_ref, qo_ref, gow_ref, h)
        gks.append((gk_ref[:, col(h)] + gk).astype(BF16))
        gvs.append((gv_ref[:, col(h)] + gv).astype(BF16))
    acc = partq_ref[...] + mm(jnp.concatenate(gks, axis=1), wk_ref[...], NT)
    acc = acc + mm(jnp.concatenate(gvs, axis=1), wv_ref[...], NT)
    if halved:
        cols = part_ref.shape[1]
        sum_ref[...] = acc
        mine, other = feature_slices(2, cols)
        part_ref[...] = sum_ref[:, mine]
        send_ref[...] = sum_ref[:, other].astype(BF16)
    else:
        part_ref[...] = acc
        send_ref[...] = acc.astype(BF16)


def combine_body(part_ref, recv_ref, inv_ref, gain_ref, wo_ref, att_ref, *refs):
    kry_ref, packed_ref, vec_ref = refs
    rows, width = att_ref.shape
    cols = kry_ref.shape[1]
    inverse = inv_ref[:, :1]
    vec = inverse * (gain_ref[...] * (part_ref[...] + recv_ref[...].astype(F32)))
    vec_ref[...] = vec
    off = pl.multiple_of(lax.axis_index("tp") * cols, HD)
    kry_ref[...] = vec_ref[:, pl.ds(off, cols)]
    go = mm(vec.astype(BF16), wo_ref[...], NT).astype(BF16)
    packed_ref[:rows, :] = go
    corr = [
        jnp.sum(go[:, col(h)].astype(F32) * att_ref[:, col(h)], axis=1, keepdims=True)
        for h in range(width // HD)
    ]
    pack_rows(packed_ref, rows, width // HD, corr)


def gram_body(part_ref, recv_ref, inv_ref, gain_ref, *refs):
    kry = refs[:SSTEP]
    last_ref, sums_ref, vec_ref = refs[SSTEP:]
    rows, cols = last_ref.shape
    inverse = inv_ref[:, :1]
    own = pl.ds(pl.multiple_of(lax.axis_index("tp") * cols, HD), cols)
    vec = part_ref[...] + recv_ref[...].astype(F32)
    if part_ref.shape[1] != cols:
        vec_ref[...] = vec
        vec = vec_ref[:, own]
    last_ref[...] = inverse * (gain_ref[:, own] * vec)
    all_k = list(kry) + [last_ref]
    count = SSTEP * (SSTEP + 1) // 2 + SSTEP
    acc = [jnp.zeros((8, HD), F32) for _ in range(count)]
    for r in range(0, rows, 8):
        for c in range(0, cols, HD):
            ks = [k[r : r + 8, c : c + HD] for k in all_k]
            ds = [ks[i] - ks[i + 1] for i in range(SSTEP)]
            i = 0
            for a in range(SSTEP):
                for b in range(a + 1):
                    acc[i] = acc[i] + ds[a] * ds[b]
                    i += 1
            for a in range(SSTEP):
                acc[i] = acc[i] + ds[a] * ks[0]
                i += 1
    lane = lax.broadcasted_iota(jnp.int32, (1, HD), 1)
    out = jnp.zeros((1, HD), F32)
    for i in range(count):
        line = jnp.sum(acc[i], axis=0, keepdims=True)
        out = jnp.where(lane == i, jnp.sum(line, axis=1, keepdims=True), out)
    for r in range(sums_ref.shape[0]):
        sums_ref[r] = out


def solve(gram, right):
    n = len(right)
    low = [[None] * n for _ in range(n)]
    for i in range(n):
        for j in range(i + 1):
            run = gram[i][j]
            for k in range(j):
                run = run - low[i][k] * low[j][k]
            low[i][j] = jnp.sqrt(run) if i == j else run / low[j][j]
    mid = []
    for i in range(n):
        run = right[i]
        for j in range(i):
            run = run - low[i][j] * mid[j]
        mid.append(run / low[i][i])
    out = [None] * n
    for i in range(n - 1, -1, -1):
        run = mid[i]
        for j in range(i + 1, n):
            run = run - low[j][i] * out[j]
        out[i] = run / low[i][i]
    return out


def finish_body(sums_ref, *refs):
    kry = refs[: SSTEP + 1]
    adj_ref, res_ref = refs[SSTEP + 1 :]
    total = jnp.sum(sums_ref[...], axis=0)
    lane = lax.broadcasted_iota(jnp.int32, total.shape, 1)
    count = SSTEP * (SSTEP + 1) // 2 + SSTEP
    vals = [
        jnp.sum(jnp.where(lane == i, total, 0.0), axis=1, keepdims=True) for i in range(count)
    ]
    idx = 0
    gram = [[None] * SSTEP for _ in range(SSTEP)]
    for a in range(SSTEP):
        for b in range(a + 1):
            gram[a][b] = vals[idx]
            idx += 1
    right = [vals[idx + a] for a in range(SSTEP)]
    coef = solve(gram, right)
    ks = [k[...] for k in kry]
    adj = coef[0] * ks[0]
    res = ks[0] - coef[0] * (ks[0] - ks[1])
    for i in range(1, SSTEP):
        adj = adj + coef[i] * ks[i]
        res = res - coef[i] * (ks[i] - ks[i + 1])
    adj_ref[...] = adj
    res_ref[...] = res


def swap_partner(c, d, odd):
    return c + d if (c // d) % 2 == odd else c - d


def on_device(state, cotangent, norm_gain, w_query, w_key, w_value, w_out):
    rows, cols = state.shape
    width = w_query.shape[1]
    heads = width // HD
    half = WIN // 2
    seq = lax.axis_size("seq")
    tps = lax.axis_size("tp")
    chips = seq // 2
    hops = hops_of(half, rows)
    blocks = 1 + len(hops)
    early, late = split_slots(blocks)
    ranks = seq * tps
    full = tps * cols

    def swap_core(x):
        return lax.ppermute(x, "seq", [(i, i ^ 1) for i in range(seq)])

    def tp_blocks(x):
        out = [x]
        for k in range(1, tps):
            out.append(lax.ppermute(x, "tp", [((i + k) % tps, i) for i in range(tps)]))
        return out

    def hop(x, i):
        d, odd = hops[i]
        pairs = []
        for c in range(chips):
            q = swap_partner(c, d, odd)
            if 0 <= q < chips:
                pairs += [(2 * c, 2 * q), (2 * c + 1, 2 * q + 1)]
            else:
                pairs += [(2 * c, 2 * c + 1), (2 * c + 1, 2 * c)]
        return lax.ppermute(x, "seq", pairs)

    def fetch(x):
        return [x] + [hop(x, i) for i in range(len(hops))]

    raw = len(hops) // 2
    states = tp_blocks(state)
    pieces = []
    for i in range(raw):
        pieces += tp_blocks(hop(state, i))
    gain = norm_gain[None, :]
    normed, inv = kernel_call(
        functools.partial(norm_body, tps),
        [sds(rows, full, dtype=BF16), sds(rows, HD)],
        states + [gain],
    )
    done = [normed] + [hop(normed, i) for i in range(raw, len(hops))]
    (cot_low,) = kernel_call(round_body, [sds(rows, cols, dtype=BF16)], [cotangent])
    held = [w_query, w_key, w_value, w_out]
    w_query, w_key, w_value, w_out = kernel_call(
        prep_body,
        held,
        held,
        scratch=[pltpu.SemaphoreType.DMA((len(held),))],
        hbm=len(held),
        limit=49 << 20,
    )
    cots = tp_blocks(cot_low)
    kv_mine, normed = kernel_call(
        functools.partial(kv_body, raw, len(done), tps),
        [
            sds(blocks * rows, 2 * width, dtype=BF16),
            sds(blocks * rows, full, dtype=BF16),
        ],
        pieces + done + [gain, w_key, w_value],
    )
    kv_other = swap_core(kv_mine)
    q_mine, go0 = kernel_call(
        functools.partial(q_body, tps),
        [sds(blocks * rows, width, dtype=BF16), sds(rows, width, dtype=BF16)],
        cots + [normed, w_query, w_out],
        scratch=[pltpu.VMEM((rows, full), BF16)],
    )
    q_other = swap_core(q_mine)
    probs, att, packed = kernel_call(
        functools.partial(stats_body, half),
        [sds(heads, rows, 2 * blocks * rows), sds(rows, width), sds(rows + PAD, width, dtype=BF16)],
        [kv_mine, kv_other, q_mine, go0],
    )
    krylov = [cotangent]
    for n in range(SSTEP):
        first, last = n == 0, n == SSTEP - 1
        if first:
            pt_early, pt_late = kernel_call(
                functools.partial(scores_t_body, half),
                [sds(heads, rows, len(early) * rows), sds(heads, rows, 2 * rows)],
                [q_mine, q_other, kv_mine],
            )
        got = fetch(packed)
        got = got + [swap_core(x) for x in got]
        (part_q,) = kernel_call(
            query_body,
            [sds(rows, full)],
            [packed, att, probs, kv_mine, kv_other, w_query],
        )
        res = kernel_call(
            functools.partial(key_early_body, len(early), first),
            [sds(rows, width), sds(rows, width)]
            + ([sds(heads, rows, len(early) * rows)] if first else []),
            [got[i] for i in early] + [pt_early, kv_mine, q_mine, q_other],
            scratch=[pltpu.VMEM((len(early) * rows, width), BF16)],
        )
        gk, gv = res[:2]
        if first:
            pt_early = res[2]
        halved = last and tps == 2
        span = cols if halved else full
        res = kernel_call(
            functools.partial(key_late_body, first, halved),
            [sds(rows, span), sds(rows, span, dtype=BF16)]
            + ([sds(heads, rows, 2 * rows)] if first else []),
            [got[i] for i in late]
            + [pt_late, kv_mine, q_mine, q_other, gk, gv, w_key, w_value, part_q],
            scratch=[pltpu.VMEM((2 * rows, width), BF16), pltpu.VMEM((rows, full), F32)],
        )
        part, send = res[:2]
        if first:
            pt_late = res[2]
        k = 1
        while True:
            recv = lax.ppermute(send, "tp", [(i, i ^ k) for i in range(tps)])
            k *= 2
            if k >= tps:
                break
            part = part + recv.astype(F32)
            send = part.astype(BF16)
        if not last:
            kry, packed = kernel_call(
                combine_body,
                [sds(rows, cols), sds(rows + PAD, width, dtype=BF16)],
                [part, recv, inv, gain, w_out, att],
                scratch=[pltpu.VMEM((rows, full), F32)],
            )
        else:
            kry, sums = kernel_call(
                gram_body,
                [sds(rows, cols), sds(ranks, 1, HD)],
                [part, recv, inv, gain] + krylov,
                scratch=[pltpu.VMEM((rows, full), F32)],
            )
        krylov.append(kry)
    sums = lax.all_to_all(sums, ("seq", "tp"), 0, 0)
    adjoint, residual = kernel_call(
        finish_body,
        [sds(rows, cols), sds(rows, cols)],
        [sums] + krylov,
    )
    return (adjoint, residual)


def solution(mesh):
    in_specs = (
        P("seq", "tp"),
        P("seq", "tp"),
        P(),
        P(None, "tp"),
        P(None, "tp"),
        P(None, "tp"),
        P("tp", None),
    )
    out_specs = (P("seq", "tp"), P("seq", "tp"))
    return jax.shard_map(
        on_device, mesh=mesh, in_specs=in_specs, out_specs=out_specs, check_vma=False
    )
```

```python
import functools
import math

import jax
import jax.numpy as jnp
from jax import lax
from jax.experimental import pallas as pl
from jax.experimental.pallas import tpu as pltpu
from jax.sharding import PartitionSpec as P


HD = 128
WIN = 1024
SSTEP = 4
EPSILON = 1e-05
PAD = 16
NEG = -1e30
SCALE = 1.0 / math.sqrt(HD)
NT = (((1,), (1,)), ((), ()))
NN = (((1,), (0,)), ((), ()))
F32 = jnp.float32
BF16 = jnp.bfloat16


def mm(a, b, dims=NN):
    return lax.dot_general(a, b, dims, preferred_element_type=F32)


def col(h):
    return slice(h * HD, (h + 1) * HD)


def kernel_call(body, outs, ins, scratch=(), hbm=0, flops=10**8, limit=12 << 20):
    in_specs = [pl.BlockSpec(memory_space=pltpu.HBM)] * hbm
    in_specs += [pl.BlockSpec(memory_space=pltpu.VMEM)] * (len(ins) - hbm)
    moved = sum(math.prod(a.shape) * a.dtype.itemsize for a in list(ins) + list(outs))
    return pl.pallas_call(
        body,
        out_shape=[jax.ShapeDtypeStruct(o.shape, o.dtype) for o in outs],
        in_specs=in_specs,
        out_specs=[pl.BlockSpec(memory_space=pltpu.VMEM)] * len(outs),
        scratch_shapes=list(scratch),
        compiler_params=pltpu.CompilerParams(vmem_limit_bytes=limit),
        cost_estimate=pl.CostEstimate(flops=flops, bytes_accessed=moved, transcendentals=0),
    )(*ins)


def sds(*shape, dtype=F32):
    return jax.ShapeDtypeStruct(shape, dtype)


def parts_of(x):
    hi = x.astype(BF16).astype(F32)
    rest = x - hi
    mid = rest.astype(BF16).astype(F32)
    low = (rest - mid).astype(BF16).astype(F32)
    return [hi, mid, low]


def pack_rows(out_ref, rows, heads, columns):
    lane = lax.broadcasted_iota(jnp.int32, (rows, HD), 1)
    mat = jnp.zeros((rows, HD), F32)
    for i, c in enumerate(columns):
        mat = jnp.where(lane == i, c, mat)
    pieces = parts_of(mat.T)
    sub = lax.broadcasted_iota(jnp.int32, (PAD, rows), 0)
    for h in range(heads):
        tile = jnp.zeros((PAD, rows), F32)
        for kind in range(len(columns) // heads):
            r = kind * heads + h
            for i, piece in enumerate(pieces):
                tile = jnp.where(sub == 3 * kind + i, piece[r : r + 1, :], tile)
        out_ref[rows : rows + PAD, col(h)] = tile.astype(BF16)


def unpack_row(slots, rows, h, kind):
    pieces = []
    for s in slots:
        t = s[rows : rows + PAD, col(h)].astype(F32)
        k = 3 * kind
        pieces.append(t[k : k + 1] + t[k + 1 : k + 2] + t[k + 2 : k + 3])
    return jnp.concatenate(pieces, axis=1)


def slot_starts(half, rows):
    me, seq = lax.axis_index("seq"), lax.axis_size("seq")
    chip, core = me // 2, me % 2
    ids = [chip]
    for d, odd in hops_of(half, rows):
        ids.append(jnp.where((chip // d) % 2 == odd, chip + d, chip - d))
    out = []
    for k in (core, 1 - core):
        for q in ids:
            inside = (q >= 0) & (q < seq // 2)
            out.append(jnp.where(inside, (2 * q + k) * rows, -(1 << 24)))
    return out


def hops_of(half, rows):
    reach = (half + rows - 1) // rows
    return [(d, odd) for odd in (1, 0) for d in range(1, (reach + 1) // 2 + 1)]


def masks_of(half, rows):
    starts = slot_starts(half, rows)
    sub = lax.broadcasted_iota(jnp.int32, (rows, rows), 0)
    lane = lax.broadcasted_iota(jnp.int32, (rows, rows), 1)
    return [jnp.abs(lane - sub + (st - starts[0])) <= half for st in starts]


def masked(s, masks):
    rows = s.shape[0]
    pieces = [
        jnp.where(m, s[:, b * rows : (b + 1) * rows], NEG) for b, m in enumerate(masks)
    ]
    return jnp.concatenate(pieces, axis=1)


def feature_slices(tps, cols):
    me = lax.axis_index("tp")
    return [pl.ds(pl.multiple_of(((me + k) % tps) * cols, HD), cols) for k in range(tps)]


def early_body(cot_ref, state_ref, gain_ref, cot_out, state_out, gain_out):
    cot_out[...] = cot_ref[...].astype(BF16)
    state_out[...] = state_ref[...]
    gain_out[...] = gain_ref[...]


def prep_body(*refs):
    count = len(refs) // 2
    sources, outs, sems = refs[:count], refs[count : 2 * count], refs[-1]
    copies = [
        pltpu.make_async_copy(src, dst, sems.at[i])
        for i, (src, dst) in enumerate(zip(sources, outs))
    ]
    for c in copies:
        c.start()
    for c in copies:
        c.wait()


def norm_block(xs, gain_ref, at):
    total = jnp.zeros((xs[0].shape[0], 1), F32)
    vals = [x[...].astype(F32) for x in xs]
    for x in vals:
        total = total + jnp.sum(x * x, axis=1, keepdims=True)
    inverse = lax.rsqrt(total / (len(xs) * xs[0].shape[1]) + EPSILON)
    return inverse, [(x * inverse * gain_ref[:, sl]).astype(BF16) for x, sl in zip(vals, at)]


def norm_body(tps, *refs):
    xs = refs[:tps]
    gain_ref, normed_ref, inv_ref = refs[tps:]
    at = feature_slices(tps, xs[0].shape[1])
    inverse, pieces = norm_block(xs, gain_ref, at)
    inv_ref[...] = jnp.broadcast_to(inverse, inv_ref.shape)
    for sl, piece in zip(at, pieces):
        normed_ref[:, sl] = piece


def kv_body(raw, done, tps, *refs):
    xs = refs[: raw * tps]
    full = refs[raw * tps : raw * tps + done]
    gain_ref, wk_ref, wv_ref, kv_ref, normed_ref = refs[raw * tps + done :]
    rows = full[0].shape[0]
    width = wk_ref.shape[1]
    at = feature_slices(tps, full[0].shape[1] // tps)
    for b in range(raw):
        _, pieces = norm_block(xs[b * tps : (b + 1) * tps], gain_ref, at)
        for sl, piece in zip(at, pieces):
            normed_ref[(b + 1) * rows : (b + 2) * rows, sl] = piece
    for i, x in enumerate(full):
        b = i if i == 0 else i + raw
        normed_ref[b * rows : (b + 1) * rows, :] = x[...]
    x = normed_ref[...]
    kv_ref[:, :width] = mm(x, wk_ref[...]).astype(BF16)
    kv_ref[:, width:] = mm(x, wv_ref[...]).astype(BF16)


def q_body(rows, normed_ref, wq_ref, kv_ref, q_ref, s_ref):
    q_ref[...] = mm(normed_ref[...], wq_ref[...]).astype(BF16)
    for h in range(s_ref.shape[0]):
        s_ref[h] = mm(q_ref[:rows, col(h)], kv_ref[:, col(h)], NT) * SCALE


def stats_body(half, tps, *refs):
    cots = refs[:tps]
    kvm_ref, kvo_ref, q_ref, s_ref, wo_ref, p_ref, att_ref, packed_ref, cot_ref = refs[tps:]
    rows, width = att_ref.shape
    heads = width // HD
    near = kvm_ref.shape[0]
    masks = masks_of(half, rows)
    for c, at in zip(cots, feature_slices(tps, cots[0].shape[1])):
        cot_ref[:, at] = c[...]
    go = mm(cot_ref[...], wo_ref[...], NT).astype(BF16)
    packed_ref[:rows, :] = go
    lse, corr = [], []
    for h in range(heads):
        q = q_ref[:rows, col(h)]
        s = jnp.concatenate([s_ref[h], mm(q, kvo_ref[:, col(h)], NT) * SCALE], axis=1)
        s = masked(s, masks)
        peak = jnp.max(s, axis=1, keepdims=True)
        raw = jnp.exp(s - peak)
        total = jnp.sum(raw, axis=1, keepdims=True)
        probs = raw * (1.0 / total)
        p_ref[h] = probs
        low = probs.astype(BF16)
        att = mm(low[:, :near], kvm_ref[:, col(heads + h)])
        att = att + mm(low[:, near:], kvo_ref[:, col(heads + h)])
        att_ref[:, col(h)] = att
        lse.append(peak + jnp.log(total))
        corr.append(jnp.sum(go[:, col(h)].astype(F32) * att, axis=1, keepdims=True))
    pack_rows(packed_ref, rows, heads, corr + lse)


def groups_of(blocks):
    cut = 1 + (blocks - 1) // 2
    return [(0, 1), (1, cut), (cut, blocks)]


def scores_t_body(half, qm_ref, qo_ref, kv_ref, *outs):
    rows = outs[0].shape[1]
    masks = masks_of(half, rows)
    blocks = len(masks) // 2
    for h in range(outs[0].shape[0]):
        k = kv_ref[:rows, col(h)]
        for ref, (lo, hi) in zip(outs, groups_of(blocks)):
            part = slice(lo * rows, hi * rows)
            s = jnp.concatenate(
                [mm(k, qm_ref[part, col(h)], NT), mm(k, qo_ref[part, col(h)], NT)], axis=1
            )
            ref[h] = masked(s * SCALE, masks[lo:hi] + masks[blocks + lo : blocks + hi])


def query_body(packed_ref, att_ref, p_ref, kvm_ref, kvo_ref, wq_ref, part_ref):
    rows, width = att_ref.shape
    heads = width // HD
    near = kvm_ref.shape[0]
    grads = []
    for h in range(heads):
        go = packed_ref[:rows, col(h)]
        corr = jnp.sum(go.astype(F32) * att_ref[:, col(h)], axis=1, keepdims=True)
        v = col(heads + h)
        gp = jnp.concatenate([mm(go, kvm_ref[:, v], NT), mm(go, kvo_ref[:, v], NT)], axis=1)
        gs = (SCALE * p_ref[h] * (gp - corr)).astype(BF16)
        gq = mm(gs[:, :near], kvm_ref[:, col(h)]) + mm(gs[:, near:], kvo_ref[:, col(h)])
        grads.append(gq.astype(BF16))
    part_ref[...] = mm(jnp.concatenate(grads, axis=1), wq_ref[...], NT)


def key_terms(got, part, first, pt_in, pt_ref, kv_ref, qm_ref, qo_ref, gow_ref, h):
    rows, width = got[0].shape[0] - PAD, got[0].shape[1]
    near = part.stop - part.start
    corr = unpack_row(got, rows, h, 0)
    if first:
        pt = jnp.exp(pt_in[h] - unpack_row(got, rows, h, 1))
        pt_ref[h] = pt
    else:
        pt = pt_in[h]
    go = gow_ref[:, col(h)]
    gp = mm(kv_ref[:rows, col(width // HD + h)], go, NT)
    gs = (SCALE * pt * (gp - corr)).astype(BF16)
    gk = mm(gs[:, :near], qm_ref[part, col(h)]) + mm(gs[:, near:], qo_ref[part, col(h)])
    return gk, mm(pt.astype(BF16), go)


def key_part_body(span, first, *refs):
    lo, hi = span
    slots = 2 * (hi - lo)
    got = refs[:slots]
    pt_in, kv_ref, qm_ref, qo_ref = refs[slots : slots + 4]
    rest = list(refs[slots + 4 :])
    gow_ref = rest.pop()
    pt_ref = rest.pop() if first else None
    gk_ref, gv_ref = rest[-2:]
    before = rest[:-2]
    rows = got[0].shape[0] - PAD
    for b in range(slots):
        gow_ref[b * rows : (b + 1) * rows, :] = got[b][:rows, :]
    part = slice(lo * rows, hi * rows)
    for h in range(pt_in.shape[0]):
        gk, gv = key_terms(got, part, first, pt_in, pt_ref, kv_ref, qm_ref, qo_ref, gow_ref, h)
        if before:
            gk = gk + before[0][:, col(h)]
            gv = gv + before[1][:, col(h)]
        gk_ref[:, col(h)] = gk
        gv_ref[:, col(h)] = gv


def key_last_body(span, first, halved, *refs):
    lo, hi = span
    slots = 2 * (hi - lo)
    got = refs[:slots]
    pt_in, kv_ref, qm_ref, qo_ref, gk_ref, gv_ref, wk_ref, wv_ref, partq_ref = refs[
        slots : slots + 9
    ]
    part_ref, send_ref = refs[slots + 9 : slots + 11]
    pt_ref = refs[slots + 11] if first else None
    gow_ref, sum_ref = refs[-2:]
    rows = got[0].shape[0] - PAD
    for b in range(slots):
        gow_ref[b * rows : (b + 1) * rows, :] = got[b][:rows, :]
    part = slice(lo * rows, hi * rows)
    gks, gvs = [], []
    for h in range(pt_in.shape[0]):
        gk, gv = key_terms(got, part, first, pt_in, pt_ref, kv_ref, qm_ref, qo_ref, gow_ref, h)
        gks.append((gk_ref[:, col(h)] + gk).astype(BF16))
        gvs.append((gv_ref[:, col(h)] + gv).astype(BF16))
    acc = partq_ref[...] + mm(jnp.concatenate(gks, axis=1), wk_ref[...], NT)
    acc = acc + mm(jnp.concatenate(gvs, axis=1), wv_ref[...], NT)
    if halved:
        cols = part_ref.shape[1]
        sum_ref[...] = acc
        mine, other = feature_slices(2, cols)
        part_ref[...] = sum_ref[:, mine]
        send_ref[...] = sum_ref[:, other].astype(BF16)
    else:
        part_ref[...] = acc
        send_ref[...] = acc.astype(BF16)


def combine_body(part_ref, recv_ref, inv_ref, gain_ref, wo_ref, att_ref, *refs):
    kry_ref, packed_ref, vec_ref = refs
    rows, width = att_ref.shape
    cols = kry_ref.shape[1]
    inverse = inv_ref[:, :1]
    vec = inverse * (gain_ref[...] * (part_ref[...] + recv_ref[...].astype(F32)))
    vec_ref[...] = vec
    off = pl.multiple_of(lax.axis_index("tp") * cols, HD)
    kry_ref[...] = vec_ref[:, pl.ds(off, cols)]
    go = mm(vec.astype(BF16), wo_ref[...], NT).astype(BF16)
    packed_ref[:rows, :] = go
    corr = [
        jnp.sum(go[:, col(h)].astype(F32) * att_ref[:, col(h)], axis=1, keepdims=True)
        for h in range(width // HD)
    ]
    pack_rows(packed_ref, rows, width // HD, corr)


def gram_body(part_ref, recv_ref, inv_ref, gain_ref, *refs):
    kry = refs[:SSTEP]
    last_ref, sums_ref, vec_ref = refs[SSTEP:]
    rows, cols = last_ref.shape
    inverse = inv_ref[:, :1]
    own = pl.ds(pl.multiple_of(lax.axis_index("tp") * cols, HD), cols)
    vec = part_ref[...] + recv_ref[...].astype(F32)
    if part_ref.shape[1] != cols:
        vec_ref[...] = vec
        vec = vec_ref[:, own]
    last_ref[...] = inverse * (gain_ref[:, own] * vec)
    all_k = list(kry) + [last_ref]
    count = SSTEP * (SSTEP + 1) // 2 + SSTEP
    acc = [jnp.zeros((8, HD), F32) for _ in range(count)]
    for r in range(0, rows, 8):
        for c in range(0, cols, HD):
            ks = [k[r : r + 8, c : c + HD] for k in all_k]
            ds = [ks[i] - ks[i + 1] for i in range(SSTEP)]
            i = 0
            for a in range(SSTEP):
                for b in range(a + 1):
                    acc[i] = acc[i] + ds[a] * ds[b]
                    i += 1
            for a in range(SSTEP):
                acc[i] = acc[i] + ds[a] * ks[0]
                i += 1
    lane = lax.broadcasted_iota(jnp.int32, (1, HD), 1)
    out = jnp.zeros((1, HD), F32)
    for i in range(count):
        line = jnp.sum(acc[i], axis=0, keepdims=True)
        out = jnp.where(lane == i, jnp.sum(line, axis=1, keepdims=True), out)
    for r in range(sums_ref.shape[0]):
        sums_ref[r] = out


def solve(gram, right):
    n = len(right)
    low = [[None] * n for _ in range(n)]
    for i in range(n):
        for j in range(i + 1):
            run = gram[i][j]
            for k in range(j):
                run = run - low[i][k] * low[j][k]
            low[i][j] = jnp.sqrt(run) if i == j else run / low[j][j]
    mid = []
    for i in range(n):
        run = right[i]
        for j in range(i):
            run = run - low[i][j] * mid[j]
        mid.append(run / low[i][i])
    out = [None] * n
    for i in range(n - 1, -1, -1):
        run = mid[i]
        for j in range(i + 1, n):
            run = run - low[j][i] * out[j]
        out[i] = run / low[i][i]
    return out


def finish_body(sums_ref, *refs):
    kry = refs[: SSTEP + 1]
    adj_ref, res_ref = refs[SSTEP + 1 :]
    total = jnp.sum(sums_ref[...], axis=0)
    lane = lax.broadcasted_iota(jnp.int32, total.shape, 1)
    count = SSTEP * (SSTEP + 1) // 2 + SSTEP
    vals = [
        jnp.sum(jnp.where(lane == i, total, 0.0), axis=1, keepdims=True) for i in range(count)
    ]
    idx = 0
    gram = [[None] * SSTEP for _ in range(SSTEP)]
    for a in range(SSTEP):
        for b in range(a + 1):
            gram[a][b] = vals[idx]
            idx += 1
    right = [vals[idx + a] for a in range(SSTEP)]
    coef = solve(gram, right)
    ks = [k[...] for k in kry]
    adj = coef[0] * ks[0]
    res = ks[0] - coef[0] * (ks[0] - ks[1])
    for i in range(1, SSTEP):
        adj = adj + coef[i] * ks[i]
        res = res - coef[i] * (ks[i] - ks[i + 1])
    adj_ref[...] = adj
    res_ref[...] = res


def swap_partner(c, d, odd):
    return c + d if (c // d) % 2 == odd else c - d


def on_device(state, cotangent, norm_gain, w_query, w_key, w_value, w_out):
    rows, cols = state.shape
    width = w_query.shape[1]
    heads = width // HD
    half = WIN // 2
    seq = lax.axis_size("seq")
    tps = lax.axis_size("tp")
    chips = seq // 2
    hops = hops_of(half, rows)
    blocks = 1 + len(hops)
    groups = groups_of(blocks)
    wide = [2 * (hi - lo) * rows for lo, hi in groups]
    ranks = seq * tps
    full = tps * cols

    def swap_core(x):
        return lax.ppermute(x, "seq", [(i, i ^ 1) for i in range(seq)])

    def tp_blocks(x):
        out = [x]
        for k in range(1, tps):
            out.append(lax.ppermute(x, "tp", [((i + k) % tps, i) for i in range(tps)]))
        return out

    def hop(x, i):
        d, odd = hops[i]
        pairs = []
        for c in range(chips):
            q = swap_partner(c, d, odd)
            if 0 <= q < chips:
                pairs += [(2 * c, 2 * q), (2 * c + 1, 2 * q + 1)]
            else:
                pairs += [(2 * c, 2 * c + 1), (2 * c + 1, 2 * c)]
        return lax.ppermute(x, "seq", pairs)

    def fetch(x):
        return [x] + [hop(x, i) for i in range(len(hops))]

    raw = len(hops) // 2
    states = tp_blocks(state)
    pieces = []
    for i in range(raw):
        pieces += tp_blocks(hop(state, i))
    cot_low, states[0], gain = kernel_call(
        early_body,
        [sds(rows, cols, dtype=BF16), state, sds(1, full)],
        [cotangent, state, norm_gain[None, :]],
    )
    normed, inv = kernel_call(
        functools.partial(norm_body, tps),
        [sds(rows, full, dtype=BF16), sds(rows, HD)],
        states + [gain],
    )
    done = [normed] + [hop(normed, i) for i in range(raw, len(hops))]
    held = [w_query, w_key, w_value, w_out]
    w_query, w_key, w_value, w_out = kernel_call(
        prep_body,
        held,
        held,
        scratch=[pltpu.SemaphoreType.DMA((len(held),))],
        hbm=len(held),
        limit=49 << 20,
    )
    cots = tp_blocks(cot_low)
    kv_mine, normed = kernel_call(
        functools.partial(kv_body, raw, len(done), tps),
        [
            sds(blocks * rows, 2 * width, dtype=BF16),
            sds(blocks * rows, full, dtype=BF16),
        ],
        pieces + done + [gain, w_key, w_value],
    )
    kv_other = swap_core(kv_mine)
    q_mine, s_mine = kernel_call(
        functools.partial(q_body, rows),
        [sds(blocks * rows, width, dtype=BF16), sds(heads, rows, blocks * rows)],
        [normed, w_query, kv_mine],
    )
    q_other = swap_core(q_mine)
    probs, att, packed = kernel_call(
        functools.partial(stats_body, half, tps),
        [sds(heads, rows, 2 * blocks * rows), sds(rows, width), sds(rows + PAD, width, dtype=BF16)],
        cots + [kv_mine, kv_other, q_mine, s_mine, w_out],
        scratch=[pltpu.VMEM((rows, full), BF16)],
    )
    krylov = [cotangent]
    for n in range(SSTEP):
        first, last = n == 0, n == SSTEP - 1
        if first:
            pts = kernel_call(
                functools.partial(scores_t_body, half),
                [sds(heads, rows, w) for w in wide],
                [q_mine, q_other, kv_mine],
            )
        got = fetch(packed)
        got = got + [swap_core(x) for x in got]
        (part_q,) = kernel_call(
            query_body,
            [sds(rows, full)],
            [packed, att, probs, kv_mine, kv_other, w_query],
        )
        static = [kv_mine, q_mine, q_other]
        grads = []
        new_pts = []
        for g in range(2):
            lo, hi = groups[g]
            res = kernel_call(
                functools.partial(key_part_body, groups[g], first),
                [sds(rows, width), sds(rows, width)]
                + ([sds(heads, rows, wide[g])] if first else []),
                got[lo:hi] + got[blocks + lo : blocks + hi] + [pts[g]] + static + grads,
                scratch=[pltpu.VMEM((wide[g], width), BF16)],
            )
            grads = list(res[:2])
            new_pts += list(res[2:])
        halved = last and tps == 2
        span = cols if halved else full
        lo, hi = groups[2]
        res = kernel_call(
            functools.partial(key_last_body, groups[2], first, halved),
            [sds(rows, span), sds(rows, span, dtype=BF16)]
            + ([sds(heads, rows, wide[2])] if first else []),
            got[lo:hi]
            + got[blocks + lo : blocks + hi]
            + [pts[2]]
            + static
            + grads
            + [w_key, w_value, part_q],
            scratch=[pltpu.VMEM((wide[2], width), BF16), pltpu.VMEM((rows, full), F32)],
        )
        part, send = res[:2]
        if first:
            pts = new_pts + list(res[2:])
        k = 1
        while True:
            recv = lax.ppermute(send, "tp", [(i, i ^ k) for i in range(tps)])
            k *= 2
            if k >= tps:
                break
            part = part + recv.astype(F32)
            send = part.astype(BF16)
        if not last:
            kry, packed = kernel_call(
                combine_body,
                [sds(rows, cols), sds(rows + PAD, width, dtype=BF16)],
                [part, recv, inv, gain, w_out, att],
                scratch=[pltpu.VMEM((rows, full), F32)],
            )
        else:
            kry, sums = kernel_call(
                gram_body,
                [sds(rows, cols), sds(ranks, 1, HD)],
                [part, recv, inv, gain] + krylov,
                scratch=[pltpu.VMEM((rows, full), F32)],
            )
        krylov.append(kry)
    sums = lax.all_to_all(sums, ("seq", "tp"), 0, 0)
    adjoint, residual = kernel_call(
        finish_body,
        [sds(rows, cols), sds(rows, cols)],
        [sums] + krylov,
    )
    return (adjoint, residual)


def solution(mesh):
    in_specs = (
        P("seq", "tp"),
        P("seq", "tp"),
        P(),
        P(None, "tp"),
        P(None, "tp"),
        P(None, "tp"),
        P("tp", None),
    )
    out_specs = (P("seq", "tp"), P("seq", "tp"))
    return jax.shard_map(
        on_device, mesh=mesh, in_specs=in_specs, out_specs=out_specs, check_vma=False
    )
```

```python
import functools
import math

import jax
import jax.numpy as jnp
from jax import lax
from jax.experimental import pallas as pl
from jax.experimental.pallas import tpu as pltpu
from jax.sharding import PartitionSpec as P


HD = 128
WIN = 1024
SSTEP = 4
EPSILON = 1e-05
PAD = 8
NEG = -1e30
SCALE = 1.0 / math.sqrt(HD)
NT = (((1,), (1,)), ((), ()))
NN = (((1,), (0,)), ((), ()))
F32 = jnp.float32
BF16 = jnp.bfloat16


def mm(a, b, dims=NN):
    return lax.dot_general(a, b, dims, preferred_element_type=F32)


def col(h):
    return slice(h * HD, (h + 1) * HD)


def kernel_call(body, outs, ins, scratch=(), hbm=0, flops=10**8, limit=12 << 20):
    in_specs = [pl.BlockSpec(memory_space=pltpu.HBM)] * hbm
    in_specs += [pl.BlockSpec(memory_space=pltpu.VMEM)] * (len(ins) - hbm)
    moved = sum(math.prod(a.shape) * a.dtype.itemsize for a in list(ins) + list(outs))
    return pl.pallas_call(
        body,
        out_shape=[jax.ShapeDtypeStruct(o.shape, o.dtype) for o in outs],
        in_specs=in_specs,
        out_specs=[pl.BlockSpec(memory_space=pltpu.VMEM)] * len(outs),
        scratch_shapes=list(scratch),
        compiler_params=pltpu.CompilerParams(vmem_limit_bytes=limit),
        cost_estimate=pl.CostEstimate(flops=flops, bytes_accessed=moved, transcendentals=0),
    )(*ins)


def sds(*shape, dtype=F32):
    return jax.ShapeDtypeStruct(shape, dtype)


def parts_of(x):
    hi = x.astype(BF16).astype(F32)
    rest = x - hi
    mid = rest.astype(BF16).astype(F32)
    low = (rest - mid).astype(BF16).astype(F32)
    return [hi, mid, low]


def pack_rows(out_ref, rows, heads, columns):
    lane = lax.broadcasted_iota(jnp.int32, (rows, HD), 1)
    mat = jnp.zeros((rows, HD), F32)
    for i, c in enumerate(columns):
        mat = jnp.where(lane == i, c, mat)
    pieces = parts_of(mat.T)
    sub = lax.broadcasted_iota(jnp.int32, (PAD, rows), 0)
    for h in range(heads):
        tile = jnp.zeros((PAD, rows), F32)
        for kind in range(len(columns) // heads):
            r = kind * heads + h
            for i, piece in enumerate(pieces):
                tile = jnp.where(sub == 3 * kind + i, piece[r : r + 1, :], tile)
        out_ref[rows : rows + PAD, col(h)] = tile.astype(BF16)


def unpack_row(slots, rows, h, kind):
    pieces = []
    for s in slots:
        t = s[rows : rows + PAD, col(h)].astype(F32)
        k = 3 * kind
        pieces.append(t[k : k + 1] + t[k + 1 : k + 2] + t[k + 2 : k + 3])
    return jnp.concatenate(pieces, axis=1)


def slot_starts(half, rows):
    me, seq = lax.axis_index("seq"), lax.axis_size("seq")
    chip, core = me // 2, me % 2
    ids = [chip]
    for d, odd in hops_of(half, rows):
        ids.append(jnp.where((chip // d) % 2 == odd, chip + d, chip - d))
    out = []
    for k in (core, 1 - core):
        for q in ids:
            inside = (q >= 0) & (q < seq // 2)
            out.append(jnp.where(inside, (2 * q + k) * rows, -(1 << 24)))
    return out


def hops_of(half, rows):
    reach = (half + rows - 1) // rows
    return [(d, odd) for odd in (1, 0) for d in range(1, (reach + 1) // 2 + 1)]


def masks_of(half, rows):
    starts = slot_starts(half, rows)
    sub = lax.broadcasted_iota(jnp.int32, (rows, rows), 0)
    lane = lax.broadcasted_iota(jnp.int32, (rows, rows), 1)
    return [jnp.abs(lane - sub + (st - starts[0])) <= half for st in starts]


def masked(s, masks):
    rows = s.shape[0]
    pieces = [
        jnp.where(m, s[:, b * rows : (b + 1) * rows], NEG) for b, m in enumerate(masks)
    ]
    return jnp.concatenate(pieces, axis=1)


def feature_slices(tps, cols):
    me = lax.axis_index("tp")
    return [pl.ds(pl.multiple_of(((me + k) % tps) * cols, HD), cols) for k in range(tps)]


def early_body(cot_ref, state_ref, gain_ref, cot_out, state_out, gain_out):
    cot_out[...] = cot_ref[...].astype(BF16)
    state_out[...] = state_ref[...]
    gain_out[...] = gain_ref[...]


def prep_body(*refs):
    count = len(refs) // 2
    sources, outs, sems = refs[:count], refs[count : 2 * count], refs[-1]
    copies = [
        pltpu.make_async_copy(src, dst, sems.at[i])
        for i, (src, dst) in enumerate(zip(sources, outs))
    ]
    for c in copies:
        c.start()
    for c in copies:
        c.wait()


def norm_block(xs, gain_ref, at):
    total = jnp.zeros((xs[0].shape[0], 1), F32)
    vals = [x[...].astype(F32) for x in xs]
    for x in vals:
        total = total + jnp.sum(x * x, axis=1, keepdims=True)
    inverse = lax.rsqrt(total / (len(xs) * xs[0].shape[1]) + EPSILON)
    return inverse, [(x * inverse * gain_ref[:, sl]).astype(BF16) for x, sl in zip(vals, at)]


def norm_body(tps, *refs):
    xs = refs[:tps]
    gain_ref, normed_ref, inv_ref = refs[tps:]
    at = feature_slices(tps, xs[0].shape[1])
    inverse, pieces = norm_block(xs, gain_ref, at)
    inv_ref[...] = jnp.broadcast_to(inverse, inv_ref.shape)
    for sl, piece in zip(at, pieces):
        normed_ref[:, sl] = piece


def kv_body(raw, done, tps, *refs):
    xs = refs[: raw * tps]
    full = refs[raw * tps : raw * tps + done]
    gain_ref, wk_ref, wv_ref, kv_ref, normed_ref = refs[raw * tps + done :]
    rows = full[0].shape[0]
    width = wk_ref.shape[1]
    at = feature_slices(tps, full[0].shape[1] // tps)
    for b in range(raw):
        _, pieces = norm_block(xs[b * tps : (b + 1) * tps], gain_ref, at)
        for sl, piece in zip(at, pieces):
            normed_ref[(b + 1) * rows : (b + 2) * rows, sl] = piece
    for i, x in enumerate(full):
        b = i if i == 0 else i + raw
        normed_ref[b * rows : (b + 1) * rows, :] = x[...]
    x = normed_ref[...]
    kv_ref[:, :width] = mm(x, wk_ref[...]).astype(BF16)
    kv_ref[:, width:] = mm(x, wv_ref[...]).astype(BF16)


def q_body(rows, normed_ref, wq_ref, kv_ref, q_ref, s_ref):
    q_ref[...] = mm(normed_ref[...], wq_ref[...]).astype(BF16)
    for h in range(s_ref.shape[0]):
        s_ref[h] = mm(q_ref[:rows, col(h)], kv_ref[:, col(h)], NT) * SCALE


def stats_body(half, tps, *refs):
    cots = refs[:tps]
    kvm_ref, kvo_ref, q_ref, s_ref, wo_ref, p_ref, att_ref, packed_ref, cot_ref = refs[tps:]
    rows, width = att_ref.shape
    heads = width // HD
    near = kvm_ref.shape[0]
    masks = masks_of(half, rows)
    for c, at in zip(cots, feature_slices(tps, cots[0].shape[1])):
        cot_ref[:, at] = c[...]
    go = mm(cot_ref[...], wo_ref[...], NT).astype(BF16)
    packed_ref[:rows, :] = go
    lse, corr = [], []
    for h in range(heads):
        q = q_ref[:rows, col(h)]
        s = jnp.concatenate([s_ref[h], mm(q, kvo_ref[:, col(h)], NT) * SCALE], axis=1)
        s = masked(s, masks)
        peak = jnp.max(s, axis=1, keepdims=True)
        raw = jnp.exp(s - peak)
        total = jnp.sum(raw, axis=1, keepdims=True)
        probs = raw * (1.0 / total)
        p_ref[h] = probs
        low = probs.astype(BF16)
        att = mm(low[:, :near], kvm_ref[:, col(heads + h)])
        att = att + mm(low[:, near:], kvo_ref[:, col(heads + h)])
        att_ref[:, col(h)] = att
        lse.append(peak + jnp.log(total))
        corr.append(jnp.sum(go[:, col(h)].astype(F32) * att, axis=1, keepdims=True))
    pack_rows(packed_ref, rows, heads, corr + lse)


def groups_of(blocks):
    cut = 1 + (blocks - 1) // 2
    return [(0, 1), (1, cut), (cut, blocks)]


def scores_t_body(half, qm_ref, qo_ref, kv_ref, *outs):
    rows = outs[0].shape[1]
    masks = masks_of(half, rows)
    blocks = len(masks) // 2
    for h in range(outs[0].shape[0]):
        k = kv_ref[:rows, col(h)]
        for ref, (lo, hi) in zip(outs, groups_of(blocks)):
            part = slice(lo * rows, hi * rows)
            s = jnp.concatenate(
                [mm(k, qm_ref[part, col(h)], NT), mm(k, qo_ref[part, col(h)], NT)], axis=1
            )
            ref[h] = masked(s * SCALE, masks[lo:hi] + masks[blocks + lo : blocks + hi])


def query_grads(packed_ref, att_ref, p_ref, kvm_ref, kvo_ref, gq_ref):
    rows, width = att_ref.shape
    heads = width // HD
    near = kvm_ref.shape[0]
    for h in range(heads):
        go = packed_ref[:rows, col(h)]
        corr = jnp.sum(go.astype(F32) * att_ref[:, col(h)], axis=1, keepdims=True)
        v = col(heads + h)
        gp = jnp.concatenate([mm(go, kvm_ref[:, v], NT), mm(go, kvo_ref[:, v], NT)], axis=1)
        gs = (SCALE * p_ref[h] * (gp - corr)).astype(BF16)
        gq = mm(gs[:, :near], kvm_ref[:, col(h)]) + mm(gs[:, near:], kvo_ref[:, col(h)])
        gq_ref[:, col(h)] = gq.astype(BF16)


def query_body(packed_ref, att_ref, p_ref, kvm_ref, kvo_ref, wq_ref, part_ref, gq_ref):
    query_grads(packed_ref, att_ref, p_ref, kvm_ref, kvo_ref, gq_ref)
    part_ref[...] = mm(gq_ref[...], wq_ref[...], NT)


def key_terms(got, part, first, pt_in, pt_ref, kv_ref, qm_ref, qo_ref, gow_ref, h):
    rows, width = got[0].shape[0] - PAD, got[0].shape[1]
    near = part.stop - part.start
    corr = unpack_row(got, rows, h, 0)
    if first:
        pt = jnp.exp(pt_in[h] - unpack_row(got, rows, h, 1))
        pt_ref[h] = pt
    else:
        pt = pt_in[h]
    go = gow_ref[:, col(h)]
    gp = mm(kv_ref[:rows, col(width // HD + h)], go, NT)
    gs = (SCALE * pt * (gp - corr)).astype(BF16)
    gk = mm(gs[:, :near], qm_ref[part, col(h)]) + mm(gs[:, near:], qo_ref[part, col(h)])
    return gk, mm(pt.astype(BF16), go)


def key_part_body(span, first, *refs):
    lo, hi = span
    slots = 2 * (hi - lo)
    got = refs[:slots]
    pt_in, kv_ref, qm_ref, qo_ref = refs[slots : slots + 4]
    rest = list(refs[slots + 4 :])
    gow_ref = rest.pop()
    pt_ref = rest.pop() if first else None
    gk_ref, gv_ref = rest[-2:]
    before = rest[:-2]
    rows = got[0].shape[0] - PAD
    for b in range(slots):
        gow_ref[b * rows : (b + 1) * rows, :] = got[b][:rows, :]
    part = slice(lo * rows, hi * rows)
    for h in range(pt_in.shape[0]):
        gk, gv = key_terms(got, part, first, pt_in, pt_ref, kv_ref, qm_ref, qo_ref, gow_ref, h)
        if before:
            gk = gk + before[0][:, col(h)]
            gv = gv + before[1][:, col(h)]
        gk_ref[:, col(h)] = gk
        gv_ref[:, col(h)] = gv


def key_last_body(span, first, halved, *refs):
    lo, hi = span
    slots = 2 * (hi - lo)
    got = refs[:slots]
    pt_in, kv_ref, qm_ref, qo_ref, gk_ref, gv_ref, wk_ref, wv_ref, partq_ref = refs[
        slots : slots + 9
    ]
    part_ref, send_ref = refs[slots + 9 : slots + 11]
    pt_ref = refs[slots + 11] if first else None
    gow_ref, sum_ref = refs[-2:]
    rows = got[0].shape[0] - PAD
    for b in range(slots):
        gow_ref[b * rows : (b + 1) * rows, :] = got[b][:rows, :]
    part = slice(lo * rows, hi * rows)
    gks, gvs = [], []
    for h in range(pt_in.shape[0]):
        gk, gv = key_terms(got, part, first, pt_in, pt_ref, kv_ref, qm_ref, qo_ref, gow_ref, h)
        gks.append((gk_ref[:, col(h)] + gk).astype(BF16))
        gvs.append((gv_ref[:, col(h)] + gv).astype(BF16))
    acc = partq_ref[...] + mm(jnp.concatenate(gks, axis=1), wk_ref[...], NT)
    acc = acc + mm(jnp.concatenate(gvs, axis=1), wv_ref[...], NT)
    if halved:
        cols = part_ref.shape[1]
        sum_ref[...] = acc
        mine, other = feature_slices(2, cols)
        part_ref[...] = sum_ref[:, mine]
        send_ref[...] = sum_ref[:, other].astype(BF16)
    else:
        part_ref[...] = acc
        send_ref[...] = acc.astype(BF16)


def half_rows_body(w_ref, o_ref):
    n = o_ref.shape[0]
    core = lax.axis_index("seq") % 2
    o_ref[...] = w_ref[pl.ds(pl.multiple_of(core * n, n), n), :]


def fold_body(wo_ref, mine_ref, other_ref, gain_ref, wq_ref, wk_ref, wv_ref, ft_ref, full_ref):
    n = mine_ref.shape[0]
    core = lax.axis_index("seq") % 2
    full_ref[pl.ds(pl.multiple_of(core * n, n), n), :] = mine_ref[...]
    full_ref[pl.ds(pl.multiple_of((1 - core) * n, n), n), :] = other_ref[...]
    for i, ref in enumerate((wo_ref, full_ref)):
        scaled = (ref[...].astype(F32) * gain_ref[...]).astype(BF16)
        for j, w in enumerate((wq_ref, wk_ref, wv_ref)):
            ft_ref[i, j] = mm(scaled, w[...]).astype(BF16)


def query_fold_body(packed_ref, att_ref, p_ref, kvm_ref, kvo_ref, ft_ref, gq_ref, own_ref, oth_ref):
    query_grads(packed_ref, att_ref, p_ref, kvm_ref, kvo_ref, gq_ref)
    gq = gq_ref[...]
    own_ref[...] = mm(gq, ft_ref[0, 0], NT)
    oth_ref[...] = mm(gq, ft_ref[1, 0], NT)


def key_fold_body(span, *refs):
    lo, hi = span
    slots = 2 * (hi - lo)
    got = refs[:slots]
    pt_in, kv_ref, qm_ref, qo_ref, gk_in, gv_in, ft_ref, ownq_ref, othq_ref = refs[
        slots : slots + 9
    ]
    own_ref, send_ref, gk_ref, gv_ref, gow_ref = refs[slots + 9 :]
    rows = got[0].shape[0] - PAD
    for b in range(slots):
        gow_ref[b * rows : (b + 1) * rows, :] = got[b][:rows, :]
    part = slice(lo * rows, hi * rows)
    for h in range(pt_in.shape[0]):
        gk, gv = key_terms(got, part, False, pt_in, None, kv_ref, qm_ref, qo_ref, gow_ref, h)
        gk_ref[:, col(h)] = (gk_in[:, col(h)] + gk).astype(BF16)
        gv_ref[:, col(h)] = (gv_in[:, col(h)] + gv).astype(BF16)
    gk, gv = gk_ref[...], gv_ref[...]
    own_ref[...] = ownq_ref[...] + mm(gk, ft_ref[0, 1], NT) + mm(gv, ft_ref[0, 2], NT)
    oth = othq_ref[...] + mm(gk, ft_ref[1, 1], NT) + mm(gv, ft_ref[1, 2], NT)
    send_ref[...] = oth.astype(BF16)


def combine_fold_body(own_ref, recv_ref, inv_ref, att_ref, packed_ref):
    rows, width = att_ref.shape
    go = (inv_ref[:, :1] * (own_ref[...] + recv_ref[...].astype(F32))).astype(BF16)
    packed_ref[:rows, :] = go
    corr = [
        jnp.sum(go[:, col(h)].astype(F32) * att_ref[:, col(h)], axis=1, keepdims=True)
        for h in range(width // HD)
    ]
    pack_rows(packed_ref, rows, width // HD, corr)


def side_body(gq_ref, gk_ref, gv_ref, wq_ref, wk_ref, wv_ref, part_ref, send_ref, sum_ref):
    acc = mm(gq_ref[...], wq_ref[...], NT) + mm(gk_ref[...], wk_ref[...], NT)
    sum_ref[...] = acc + mm(gv_ref[...], wv_ref[...], NT)
    mine, other = feature_slices(2, part_ref.shape[1])
    part_ref[...] = sum_ref[:, mine]
    send_ref[...] = sum_ref[:, other].astype(BF16)


def side_sum_body(part_ref, recv_ref, inv_ref, gain_ref, kry_ref):
    mine = feature_slices(2, part_ref.shape[1])[0]
    vec = part_ref[...] + recv_ref[...].astype(F32)
    kry_ref[...] = inv_ref[:, :1] * (gain_ref[:, mine] * vec)


def combine_body(part_ref, recv_ref, inv_ref, gain_ref, wo_ref, att_ref, *refs):
    kry_ref, packed_ref, vec_ref = refs
    rows, width = att_ref.shape
    cols = kry_ref.shape[1]
    inverse = inv_ref[:, :1]
    vec = inverse * (gain_ref[...] * (part_ref[...] + recv_ref[...].astype(F32)))
    vec_ref[...] = vec
    off = pl.multiple_of(lax.axis_index("tp") * cols, HD)
    kry_ref[...] = vec_ref[:, pl.ds(off, cols)]
    go = mm(vec.astype(BF16), wo_ref[...], NT).astype(BF16)
    packed_ref[:rows, :] = go
    corr = [
        jnp.sum(go[:, col(h)].astype(F32) * att_ref[:, col(h)], axis=1, keepdims=True)
        for h in range(width // HD)
    ]
    pack_rows(packed_ref, rows, width // HD, corr)


def gram_body(part_ref, recv_ref, inv_ref, gain_ref, *refs):
    kry = refs[:SSTEP]
    last_ref, sums_ref, vec_ref = refs[SSTEP:]
    rows, cols = last_ref.shape
    inverse = inv_ref[:, :1]
    own = pl.ds(pl.multiple_of(lax.axis_index("tp") * cols, HD), cols)
    vec = part_ref[...] + recv_ref[...].astype(F32)
    if part_ref.shape[1] != cols:
        vec_ref[...] = vec
        vec = vec_ref[:, own]
    last_ref[...] = inverse * (gain_ref[:, own] * vec)
    all_k = list(kry) + [last_ref]
    count = SSTEP * (SSTEP + 1) // 2 + SSTEP
    acc = [jnp.zeros((8, HD), F32) for _ in range(count)]
    for r in range(0, rows, 8):
        for c in range(0, cols, HD):
            ks = [k[r : r + 8, c : c + HD] for k in all_k]
            ds = [ks[i] - ks[i + 1] for i in range(SSTEP)]
            i = 0
            for a in range(SSTEP):
                for b in range(a + 1):
                    acc[i] = acc[i] + ds[a] * ds[b]
                    i += 1
            for a in range(SSTEP):
                acc[i] = acc[i] + ds[a] * ks[0]
                i += 1
    lane = lax.broadcasted_iota(jnp.int32, (1, HD), 1)
    out = jnp.zeros((1, HD), F32)
    for i in range(count):
        line = jnp.sum(acc[i], axis=0, keepdims=True)
        out = jnp.where(lane == i, jnp.sum(line, axis=1, keepdims=True), out)
    for r in range(sums_ref.shape[0]):
        sums_ref[r] = out


def solve(gram, right):
    n = len(right)
    low = [[None] * n for _ in range(n)]
    for i in range(n):
        for j in range(i + 1):
            run = gram[i][j]
            for k in range(j):
                run = run - low[i][k] * low[j][k]
            low[i][j] = jnp.sqrt(run) if i == j else run / low[j][j]
    mid = []
    for i in range(n):
        run = right[i]
        for j in range(i):
            run = run - low[i][j] * mid[j]
        mid.append(run / low[i][i])
    out = [None] * n
    for i in range(n - 1, -1, -1):
        run = mid[i]
        for j in range(i + 1, n):
            run = run - low[j][i] * out[j]
        out[i] = run / low[i][i]
    return out


def finish_body(sums_ref, *refs):
    kry = refs[: SSTEP + 1]
    adj_ref, res_ref = refs[SSTEP + 1 :]
    total = jnp.sum(sums_ref[...], axis=0)
    lane = lax.broadcasted_iota(jnp.int32, total.shape, 1)
    count = SSTEP * (SSTEP + 1) // 2 + SSTEP
    vals = [
        jnp.sum(jnp.where(lane == i, total, 0.0), axis=1, keepdims=True) for i in range(count)
    ]
    idx = 0
    gram = [[None] * SSTEP for _ in range(SSTEP)]
    for a in range(SSTEP):
        for b in range(a + 1):
            gram[a][b] = vals[idx]
            idx += 1
    right = [vals[idx + a] for a in range(SSTEP)]
    coef = solve(gram, right)
    ks = [k[...] for k in kry]
    adj = coef[0] * ks[0]
    res = ks[0] - coef[0] * (ks[0] - ks[1])
    for i in range(1, SSTEP):
        adj = adj + coef[i] * ks[i]
        res = res - coef[i] * (ks[i] - ks[i + 1])
    adj_ref[...] = adj
    res_ref[...] = res


def swap_partner(c, d, odd):
    return c + d if (c // d) % 2 == odd else c - d


def on_device(state, cotangent, norm_gain, w_query, w_key, w_value, w_out):
    rows, cols = state.shape
    width = w_query.shape[1]
    heads = width // HD
    half = WIN // 2
    seq = lax.axis_size("seq")
    tps = lax.axis_size("tp")
    chips = seq // 2
    hops = hops_of(half, rows)
    blocks = 1 + len(hops)
    groups = groups_of(blocks)
    wide = [2 * (hi - lo) * rows for lo, hi in groups]
    ranks = seq * tps
    full = tps * cols

    def swap_core(x):
        return lax.ppermute(x, "seq", [(i, i ^ 1) for i in range(seq)])

    def tp_blocks(x):
        out = [x]
        for k in range(1, tps):
            out.append(lax.ppermute(x, "tp", [((i + k) % tps, i) for i in range(tps)]))
        return out

    def hop(x, i):
        d, odd = hops[i]
        pairs = []
        for c in range(chips):
            q = swap_partner(c, d, odd)
            if 0 <= q < chips:
                pairs += [(2 * c, 2 * q), (2 * c + 1, 2 * q + 1)]
            else:
                pairs += [(2 * c, 2 * c + 1), (2 * c + 1, 2 * c)]
        return lax.ppermute(x, "seq", pairs)

    def fetch(x):
        return [x] + [hop(x, i) for i in range(len(hops))]

    raw = len(hops) // 2
    states = tp_blocks(state)
    pieces = []
    for i in range(raw):
        pieces += tp_blocks(hop(state, i))
    cot_low, states[0], gain = kernel_call(
        early_body,
        [sds(rows, cols, dtype=BF16), state, sds(1, full)],
        [cotangent, state, norm_gain[None, :]],
    )
    normed, inv = kernel_call(
        functools.partial(norm_body, tps),
        [sds(rows, full, dtype=BF16), sds(rows, HD)],
        states + [gain],
    )
    done = [normed] + [hop(normed, i) for i in range(raw, len(hops))]
    held = [w_query, w_key, w_value, w_out]
    w_query, w_key, w_value, w_out = kernel_call(
        prep_body,
        held,
        held,
        scratch=[pltpu.SemaphoreType.DMA((len(held),))],
        hbm=len(held),
        limit=49 << 20,
    )
    cots = tp_blocks(cot_low)
    kv_mine, normed = kernel_call(
        functools.partial(kv_body, raw, len(done), tps),
        [
            sds(blocks * rows, 2 * width, dtype=BF16),
            sds(blocks * rows, full, dtype=BF16),
        ],
        pieces + done + [gain, w_key, w_value],
    )
    kv_other = swap_core(kv_mine)
    q_mine, s_mine = kernel_call(
        functools.partial(q_body, rows),
        [sds(blocks * rows, width, dtype=BF16), sds(heads, rows, blocks * rows)],
        [normed, w_query, kv_mine],
    )
    q_other = swap_core(q_mine)
    probs, att, packed = kernel_call(
        functools.partial(stats_body, half, tps),
        [sds(heads, rows, 2 * blocks * rows), sds(rows, width), sds(rows + PAD, width, dtype=BF16)],
        cots + [kv_mine, kv_other, q_mine, s_mine, w_out],
        scratch=[pltpu.VMEM((rows, full), BF16)],
    )
    fold = tps == 2
    if fold:
        (wo_half,) = kernel_call(half_rows_body, [sds(width // 2, full, dtype=BF16)], [w_out])
        wo_mine = tp_blocks(wo_half)[1]
    krylov = [cotangent]
    side = None
    for n in range(SSTEP):
        first, last = n == 0, n == SSTEP - 1
        if first:
            pts = kernel_call(
                functools.partial(scores_t_body, half),
                [sds(heads, rows, w) for w in wide],
                [q_mine, q_other, kv_mine],
            )
        got = fetch(packed)
        got = got + [swap_core(x) for x in got]
        folded = fold and 1 <= n < SSTEP - 1
        if side is not None:
            mine, other = kernel_call(
                side_body,
                [sds(rows, cols), sds(rows, cols, dtype=BF16)],
                side + [w_query, w_key, w_value],
                scratch=[pltpu.VMEM((rows, full), F32)],
            )
            other = tp_blocks(other)[1]
            (kry,) = kernel_call(
                side_sum_body, [sds(rows, cols)], [mine, other, inv, gain]
            )
            krylov.append(kry)
            side = None
        inputs = [packed, att, probs, kv_mine, kv_other]
        if folded:
            gq, *part_q = kernel_call(
                query_fold_body,
                [sds(rows, width, dtype=BF16), sds(rows, width), sds(rows, width)],
                inputs + [folds],
            )
        else:
            part_q = kernel_call(
                query_body,
                [sds(rows, full)],
                inputs + [w_query],
                scratch=[pltpu.VMEM((rows, width), BF16)],
            )
        static = [kv_mine, q_mine, q_other]
        grads = []
        new_pts = []
        for g in range(2):
            lo, hi = groups[g]
            res = kernel_call(
                functools.partial(key_part_body, groups[g], first),
                [sds(rows, width), sds(rows, width)]
                + ([sds(heads, rows, wide[g])] if first else []),
                got[lo:hi] + got[blocks + lo : blocks + hi] + [pts[g]] + static + grads,
                scratch=[pltpu.VMEM((wide[g], width), BF16)],
            )
            grads = list(res[:2])
            new_pts += list(res[2:])
        halved = last and tps == 2
        span = cols if halved else full
        lo, hi = groups[2]
        if folded:
            own, send, gk, gv = kernel_call(
                functools.partial(key_fold_body, groups[2]),
                [sds(rows, width), sds(rows, width, dtype=BF16)]
                + [sds(rows, width, dtype=BF16)] * 2,
                got[lo:hi]
                + got[blocks + lo : blocks + hi]
                + [pts[2]]
                + static
                + grads
                + [folds]
                + list(part_q),
                scratch=[pltpu.VMEM((wide[2], width), BF16)],
            )
            recv = tp_blocks(send)[1]
            (packed,) = kernel_call(
                combine_fold_body,
                [sds(rows + PAD, width, dtype=BF16)],
                [own, recv, inv, att],
            )
            side = [gq, gk, gv]
            continue
        res = kernel_call(
            functools.partial(key_last_body, groups[2], first, halved),
            [sds(rows, span), sds(rows, span, dtype=BF16)]
            + ([sds(heads, rows, wide[2])] if first else []),
            got[lo:hi]
            + got[blocks + lo : blocks + hi]
            + [pts[2]]
            + static
            + grads
            + [w_key, w_value]
            + list(part_q),
            scratch=[pltpu.VMEM((wide[2], width), BF16), pltpu.VMEM((rows, full), F32)],
        )
        part, send = res[:2]
        if first:
            pts = new_pts + list(res[2:])
        k = 1
        while True:
            recv = lax.ppermute(send, "tp", [(i, i ^ k) for i in range(tps)])
            k *= 2
            if k >= tps:
                break
            part = part + recv.astype(F32)
            send = part.astype(BF16)
        if fold and first:
            wo_other = swap_core(wo_mine)
            (folds,) = kernel_call(
                fold_body,
                [sds(2, 3, width, width, dtype=BF16)],
                [w_out, wo_mine, wo_other, gain, w_query, w_key, w_value],
                scratch=[pltpu.VMEM((width, full), BF16)],
                limit=16 << 20,
            )
        if not last:
            kry, packed = kernel_call(
                combine_body,
                [sds(rows, cols), sds(rows + PAD, width, dtype=BF16)],
                [part, recv, inv, gain, w_out, att],
                scratch=[pltpu.VMEM((rows, full), F32)],
            )
        else:
            kry, sums = kernel_call(
                gram_body,
                [sds(rows, cols), sds(ranks, 1, HD)],
                [part, recv, inv, gain] + krylov,
                scratch=[pltpu.VMEM((rows, full), F32)],
            )
        krylov.append(kry)
    sums = lax.all_to_all(sums, ("seq", "tp"), 0, 0)
    adjoint, residual = kernel_call(
        finish_body,
        [sds(rows, cols), sds(rows, cols)],
        [sums] + krylov,
    )
    return (adjoint, residual)


def solution(mesh):
    in_specs = (
        P("seq", "tp"),
        P("seq", "tp"),
        P(),
        P(None, "tp"),
        P(None, "tp"),
        P(None, "tp"),
        P("tp", None),
    )
    out_specs = (P("seq", "tp"), P("seq", "tp"))
    return jax.shard_map(
        on_device, mesh=mesh, in_specs=in_specs, out_specs=out_specs, check_vma=False
    )
```

```python
import functools
import math

import jax
import jax.numpy as jnp
from jax import lax
from jax.experimental import pallas as pl
from jax.experimental.pallas import tpu as pltpu
from jax.sharding import PartitionSpec as P


HD = 128
WIN = 1024
SSTEP = 4
EPSILON = 1e-05
PAD = 8
NEG = -1e30
SCALE = 1.0 / math.sqrt(HD)
NT = (((1,), (1,)), ((), ()))
NN = (((1,), (0,)), ((), ()))
F32 = jnp.float32
BF16 = jnp.bfloat16


def mm(a, b, dims=NN):
    return lax.dot_general(a, b, dims, preferred_element_type=F32)


def col(h):
    return slice(h * HD, (h + 1) * HD)


def kernel_call(body, outs, ins, scratch=(), hbm=0, flops=10**8, limit=12 << 20):
    in_specs = [pl.BlockSpec(memory_space=pltpu.HBM)] * hbm
    in_specs += [pl.BlockSpec(memory_space=pltpu.VMEM)] * (len(ins) - hbm)
    moved = sum(math.prod(a.shape) * a.dtype.itemsize for a in list(ins) + list(outs))
    return pl.pallas_call(
        body,
        out_shape=[jax.ShapeDtypeStruct(o.shape, o.dtype) for o in outs],
        in_specs=in_specs,
        out_specs=[pl.BlockSpec(memory_space=pltpu.VMEM)] * len(outs),
        scratch_shapes=list(scratch),
        compiler_params=pltpu.CompilerParams(vmem_limit_bytes=limit),
        cost_estimate=pl.CostEstimate(flops=flops, bytes_accessed=moved, transcendentals=0),
    )(*ins)


def sds(*shape, dtype=F32):
    return jax.ShapeDtypeStruct(shape, dtype)


def parts_of(x):
    hi = x.astype(BF16).astype(F32)
    rest = x - hi
    mid = rest.astype(BF16).astype(F32)
    low = (rest - mid).astype(BF16).astype(F32)
    return [hi, mid, low]


def pack_rows(out_ref, rows, heads, columns):
    lane = lax.broadcasted_iota(jnp.int32, (rows, HD), 1)
    mat = jnp.zeros((rows, HD), F32)
    for i, c in enumerate(columns):
        mat = jnp.where(lane == i, c, mat)
    pieces = parts_of(mat.T)
    sub = lax.broadcasted_iota(jnp.int32, (PAD, rows), 0)
    for h in range(heads):
        tile = jnp.zeros((PAD, rows), F32)
        for kind in range(len(columns) // heads):
            r = kind * heads + h
            for i, piece in enumerate(pieces):
                tile = jnp.where(sub == 3 * kind + i, piece[r : r + 1, :], tile)
        out_ref[rows : rows + PAD, col(h)] = tile.astype(BF16)


def unpack_row(slots, rows, h, kind):
    pieces = []
    for s in slots:
        t = s[rows : rows + PAD, col(h)].astype(F32)
        k = 3 * kind
        pieces.append(t[k : k + 1] + t[k + 1 : k + 2] + t[k + 2 : k + 3])
    return jnp.concatenate(pieces, axis=1)


def slot_starts(half, rows):
    me, seq = lax.axis_index("seq"), lax.axis_size("seq")
    chip, core = me // 2, me % 2
    ids = [chip]
    for d, odd in hops_of(half, rows):
        ids.append(jnp.where((chip // d) % 2 == odd, chip + d, chip - d))
    out = []
    for k in (core, 1 - core):
        for q in ids:
            inside = (q >= 0) & (q < seq // 2)
            out.append(jnp.where(inside, (2 * q + k) * rows, -(1 << 24)))
    return out


def hops_of(half, rows):
    reach = (half + rows - 1) // rows
    return [(d, odd) for odd in (1, 0) for d in range(1, (reach + 1) // 2 + 1)]


def masks_of(half, rows):
    starts = slot_starts(half, rows)
    sub = lax.broadcasted_iota(jnp.int32, (rows, rows), 0)
    lane = lax.broadcasted_iota(jnp.int32, (rows, rows), 1)
    return [jnp.abs(lane - sub + (st - starts[0])) <= half for st in starts]


def masked(s, masks):
    rows = s.shape[0]
    pieces = [
        jnp.where(m, s[:, b * rows : (b + 1) * rows], NEG) for b, m in enumerate(masks)
    ]
    return jnp.concatenate(pieces, axis=1)


def feature_slices(tps, cols):
    me = lax.axis_index("tp")
    return [pl.ds(pl.multiple_of(((me + k) % tps) * cols, HD), cols) for k in range(tps)]


def early_body(cot_ref, state_ref, gain_ref, cot_out, state_out, gain_out):
    cot_out[...] = cot_ref[...].astype(BF16)
    state_out[...] = state_ref[...]
    gain_out[...] = gain_ref[...]


def prep_body(*refs):
    count = len(refs) // 2
    sources, outs, sems = refs[:count], refs[count : 2 * count], refs[-1]
    copies = [
        pltpu.make_async_copy(src, dst, sems.at[i])
        for i, (src, dst) in enumerate(zip(sources, outs))
    ]
    for c in copies:
        c.start()
    for c in copies:
        c.wait()


def norm_block(xs, gain_ref, at):
    total = jnp.zeros((xs[0].shape[0], 1), F32)
    vals = [x[...].astype(F32) for x in xs]
    for x in vals:
        total = total + jnp.sum(x * x, axis=1, keepdims=True)
    inverse = lax.rsqrt(total / (len(xs) * xs[0].shape[1]) + EPSILON)
    return inverse, [(x * inverse * gain_ref[:, sl]).astype(BF16) for x, sl in zip(vals, at)]


def norm_body(tps, *refs):
    xs = refs[:tps]
    gain_ref, normed_ref, inv_ref = refs[tps:]
    at = feature_slices(tps, xs[0].shape[1])
    inverse, pieces = norm_block(xs, gain_ref, at)
    inv_ref[...] = jnp.broadcast_to(inverse, inv_ref.shape)
    for sl, piece in zip(at, pieces):
        normed_ref[:, sl] = piece


def kv_body(raw, done, tps, *refs):
    xs = refs[: raw * tps]
    full = refs[raw * tps : raw * tps + done]
    gain_ref, wk_ref, wv_ref, kv_ref, normed_ref = refs[raw * tps + done :]
    rows = full[0].shape[0]
    width = wk_ref.shape[1]
    at = feature_slices(tps, full[0].shape[1] // tps)
    for b in range(raw):
        _, pieces = norm_block(xs[b * tps : (b + 1) * tps], gain_ref, at)
        for sl, piece in zip(at, pieces):
            normed_ref[(b + 1) * rows : (b + 2) * rows, sl] = piece
    for i, x in enumerate(full):
        b = i if i == 0 else i + raw
        normed_ref[b * rows : (b + 1) * rows, :] = x[...]
    x = normed_ref[...]
    kv_ref[:, :width] = mm(x, wk_ref[...]).astype(BF16)
    kv_ref[:, width:] = mm(x, wv_ref[...]).astype(BF16)


def q_body(rows, normed_ref, wq_ref, kv_ref, q_ref, s_ref):
    q_ref[...] = mm(normed_ref[...], wq_ref[...]).astype(BF16)
    for h in range(s_ref.shape[0]):
        s_ref[h] = mm(q_ref[:rows, col(h)], kv_ref[:, col(h)], NT) * SCALE


def stats_body(half, tps, *refs):
    cots = refs[:tps]
    kvm_ref, kvo_ref, q_ref, s_ref, wo_ref, p_ref, att_ref, packed_ref, cot_ref = refs[tps:]
    rows, width = att_ref.shape
    heads = width // HD
    near = kvm_ref.shape[0]
    masks = masks_of(half, rows)
    for c, at in zip(cots, feature_slices(tps, cots[0].shape[1])):
        cot_ref[:, at] = c[...]
    go = mm(cot_ref[...], wo_ref[...], NT).astype(BF16)
    packed_ref[:rows, :] = go
    lse, corr = [], []
    for h in range(heads):
        q = q_ref[:rows, col(h)]
        s = jnp.concatenate([s_ref[h], mm(q, kvo_ref[:, col(h)], NT) * SCALE], axis=1)
        s = masked(s, masks)
        peak = jnp.max(s, axis=1, keepdims=True)
        raw = jnp.exp(s - peak)
        total = jnp.sum(raw, axis=1, keepdims=True)
        probs = raw * (1.0 / total)
        p_ref[h] = probs
        low = probs.astype(BF16)
        att = mm(low[:, :near], kvm_ref[:, col(heads + h)])
        att = att + mm(low[:, near:], kvo_ref[:, col(heads + h)])
        att_ref[:, col(h)] = att
        lse.append(peak + jnp.log(total))
        corr.append(jnp.sum(go[:, col(h)].astype(F32) * att, axis=1, keepdims=True))
    pack_rows(packed_ref, rows, heads, corr + lse)


def groups_of(blocks):
    cut = 1 + (blocks - 1) // 2
    return [(0, 1), (1, cut), (cut, blocks)]


def scores_t_body(half, qm_ref, qo_ref, kv_ref, *outs):
    rows = outs[0].shape[1]
    masks = masks_of(half, rows)
    blocks = len(masks) // 2
    for h in range(outs[0].shape[0]):
        k = kv_ref[:rows, col(h)]
        for ref, (lo, hi) in zip(outs, groups_of(blocks)):
            part = slice(lo * rows, hi * rows)
            s = jnp.concatenate(
                [mm(k, qm_ref[part, col(h)], NT), mm(k, qo_ref[part, col(h)], NT)], axis=1
            )
            ref[h] = masked(s * SCALE, masks[lo:hi] + masks[blocks + lo : blocks + hi])


def query_grads(packed_ref, att_ref, p_ref, kvm_ref, kvo_ref, gq_ref):
    rows, width = att_ref.shape
    heads = width // HD
    near = kvm_ref.shape[0]
    for h in range(heads):
        go = packed_ref[:rows, col(h)]
        corr = jnp.sum(go.astype(F32) * att_ref[:, col(h)], axis=1, keepdims=True)
        v = col(heads + h)
        gp = jnp.concatenate([mm(go, kvm_ref[:, v], NT), mm(go, kvo_ref[:, v], NT)], axis=1)
        gs = (SCALE * p_ref[h] * (gp - corr)).astype(BF16)
        gq = mm(gs[:, :near], kvm_ref[:, col(h)]) + mm(gs[:, near:], kvo_ref[:, col(h)])
        gq_ref[:, col(h)] = gq.astype(BF16)


def query_body(packed_ref, att_ref, p_ref, kvm_ref, kvo_ref, wq_ref, part_ref, gq_ref):
    query_grads(packed_ref, att_ref, p_ref, kvm_ref, kvo_ref, gq_ref)
    part_ref[...] = mm(gq_ref[...], wq_ref[...], NT)


def key_terms(got, part, first, pt_in, pt_ref, kv_ref, qm_ref, qo_ref, gow_ref, h):
    rows, width = got[0].shape[0] - PAD, got[0].shape[1]
    near = part.stop - part.start
    corr = unpack_row(got, rows, h, 0)
    if first:
        pt = jnp.exp(pt_in[h] - unpack_row(got, rows, h, 1))
        pt_ref[h] = pt
    else:
        pt = pt_in[h]
    go = gow_ref[:, col(h)]
    gp = mm(kv_ref[:rows, col(width // HD + h)], go, NT)
    gs = (SCALE * pt * (gp - corr)).astype(BF16)
    gk = mm(gs[:, :near], qm_ref[part, col(h)]) + mm(gs[:, near:], qo_ref[part, col(h)])
    return gk, mm(pt.astype(BF16), go)


def key_part_body(span, first, *refs):
    lo, hi = span
    slots = 2 * (hi - lo)
    got = refs[:slots]
    pt_in, kv_ref, qm_ref, qo_ref = refs[slots : slots + 4]
    rest = list(refs[slots + 4 :])
    gow_ref = rest.pop()
    pt_ref = rest.pop() if first else None
    gk_ref, gv_ref = rest[-2:]
    before = rest[:-2]
    rows = got[0].shape[0] - PAD
    for b in range(slots):
        gow_ref[b * rows : (b + 1) * rows, :] = got[b][:rows, :]
    part = slice(lo * rows, hi * rows)
    for h in range(pt_in.shape[0]):
        gk, gv = key_terms(got, part, first, pt_in, pt_ref, kv_ref, qm_ref, qo_ref, gow_ref, h)
        if before:
            gk = gk + before[0][:, col(h)]
            gv = gv + before[1][:, col(h)]
        gk_ref[:, col(h)] = gk
        gv_ref[:, col(h)] = gv


def key_last_body(span, first, halved, *refs):
    lo, hi = span
    slots = 2 * (hi - lo)
    got = refs[:slots]
    pt_in, kv_ref, qm_ref, qo_ref, gk_ref, gv_ref, wk_ref, wv_ref, partq_ref = refs[
        slots : slots + 9
    ]
    part_ref, send_ref = refs[slots + 9 : slots + 11]
    pt_ref = refs[slots + 11] if first else None
    gow_ref, sum_ref = refs[-2:]
    rows = got[0].shape[0] - PAD
    for b in range(slots):
        gow_ref[b * rows : (b + 1) * rows, :] = got[b][:rows, :]
    part = slice(lo * rows, hi * rows)
    gks, gvs = [], []
    for h in range(pt_in.shape[0]):
        gk, gv = key_terms(got, part, first, pt_in, pt_ref, kv_ref, qm_ref, qo_ref, gow_ref, h)
        gks.append((gk_ref[:, col(h)] + gk).astype(BF16))
        gvs.append((gv_ref[:, col(h)] + gv).astype(BF16))
    acc = partq_ref[...] + mm(jnp.concatenate(gks, axis=1), wk_ref[...], NT)
    acc = acc + mm(jnp.concatenate(gvs, axis=1), wv_ref[...], NT)
    if halved:
        cols = part_ref.shape[1]
        sum_ref[...] = acc
        mine, other = feature_slices(2, cols)
        part_ref[...] = sum_ref[:, mine]
        send_ref[...] = sum_ref[:, other].astype(BF16)
    else:
        part_ref[...] = acc
        send_ref[...] = acc.astype(BF16)


def half_rows_body(w_ref, o_ref):
    n = o_ref.shape[0]
    core = lax.axis_index("seq") % 2
    o_ref[...] = w_ref[pl.ds(pl.multiple_of(core * n, n), n), :]


def fold_body(wo_ref, mine_ref, other_ref, gain_ref, wq_ref, wk_ref, wv_ref, ft_ref, full_ref):
    n = mine_ref.shape[0]
    core = lax.axis_index("seq") % 2
    full_ref[pl.ds(pl.multiple_of(core * n, n), n), :] = mine_ref[...]
    full_ref[pl.ds(pl.multiple_of((1 - core) * n, n), n), :] = other_ref[...]
    for i, ref in enumerate((wo_ref, full_ref)):
        scaled = (ref[...].astype(F32) * gain_ref[...]).astype(BF16)
        for j, w in enumerate((wq_ref, wk_ref, wv_ref)):
            ft_ref[i, j] = mm(scaled, w[...]).astype(BF16)


def query_fold_body(packed_ref, att_ref, p_ref, kvm_ref, kvo_ref, ft_ref, gq_ref, own_ref, oth_ref):
    query_grads(packed_ref, att_ref, p_ref, kvm_ref, kvo_ref, gq_ref)
    gq = gq_ref[...]
    own_ref[...] = mm(gq, ft_ref[0, 0], NT)
    oth_ref[...] = mm(gq, ft_ref[1, 0], NT)


def key_fold_body(span, *refs):
    lo, hi = span
    slots = 2 * (hi - lo)
    got = refs[:slots]
    pt_in, kv_ref, qm_ref, qo_ref, gk_in, gv_in, ft_ref, ownq_ref, othq_ref = refs[
        slots : slots + 9
    ]
    own_ref, send_ref, gk_ref, gv_ref, gow_ref = refs[slots + 9 :]
    rows = got[0].shape[0] - PAD
    for b in range(slots):
        gow_ref[b * rows : (b + 1) * rows, :] = got[b][:rows, :]
    part = slice(lo * rows, hi * rows)
    for h in range(pt_in.shape[0]):
        gk, gv = key_terms(got, part, False, pt_in, None, kv_ref, qm_ref, qo_ref, gow_ref, h)
        gk_ref[:, col(h)] = (gk_in[:, col(h)] + gk).astype(BF16)
        gv_ref[:, col(h)] = (gv_in[:, col(h)] + gv).astype(BF16)
    gk, gv = gk_ref[...], gv_ref[...]
    own_ref[...] = ownq_ref[...] + mm(gk, ft_ref[0, 1], NT) + mm(gv, ft_ref[0, 2], NT)
    oth = othq_ref[...] + mm(gk, ft_ref[1, 1], NT) + mm(gv, ft_ref[1, 2], NT)
    send_ref[...] = oth.astype(BF16)


def combine_fold_body(own_ref, recv_ref, inv_ref, att_ref, packed_ref):
    rows, width = att_ref.shape
    go = (inv_ref[:, :1] * (own_ref[...] + recv_ref[...].astype(F32))).astype(BF16)
    packed_ref[:rows, :] = go
    corr = [
        jnp.sum(go[:, col(h)].astype(F32) * att_ref[:, col(h)], axis=1, keepdims=True)
        for h in range(width // HD)
    ]
    pack_rows(packed_ref, rows, width // HD, corr)


def side_body(gq_ref, gk_ref, gv_ref, wq_ref, wk_ref, wv_ref, part_ref, send_ref, sum_ref):
    acc = mm(gq_ref[...], wq_ref[...], NT) + mm(gk_ref[...], wk_ref[...], NT)
    sum_ref[...] = acc + mm(gv_ref[...], wv_ref[...], NT)
    mine, other = feature_slices(2, part_ref.shape[1])
    part_ref[...] = sum_ref[:, mine]
    send_ref[...] = sum_ref[:, other].astype(BF16)


def side_sum_body(part_ref, recv_ref, inv_ref, gain_ref, kry_ref):
    mine = feature_slices(2, part_ref.shape[1])[0]
    vec = part_ref[...] + recv_ref[...].astype(F32)
    kry_ref[...] = inv_ref[:, :1] * (gain_ref[:, mine] * vec)


def combine_body(part_ref, recv_ref, inv_ref, gain_ref, wo_ref, att_ref, *refs):
    kry_ref, packed_ref, vec_ref = refs
    rows, width = att_ref.shape
    cols = kry_ref.shape[1]
    inverse = inv_ref[:, :1]
    vec = inverse * (gain_ref[...] * (part_ref[...] + recv_ref[...].astype(F32)))
    vec_ref[...] = vec
    off = pl.multiple_of(lax.axis_index("tp") * cols, HD)
    kry_ref[...] = vec_ref[:, pl.ds(off, cols)]
    go = mm(vec.astype(BF16), wo_ref[...], NT).astype(BF16)
    packed_ref[:rows, :] = go
    corr = [
        jnp.sum(go[:, col(h)].astype(F32) * att_ref[:, col(h)], axis=1, keepdims=True)
        for h in range(width // HD)
    ]
    pack_rows(packed_ref, rows, width // HD, corr)


def gram_body(part_ref, recv_ref, inv_ref, gain_ref, *refs):
    kry = refs[:SSTEP]
    last_ref, sums_ref, vec_ref = refs[SSTEP:]
    rows, cols = last_ref.shape
    inverse = inv_ref[:, :1]
    own = pl.ds(pl.multiple_of(lax.axis_index("tp") * cols, HD), cols)
    vec = part_ref[...] + recv_ref[...].astype(F32)
    if part_ref.shape[1] != cols:
        vec_ref[...] = vec
        vec = vec_ref[:, own]
    last_ref[...] = inverse * (gain_ref[:, own] * vec)
    all_k = list(kry) + [last_ref]
    count = SSTEP * (SSTEP + 1) // 2 + SSTEP
    acc = [jnp.zeros((8, HD), F32) for _ in range(count)]
    for r in range(0, rows, 8):
        for c in range(0, cols, HD):
            ks = [k[r : r + 8, c : c + HD] for k in all_k]
            ds = [ks[i] - ks[i + 1] for i in range(SSTEP)]
            i = 0
            for a in range(SSTEP):
                for b in range(a + 1):
                    acc[i] = acc[i] + ds[a] * ds[b]
                    i += 1
            for a in range(SSTEP):
                acc[i] = acc[i] + ds[a] * ks[0]
                i += 1
    lane = lax.broadcasted_iota(jnp.int32, (1, HD), 1)
    out = jnp.zeros((1, HD), F32)
    for i in range(count):
        line = jnp.sum(acc[i], axis=0, keepdims=True)
        out = jnp.where(lane == i, jnp.sum(line, axis=1, keepdims=True), out)
    for r in range(sums_ref.shape[0]):
        sums_ref[r] = out


def solve(gram, right):
    n = len(right)
    low = [[None] * n for _ in range(n)]
    for i in range(n):
        for j in range(i + 1):
            run = gram[i][j]
            for k in range(j):
                run = run - low[i][k] * low[j][k]
            low[i][j] = jnp.sqrt(run) if i == j else run / low[j][j]
    mid = []
    for i in range(n):
        run = right[i]
        for j in range(i):
            run = run - low[i][j] * mid[j]
        mid.append(run / low[i][i])
    out = [None] * n
    for i in range(n - 1, -1, -1):
        run = mid[i]
        for j in range(i + 1, n):
            run = run - low[j][i] * out[j]
        out[i] = run / low[i][i]
    return out


def finish_body(sums_ref, *refs):
    kry = refs[: SSTEP + 1]
    adj_ref, res_ref = refs[SSTEP + 1 :]
    total = jnp.sum(sums_ref[...], axis=0)
    lane = lax.broadcasted_iota(jnp.int32, total.shape, 1)
    count = SSTEP * (SSTEP + 1) // 2 + SSTEP
    vals = [
        jnp.sum(jnp.where(lane == i, total, 0.0), axis=1, keepdims=True) for i in range(count)
    ]
    idx = 0
    gram = [[None] * SSTEP for _ in range(SSTEP)]
    for a in range(SSTEP):
        for b in range(a + 1):
            gram[a][b] = vals[idx]
            idx += 1
    right = [vals[idx + a] for a in range(SSTEP)]
    coef = solve(gram, right)
    ks = [k[...] for k in kry]
    adj = coef[0] * ks[0]
    res = ks[0] - coef[0] * (ks[0] - ks[1])
    for i in range(1, SSTEP):
        adj = adj + coef[i] * ks[i]
        res = res - coef[i] * (ks[i] - ks[i + 1])
    adj_ref[...] = adj
    res_ref[...] = res


def swap_partner(c, d, odd):
    return c + d if (c // d) % 2 == odd else c - d


def on_device(state, cotangent, norm_gain, w_query, w_key, w_value, w_out):
    rows, cols = state.shape
    width = w_query.shape[1]
    heads = width // HD
    half = WIN // 2
    seq = lax.axis_size("seq")
    tps = lax.axis_size("tp")
    chips = seq // 2
    hops = hops_of(half, rows)
    blocks = 1 + len(hops)
    groups = groups_of(blocks)
    wide = [2 * (hi - lo) * rows for lo, hi in groups]
    ranks = seq * tps
    full = tps * cols

    def swap_core(x):
        return lax.ppermute(x, "seq", [(i, i ^ 1) for i in range(seq)])

    def tp_blocks(x):
        out = [x]
        for k in range(1, tps):
            out.append(lax.ppermute(x, "tp", [((i + k) % tps, i) for i in range(tps)]))
        return out

    def hop(x, i):
        d, odd = hops[i]
        pairs = []
        for c in range(chips):
            q = swap_partner(c, d, odd)
            if 0 <= q < chips:
                pairs += [(2 * c, 2 * q), (2 * c + 1, 2 * q + 1)]
            else:
                pairs += [(2 * c, 2 * c + 1), (2 * c + 1, 2 * c)]
        return lax.ppermute(x, "seq", pairs)

    def fetch(x):
        return [x] + [hop(x, i) for i in range(len(hops))]

    raw = len(hops) // 2
    states = tp_blocks(state)
    pieces = []
    for i in range(raw):
        pieces += tp_blocks(hop(state, i))
    cot_low, states[0], gain = kernel_call(
        early_body,
        [sds(rows, cols, dtype=BF16), state, sds(1, full)],
        [cotangent, state, norm_gain[None, :]],
    )
    normed, inv = kernel_call(
        functools.partial(norm_body, tps),
        [sds(rows, full, dtype=BF16), sds(rows, HD)],
        states + [gain],
    )
    done = [normed] + [hop(normed, i) for i in range(raw, len(hops))]
    held = [w_query, w_key, w_value, w_out]
    w_query, w_key, w_value, w_out = kernel_call(
        prep_body,
        held,
        held,
        scratch=[pltpu.SemaphoreType.DMA((len(held),))],
        hbm=len(held),
        limit=49 << 20,
    )
    cots = tp_blocks(cot_low)
    kv_mine, normed = kernel_call(
        functools.partial(kv_body, raw, len(done), tps),
        [
            sds(blocks * rows, 2 * width, dtype=BF16),
            sds(blocks * rows, full, dtype=BF16),
        ],
        pieces + done + [gain, w_key, w_value],
    )
    kv_other = swap_core(kv_mine)
    q_mine, s_mine = kernel_call(
        functools.partial(q_body, rows),
        [sds(blocks * rows, width, dtype=BF16), sds(heads, rows, blocks * rows)],
        [normed, w_query, kv_mine],
    )
    q_other = swap_core(q_mine)
    probs, att, packed = kernel_call(
        functools.partial(stats_body, half, tps),
        [sds(heads, rows, 2 * blocks * rows), sds(rows, width), sds(rows + PAD, width, dtype=BF16)],
        cots + [kv_mine, kv_other, q_mine, s_mine, w_out],
        scratch=[pltpu.VMEM((rows, full), BF16)],
    )
    fold = tps == 2
    if fold:
        (wo_half,) = kernel_call(half_rows_body, [sds(width // 2, full, dtype=BF16)], [w_out])
        wo_mine = tp_blocks(wo_half)[1]
    krylov = [cotangent]
    side = None
    for n in range(SSTEP):
        first, last = n == 0, n == SSTEP - 1
        if first:
            pts = kernel_call(
                functools.partial(scores_t_body, half),
                [sds(heads, rows, w) for w in wide],
                [q_mine, q_other, kv_mine],
            )
        got = fetch(packed)
        got = got + [swap_core(x) for x in got]
        folded = fold and 1 <= n < SSTEP - 1
        if side is not None:
            mine, other = side
            other = tp_blocks(other)[1]
            (kry,) = kernel_call(
                side_sum_body, [sds(rows, cols)], [mine, other, inv, gain]
            )
            krylov.append(kry)
            side = None
        inputs = [packed, att, probs, kv_mine, kv_other]
        if folded:
            gq, *part_q = kernel_call(
                query_fold_body,
                [sds(rows, width, dtype=BF16), sds(rows, width), sds(rows, width)],
                inputs + [folds],
            )
        else:
            part_q = kernel_call(
                query_body,
                [sds(rows, full)],
                inputs + [w_query],
                scratch=[pltpu.VMEM((rows, width), BF16)],
            )
        static = [kv_mine, q_mine, q_other]
        grads = []
        new_pts = []
        for g in range(2):
            lo, hi = groups[g]
            res = kernel_call(
                functools.partial(key_part_body, groups[g], first),
                [sds(rows, width), sds(rows, width)]
                + ([sds(heads, rows, wide[g])] if first else []),
                got[lo:hi] + got[blocks + lo : blocks + hi] + [pts[g]] + static + grads,
                scratch=[pltpu.VMEM((wide[g], width), BF16)],
            )
            grads = list(res[:2])
            new_pts += list(res[2:])
        halved = last and tps == 2
        span = cols if halved else full
        lo, hi = groups[2]
        if folded:
            own, send, gk, gv = kernel_call(
                functools.partial(key_fold_body, groups[2]),
                [sds(rows, width), sds(rows, width, dtype=BF16)]
                + [sds(rows, width, dtype=BF16)] * 2,
                got[lo:hi]
                + got[blocks + lo : blocks + hi]
                + [pts[2]]
                + static
                + grads
                + [folds]
                + list(part_q),
                scratch=[pltpu.VMEM((wide[2], width), BF16)],
            )
            recv = tp_blocks(send)[1]
            (packed,) = kernel_call(
                combine_fold_body,
                [sds(rows + PAD, width, dtype=BF16)],
                [own, recv, inv, att],
            )
            side = kernel_call(
                side_body,
                [sds(rows, cols), sds(rows, cols, dtype=BF16)],
                [gq, gk, gv, w_query, w_key, w_value],
                scratch=[pltpu.VMEM((rows, full), F32)],
            )
            continue
        res = kernel_call(
            functools.partial(key_last_body, groups[2], first, halved),
            [sds(rows, span), sds(rows, span, dtype=BF16)]
            + ([sds(heads, rows, wide[2])] if first else []),
            got[lo:hi]
            + got[blocks + lo : blocks + hi]
            + [pts[2]]
            + static
            + grads
            + [w_key, w_value]
            + list(part_q),
            scratch=[pltpu.VMEM((wide[2], width), BF16), pltpu.VMEM((rows, full), F32)],
        )
        part, send = res[:2]
        if first:
            pts = new_pts + list(res[2:])
        k = 1
        while True:
            recv = lax.ppermute(send, "tp", [(i, i ^ k) for i in range(tps)])
            k *= 2
            if k >= tps:
                break
            part = part + recv.astype(F32)
            send = part.astype(BF16)
        if fold and first:
            wo_other = swap_core(wo_mine)
            (folds,) = kernel_call(
                fold_body,
                [sds(2, 3, width, width, dtype=BF16)],
                [w_out, wo_mine, wo_other, gain, w_query, w_key, w_value],
                scratch=[pltpu.VMEM((width, full), BF16)],
                limit=16 << 20,
            )
        if not last:
            kry, packed = kernel_call(
                combine_body,
                [sds(rows, cols), sds(rows + PAD, width, dtype=BF16)],
                [part, recv, inv, gain, w_out, att],
                scratch=[pltpu.VMEM((rows, full), F32)],
            )
        else:
            kry, sums = kernel_call(
                gram_body,
                [sds(rows, cols), sds(ranks, 1, HD)],
                [part, recv, inv, gain] + krylov,
                scratch=[pltpu.VMEM((rows, full), F32)],
            )
        krylov.append(kry)
    sums = lax.all_to_all(sums, ("seq", "tp"), 0, 0)
    adjoint, residual = kernel_call(
        finish_body,
        [sds(rows, cols), sds(rows, cols)],
        [sums] + krylov,
    )
    return (adjoint, residual)


def solution(mesh):
    in_specs = (
        P("seq", "tp"),
        P("seq", "tp"),
        P(),
        P(None, "tp"),
        P(None, "tp"),
        P(None, "tp"),
        P("tp", None),
    )
    out_specs = (P("seq", "tp"), P("seq", "tp"))
    return jax.shard_map(
        on_device, mesh=mesh, in_specs=in_specs, out_specs=out_specs, check_vma=False
    )
```

```python
import functools
import math

import jax
import jax.numpy as jnp
from jax import lax
from jax.experimental import pallas as pl
from jax.experimental.pallas import tpu as pltpu
from jax.sharding import PartitionSpec as P


HD = 128
WIN = 1024
SSTEP = 4
EPSILON = 1e-05
PAD = 8
NEG = -1e30
SCALE = 1.0 / math.sqrt(HD)
NT = (((1,), (1,)), ((), ()))
NN = (((1,), (0,)), ((), ()))
F32 = jnp.float32
BF16 = jnp.bfloat16


def mm(a, b, dims=NN):
    return lax.dot_general(a, b, dims, preferred_element_type=F32)


def col(h):
    return slice(h * HD, (h + 1) * HD)


def kernel_call(body, outs, ins, scratch=(), hbm=0, flops=10**8, limit=12 << 20, aliases=None):
    in_specs = [pl.BlockSpec(memory_space=pltpu.HBM)] * hbm
    in_specs += [pl.BlockSpec(memory_space=pltpu.VMEM)] * (len(ins) - hbm)
    moved = sum(math.prod(a.shape) * a.dtype.itemsize for a in list(ins) + list(outs))
    return pl.pallas_call(
        body,
        out_shape=[jax.ShapeDtypeStruct(o.shape, o.dtype) for o in outs],
        in_specs=in_specs,
        out_specs=[pl.BlockSpec(memory_space=pltpu.VMEM)] * len(outs),
        scratch_shapes=list(scratch),
        input_output_aliases=aliases or {},
        compiler_params=pltpu.CompilerParams(vmem_limit_bytes=limit),
        cost_estimate=pl.CostEstimate(flops=flops, bytes_accessed=moved, transcendentals=0),
    )(*ins)


def sds(*shape, dtype=F32):
    return jax.ShapeDtypeStruct(shape, dtype)


def parts_of(x):
    hi = x.astype(BF16).astype(F32)
    rest = x - hi
    mid = rest.astype(BF16).astype(F32)
    low = (rest - mid).astype(BF16).astype(F32)
    return [hi, mid, low]


def pack_rows(out_ref, rows, heads, columns):
    lane = lax.broadcasted_iota(jnp.int32, (rows, HD), 1)
    mat = jnp.zeros((rows, HD), F32)
    for i, c in enumerate(columns):
        mat = jnp.where(lane == i, c, mat)
    pieces = parts_of(mat.T)
    sub = lax.broadcasted_iota(jnp.int32, (PAD, rows), 0)
    for h in range(heads):
        tile = jnp.zeros((PAD, rows), F32)
        for kind in range(len(columns) // heads):
            r = kind * heads + h
            for i, piece in enumerate(pieces):
                tile = jnp.where(sub == 3 * kind + i, piece[r : r + 1, :], tile)
        out_ref[rows : rows + PAD, col(h)] = tile.astype(BF16)


def unpack_row(slots, rows, h, kind):
    pieces = []
    for s in slots:
        t = s[rows : rows + PAD, col(h)].astype(F32)
        k = 3 * kind
        pieces.append(t[k : k + 1] + t[k + 1 : k + 2] + t[k + 2 : k + 3])
    return jnp.concatenate(pieces, axis=1)


def slot_starts(half, rows):
    me, seq = lax.axis_index("seq"), lax.axis_size("seq")
    chip, core = me // 2, me % 2
    ids = [chip]
    for d, odd in hops_of(half, rows):
        ids.append(jnp.where((chip // d) % 2 == odd, chip + d, chip - d))
    out = []
    for k in (core, 1 - core):
        for q in ids:
            inside = (q >= 0) & (q < seq // 2)
            out.append(jnp.where(inside, (2 * q + k) * rows, -(1 << 24)))
    return out


def hops_of(half, rows):
    reach = (half + rows - 1) // rows
    return [(d, odd) for odd in (1, 0) for d in range(1, (reach + 1) // 2 + 1)]


def masks_of(half, rows):
    starts = slot_starts(half, rows)
    sub = lax.broadcasted_iota(jnp.int32, (rows, rows), 0)
    lane = lax.broadcasted_iota(jnp.int32, (rows, rows), 1)
    return [jnp.abs(lane - sub + (st - starts[0])) <= half for st in starts]


def masked(s, masks):
    rows = s.shape[0]
    pieces = [
        jnp.where(m, s[:, b * rows : (b + 1) * rows], NEG) for b, m in enumerate(masks)
    ]
    return jnp.concatenate(pieces, axis=1)


def feature_slices(tps, cols):
    me = lax.axis_index("tp")
    return [pl.ds(pl.multiple_of(((me + k) % tps) * cols, HD), cols) for k in range(tps)]


def early_body(cot_ref, state_ref, gain_ref, cot_out, state_out, gain_out):
    cot_out[...] = cot_ref[...].astype(BF16)
    state_out[...] = state_ref[...]
    gain_out[...] = gain_ref[...]


def prep_body(*refs):
    count = len(refs) // 2
    sources, outs, sems = refs[:count], refs[count : 2 * count], refs[-1]
    copies = [
        pltpu.make_async_copy(src, dst, sems.at[i])
        for i, (src, dst) in enumerate(zip(sources, outs))
    ]
    for c in copies:
        c.start()
    for c in copies:
        c.wait()


def norm_block(xs, gain_ref, at):
    total = jnp.zeros((xs[0].shape[0], 1), F32)
    vals = [x[...].astype(F32) for x in xs]
    for x in vals:
        total = total + jnp.sum(x * x, axis=1, keepdims=True)
    inverse = lax.rsqrt(total / (len(xs) * xs[0].shape[1]) + EPSILON)
    return inverse, [(x * inverse * gain_ref[:, sl]).astype(BF16) for x, sl in zip(vals, at)]


def norm_body(tps, *refs):
    xs = refs[:tps]
    gain_ref, normed_ref, inv_ref = refs[tps:]
    at = feature_slices(tps, xs[0].shape[1])
    inverse, pieces = norm_block(xs, gain_ref, at)
    inv_ref[...] = jnp.broadcast_to(inverse, inv_ref.shape)
    for sl, piece in zip(at, pieces):
        normed_ref[:, sl] = piece


def kv_first_body(raw, done, *refs):
    full = refs[:done]
    wk_ref, wv_ref, kv_ref, normed_ref = refs[done:]
    rows = full[0].shape[0]
    width = wk_ref.shape[1]
    x = jnp.concatenate([r[...] for r in full], axis=0)
    keys = mm(x, wk_ref[...]).astype(BF16)
    values = mm(x, wv_ref[...]).astype(BF16)
    for i, ref in enumerate(full):
        b = i if i == 0 else i + raw
        there, here = slice(b * rows, (b + 1) * rows), slice(i * rows, (i + 1) * rows)
        normed_ref[there, :] = ref[...]
        kv_ref[there, :width] = keys[here]
        kv_ref[there, width:] = values[here]


def kv_rest_body(raw, tps, *refs):
    xs = refs[: raw * tps]
    gain_ref, wk_ref, wv_ref, _, _, kv_ref, normed_ref = refs[raw * tps :]
    rows, cols = xs[0].shape
    width = wk_ref.shape[1]
    at = feature_slices(tps, cols)
    for b in range(raw):
        _, pieces = norm_block(xs[b * tps : (b + 1) * tps], gain_ref, at)
        for sl, piece in zip(at, pieces):
            normed_ref[(b + 1) * rows : (b + 2) * rows, sl] = piece
    new = slice(rows, (raw + 1) * rows)
    x = normed_ref[new, :]
    kv_ref[new, :width] = mm(x, wk_ref[...]).astype(BF16)
    kv_ref[new, width:] = mm(x, wv_ref[...]).astype(BF16)


def q_body(rows, normed_ref, wq_ref, kv_ref, q_ref, s_ref):
    q_ref[...] = mm(normed_ref[...], wq_ref[...]).astype(BF16)
    for h in range(s_ref.shape[0]):
        s_ref[h] = mm(q_ref[:rows, col(h)], kv_ref[:, col(h)], NT) * SCALE


def stats_body(half, tps, *refs):
    cots = refs[:tps]
    kvm_ref, kvo_ref, q_ref, s_ref, wo_ref, p_ref, att_ref, packed_ref, cot_ref = refs[tps:]
    rows, width = att_ref.shape
    heads = width // HD
    near = kvm_ref.shape[0]
    masks = masks_of(half, rows)
    for c, at in zip(cots, feature_slices(tps, cots[0].shape[1])):
        cot_ref[:, at] = c[...]
    go = mm(cot_ref[...], wo_ref[...], NT).astype(BF16)
    packed_ref[:rows, :] = go
    lse, corr = [], []
    for h in range(heads):
        q = q_ref[:rows, col(h)]
        s = jnp.concatenate([s_ref[h], mm(q, kvo_ref[:, col(h)], NT) * SCALE], axis=1)
        s = masked(s, masks)
        peak = jnp.max(s, axis=1, keepdims=True)
        raw = jnp.exp(s - peak)
        total = jnp.sum(raw, axis=1, keepdims=True)
        probs = raw * (1.0 / total)
        p_ref[h] = probs
        low = probs.astype(BF16)
        att = mm(low[:, :near], kvm_ref[:, col(heads + h)])
        att = att + mm(low[:, near:], kvo_ref[:, col(heads + h)])
        att_ref[:, col(h)] = att
        lse.append(peak + jnp.log(total))
        corr.append(jnp.sum(go[:, col(h)].astype(F32) * att, axis=1, keepdims=True))
    pack_rows(packed_ref, rows, heads, corr + lse)


def groups_of(blocks):
    cut = 1 + (blocks - 1) // 2
    return [(0, 1), (1, cut), (cut, blocks)]


def scores_t_body(half, qm_ref, qo_ref, kv_ref, *outs):
    rows = outs[0].shape[1]
    masks = masks_of(half, rows)
    blocks = len(masks) // 2
    for h in range(outs[0].shape[0]):
        k = kv_ref[:rows, col(h)]
        for ref, (lo, hi) in zip(outs, groups_of(blocks)):
            part = slice(lo * rows, hi * rows)
            s = jnp.concatenate(
                [mm(k, qm_ref[part, col(h)], NT), mm(k, qo_ref[part, col(h)], NT)], axis=1
            )
            ref[h] = masked(s * SCALE, masks[lo:hi] + masks[blocks + lo : blocks + hi])


def query_grads(packed_ref, att_ref, p_ref, kvm_ref, kvo_ref, gq_ref):
    rows, width = att_ref.shape
    heads = width // HD
    near = kvm_ref.shape[0]
    for h in range(heads):
        go = packed_ref[:rows, col(h)]
        corr = jnp.sum(go.astype(F32) * att_ref[:, col(h)], axis=1, keepdims=True)
        v = col(heads + h)
        gp = jnp.concatenate([mm(go, kvm_ref[:, v], NT), mm(go, kvo_ref[:, v], NT)], axis=1)
        gs = (SCALE * p_ref[h] * (gp - corr)).astype(BF16)
        gq = mm(gs[:, :near], kvm_ref[:, col(h)]) + mm(gs[:, near:], kvo_ref[:, col(h)])
        gq_ref[:, col(h)] = gq.astype(BF16)


def query_body(packed_ref, att_ref, p_ref, kvm_ref, kvo_ref, wq_ref, part_ref, gq_ref):
    query_grads(packed_ref, att_ref, p_ref, kvm_ref, kvo_ref, gq_ref)
    part_ref[...] = mm(gq_ref[...], wq_ref[...], NT)


def key_terms(got, part, first, pt_in, pt_ref, kv_ref, qm_ref, qo_ref, gow_ref, h):
    rows, width = got[0].shape[0] - PAD, got[0].shape[1]
    near = part.stop - part.start
    corr = unpack_row(got, rows, h, 0)
    if first:
        pt = jnp.exp(pt_in[h] - unpack_row(got, rows, h, 1))
        pt_ref[h] = pt
    else:
        pt = pt_in[h]
    go = gow_ref[:, col(h)]
    gp = mm(kv_ref[:rows, col(width // HD + h)], go, NT)
    gs = (SCALE * pt * (gp - corr)).astype(BF16)
    gk = mm(gs[:, :near], qm_ref[part, col(h)]) + mm(gs[:, near:], qo_ref[part, col(h)])
    return gk, mm(pt.astype(BF16), go)


def key_part_body(span, first, *refs):
    lo, hi = span
    slots = 2 * (hi - lo)
    got = refs[:slots]
    pt_in, kv_ref, qm_ref, qo_ref = refs[slots : slots + 4]
    rest = list(refs[slots + 4 :])
    gow_ref = rest.pop()
    pt_ref = rest.pop() if first else None
    gk_ref, gv_ref = rest[-2:]
    before = rest[:-2]
    rows = got[0].shape[0] - PAD
    for b in range(slots):
        gow_ref[b * rows : (b + 1) * rows, :] = got[b][:rows, :]
    part = slice(lo * rows, hi * rows)
    for h in range(pt_in.shape[0]):
        gk, gv = key_terms(got, part, first, pt_in, pt_ref, kv_ref, qm_ref, qo_ref, gow_ref, h)
        if before:
            gk = gk + before[0][:, col(h)]
            gv = gv + before[1][:, col(h)]
        gk_ref[:, col(h)] = gk
        gv_ref[:, col(h)] = gv


def key_last_body(span, first, halved, *refs):
    lo, hi = span
    slots = 2 * (hi - lo)
    got = refs[:slots]
    pt_in, kv_ref, qm_ref, qo_ref, gk_ref, gv_ref, wk_ref, wv_ref, partq_ref = refs[
        slots : slots + 9
    ]
    part_ref, send_ref = refs[slots + 9 : slots + 11]
    pt_ref = refs[slots + 11] if first else None
    gow_ref, sum_ref = refs[-2:]
    rows = got[0].shape[0] - PAD
    for b in range(slots):
        gow_ref[b * rows : (b + 1) * rows, :] = got[b][:rows, :]
    part = slice(lo * rows, hi * rows)
    gks, gvs = [], []
    for h in range(pt_in.shape[0]):
        gk, gv = key_terms(got, part, first, pt_in, pt_ref, kv_ref, qm_ref, qo_ref, gow_ref, h)
        gks.append((gk_ref[:, col(h)] + gk).astype(BF16))
        gvs.append((gv_ref[:, col(h)] + gv).astype(BF16))
    acc = partq_ref[...] + mm(jnp.concatenate(gks, axis=1), wk_ref[...], NT)
    acc = acc + mm(jnp.concatenate(gvs, axis=1), wv_ref[...], NT)
    if halved:
        cols = part_ref.shape[1]
        sum_ref[...] = acc
        mine, other = feature_slices(2, cols)
        part_ref[...] = sum_ref[:, mine]
        send_ref[...] = sum_ref[:, other].astype(BF16)
    else:
        part_ref[...] = acc
        send_ref[...] = acc.astype(BF16)


def half_rows_body(w_ref, o_ref):
    n = o_ref.shape[0]
    core = lax.axis_index("seq") % 2
    o_ref[...] = w_ref[pl.ds(pl.multiple_of(core * n, n), n), :]


def fold_body(wo_ref, mine_ref, other_ref, gain_ref, wq_ref, wk_ref, wv_ref, ft_ref, full_ref):
    n = mine_ref.shape[0]
    core = lax.axis_index("seq") % 2
    full_ref[pl.ds(pl.multiple_of(core * n, n), n), :] = mine_ref[...]
    full_ref[pl.ds(pl.multiple_of((1 - core) * n, n), n), :] = other_ref[...]
    for i, ref in enumerate((wo_ref, full_ref)):
        scaled = (ref[...].astype(F32) * gain_ref[...]).astype(BF16)
        for j, w in enumerate((wq_ref, wk_ref, wv_ref)):
            ft_ref[i, j] = mm(scaled, w[...]).astype(BF16)


def query_fold_body(packed_ref, att_ref, p_ref, kvm_ref, kvo_ref, ft_ref, gq_ref, own_ref, oth_ref):
    query_grads(packed_ref, att_ref, p_ref, kvm_ref, kvo_ref, gq_ref)
    gq = gq_ref[...]
    own_ref[...] = mm(gq, ft_ref[0, 0], NT)
    oth_ref[...] = mm(gq, ft_ref[1, 0], NT)


def key_fold_body(span, *refs):
    lo, hi = span
    slots = 2 * (hi - lo)
    got = refs[:slots]
    pt_in, kv_ref, qm_ref, qo_ref, gk_in, gv_in, ft_ref, ownq_ref, othq_ref = refs[
        slots : slots + 9
    ]
    own_ref, send_ref, gk_ref, gv_ref, gow_ref = refs[slots + 9 :]
    rows = got[0].shape[0] - PAD
    for b in range(slots):
        gow_ref[b * rows : (b + 1) * rows, :] = got[b][:rows, :]
    part = slice(lo * rows, hi * rows)
    for h in range(pt_in.shape[0]):
        gk, gv = key_terms(got, part, False, pt_in, None, kv_ref, qm_ref, qo_ref, gow_ref, h)
        gk_ref[:, col(h)] = (gk_in[:, col(h)] + gk).astype(BF16)
        gv_ref[:, col(h)] = (gv_in[:, col(h)] + gv).astype(BF16)
    gk, gv = gk_ref[...], gv_ref[...]
    own_ref[...] = ownq_ref[...] + mm(gk, ft_ref[0, 1], NT) + mm(gv, ft_ref[0, 2], NT)
    oth = othq_ref[...] + mm(gk, ft_ref[1, 1], NT) + mm(gv, ft_ref[1, 2], NT)
    send_ref[...] = oth.astype(BF16)


def combine_fold_body(own_ref, recv_ref, inv_ref, att_ref, packed_ref):
    rows, width = att_ref.shape
    go = (inv_ref[:, :1] * (own_ref[...] + recv_ref[...].astype(F32))).astype(BF16)
    packed_ref[:rows, :] = go
    corr = [
        jnp.sum(go[:, col(h)].astype(F32) * att_ref[:, col(h)], axis=1, keepdims=True)
        for h in range(width // HD)
    ]
    pack_rows(packed_ref, rows, width // HD, corr)


def side_body(gq_ref, gk_ref, gv_ref, wq_ref, wk_ref, wv_ref, part_ref, send_ref, sum_ref):
    acc = mm(gq_ref[...], wq_ref[...], NT) + mm(gk_ref[...], wk_ref[...], NT)
    sum_ref[...] = acc + mm(gv_ref[...], wv_ref[...], NT)
    mine, other = feature_slices(2, part_ref.shape[1])
    part_ref[...] = sum_ref[:, mine]
    send_ref[...] = sum_ref[:, other].astype(BF16)


def side_sum_body(part_ref, recv_ref, inv_ref, gain_ref, kry_ref):
    mine = feature_slices(2, part_ref.shape[1])[0]
    vec = part_ref[...] + recv_ref[...].astype(F32)
    kry_ref[...] = inv_ref[:, :1] * (gain_ref[:, mine] * vec)


def combine_body(part_ref, recv_ref, inv_ref, gain_ref, wo_ref, att_ref, *refs):
    kry_ref, packed_ref, vec_ref = refs
    rows, width = att_ref.shape
    cols = kry_ref.shape[1]
    inverse = inv_ref[:, :1]
    vec = inverse * (gain_ref[...] * (part_ref[...] + recv_ref[...].astype(F32)))
    vec_ref[...] = vec
    off = pl.multiple_of(lax.axis_index("tp") * cols, HD)
    kry_ref[...] = vec_ref[:, pl.ds(off, cols)]
    go = mm(vec.astype(BF16), wo_ref[...], NT).astype(BF16)
    packed_ref[:rows, :] = go
    corr = [
        jnp.sum(go[:, col(h)].astype(F32) * att_ref[:, col(h)], axis=1, keepdims=True)
        for h in range(width // HD)
    ]
    pack_rows(packed_ref, rows, width // HD, corr)


def gram_body(part_ref, recv_ref, inv_ref, gain_ref, *refs):
    kry = refs[:SSTEP]
    last_ref, sums_ref, vec_ref = refs[SSTEP:]
    rows, cols = last_ref.shape
    inverse = inv_ref[:, :1]
    own = pl.ds(pl.multiple_of(lax.axis_index("tp") * cols, HD), cols)
    vec = part_ref[...] + recv_ref[...].astype(F32)
    if part_ref.shape[1] != cols:
        vec_ref[...] = vec
        vec = vec_ref[:, own]
    last_ref[...] = inverse * (gain_ref[:, own] * vec)
    all_k = list(kry) + [last_ref]
    count = SSTEP * (SSTEP + 1) // 2 + SSTEP
    acc = [jnp.zeros((8, HD), F32) for _ in range(count)]
    for r in range(0, rows, 8):
        for c in range(0, cols, HD):
            ks = [k[r : r + 8, c : c + HD] for k in all_k]
            ds = [ks[i] - ks[i + 1] for i in range(SSTEP)]
            i = 0
            for a in range(SSTEP):
                for b in range(a + 1):
                    acc[i] = acc[i] + ds[a] * ds[b]
                    i += 1
            for a in range(SSTEP):
                acc[i] = acc[i] + ds[a] * ks[0]
                i += 1
    lane = lax.broadcasted_iota(jnp.int32, (1, HD), 1)
    out = jnp.zeros((1, HD), F32)
    for i in range(count):
        line = jnp.sum(acc[i], axis=0, keepdims=True)
        out = jnp.where(lane == i, jnp.sum(line, axis=1, keepdims=True), out)
    for r in range(sums_ref.shape[0]):
        sums_ref[r] = out


def solve(gram, right):
    n = len(right)
    low = [[None] * n for _ in range(n)]
    for i in range(n):
        for j in range(i + 1):
            run = gram[i][j]
            for k in range(j):
                run = run - low[i][k] * low[j][k]
            low[i][j] = jnp.sqrt(run) if i == j else run / low[j][j]
    mid = []
    for i in range(n):
        run = right[i]
        for j in range(i):
            run = run - low[i][j] * mid[j]
        mid.append(run / low[i][i])
    out = [None] * n
    for i in range(n - 1, -1, -1):
        run = mid[i]
        for j in range(i + 1, n):
            run = run - low[j][i] * out[j]
        out[i] = run / low[i][i]
    return out


def finish_body(sums_ref, *refs):
    kry = refs[: SSTEP + 1]
    adj_ref, res_ref = refs[SSTEP + 1 :]
    total = jnp.sum(sums_ref[...], axis=0)
    lane = lax.broadcasted_iota(jnp.int32, total.shape, 1)
    count = SSTEP * (SSTEP + 1) // 2 + SSTEP
    vals = [
        jnp.sum(jnp.where(lane == i, total, 0.0), axis=1, keepdims=True) for i in range(count)
    ]
    idx = 0
    gram = [[None] * SSTEP for _ in range(SSTEP)]
    for a in range(SSTEP):
        for b in range(a + 1):
            gram[a][b] = vals[idx]
            idx += 1
    right = [vals[idx + a] for a in range(SSTEP)]
    coef = solve(gram, right)
    ks = [k[...] for k in kry]
    adj = coef[0] * ks[0]
    res = ks[0] - coef[0] * (ks[0] - ks[1])
    for i in range(1, SSTEP):
        adj = adj + coef[i] * ks[i]
        res = res - coef[i] * (ks[i] - ks[i + 1])
    adj_ref[...] = adj
    res_ref[...] = res


def swap_partner(c, d, odd):
    return c + d if (c // d) % 2 == odd else c - d


def on_device(state, cotangent, norm_gain, w_query, w_key, w_value, w_out):
    rows, cols = state.shape
    width = w_query.shape[1]
    heads = width // HD
    half = WIN // 2
    seq = lax.axis_size("seq")
    tps = lax.axis_size("tp")
    chips = seq // 2
    hops = hops_of(half, rows)
    blocks = 1 + len(hops)
    groups = groups_of(blocks)
    wide = [2 * (hi - lo) * rows for lo, hi in groups]
    ranks = seq * tps
    full = tps * cols

    def swap_core(x):
        return lax.ppermute(x, "seq", [(i, i ^ 1) for i in range(seq)])

    def tp_blocks(x):
        out = [x]
        for k in range(1, tps):
            out.append(lax.ppermute(x, "tp", [((i + k) % tps, i) for i in range(tps)]))
        return out

    def hop(x, i):
        d, odd = hops[i]
        pairs = []
        for c in range(chips):
            q = swap_partner(c, d, odd)
            if 0 <= q < chips:
                pairs += [(2 * c, 2 * q), (2 * c + 1, 2 * q + 1)]
            else:
                pairs += [(2 * c, 2 * c + 1), (2 * c + 1, 2 * c)]
        return lax.ppermute(x, "seq", pairs)

    def fetch(x):
        return [x] + [hop(x, i) for i in range(len(hops))]

    raw = len(hops) // 2
    states = tp_blocks(state)
    pieces = []
    for i in range(raw):
        pieces += tp_blocks(hop(state, i))
    cot_low, states[0], gain = kernel_call(
        early_body,
        [sds(rows, cols, dtype=BF16), state, sds(1, full)],
        [cotangent, state, norm_gain[None, :]],
    )
    normed, inv = kernel_call(
        functools.partial(norm_body, tps),
        [sds(rows, full, dtype=BF16), sds(rows, HD)],
        states + [gain],
    )
    done = [normed] + [hop(normed, i) for i in range(raw, len(hops))]
    held = [w_query, w_key, w_value, w_out]
    w_query, w_key, w_value, w_out = kernel_call(
        prep_body,
        held,
        held,
        scratch=[pltpu.SemaphoreType.DMA((len(held),))],
        hbm=len(held),
        limit=49 << 20,
    )
    cots = tp_blocks(cot_low)
    shapes = [
        sds(blocks * rows, 2 * width, dtype=BF16),
        sds(blocks * rows, full, dtype=BF16),
    ]
    kv_mine, normed = kernel_call(
        functools.partial(kv_first_body, raw, len(done)), shapes, done + [w_key, w_value]
    )
    inputs = pieces + [gain, w_key, w_value]
    kv_mine, normed = kernel_call(
        functools.partial(kv_rest_body, raw, tps),
        shapes,
        inputs + [kv_mine, normed],
        aliases={len(inputs): 0, len(inputs) + 1: 1},
    )
    kv_other = swap_core(kv_mine)
    q_mine, s_mine = kernel_call(
        functools.partial(q_body, rows),
        [sds(blocks * rows, width, dtype=BF16), sds(heads, rows, blocks * rows)],
        [normed, w_query, kv_mine],
    )
    q_other = swap_core(q_mine)
    probs, att, packed = kernel_call(
        functools.partial(stats_body, half, tps),
        [sds(heads, rows, 2 * blocks * rows), sds(rows, width), sds(rows + PAD, width, dtype=BF16)],
        cots + [kv_mine, kv_other, q_mine, s_mine, w_out],
        scratch=[pltpu.VMEM((rows, full), BF16)],
    )
    fold = tps == 2
    if fold:
        (wo_half,) = kernel_call(half_rows_body, [sds(width // 2, full, dtype=BF16)], [w_out])
        wo_mine = tp_blocks(wo_half)[1]
    krylov = [cotangent]
    side = None
    for n in range(SSTEP):
        first, last = n == 0, n == SSTEP - 1
        if first:
            pts = kernel_call(
                functools.partial(scores_t_body, half),
                [sds(heads, rows, w) for w in wide],
                [q_mine, q_other, kv_mine],
            )
        got = fetch(packed)
        got = got + [swap_core(x) for x in got]
        folded = fold and 1 <= n < SSTEP - 1
        if side is not None:
            mine, other = side
            other = tp_blocks(other)[1]
            (kry,) = kernel_call(
                side_sum_body, [sds(rows, cols)], [mine, other, inv, gain]
            )
            krylov.append(kry)
            side = None
        inputs = [packed, att, probs, kv_mine, kv_other]
        if folded:
            gq, *part_q = kernel_call(
                query_fold_body,
                [sds(rows, width, dtype=BF16), sds(rows, width), sds(rows, width)],
                inputs + [folds],
            )
        else:
            part_q = kernel_call(
                query_body,
                [sds(rows, full)],
                inputs + [w_query],
                scratch=[pltpu.VMEM((rows, width), BF16)],
            )
        static = [kv_mine, q_mine, q_other]
        grads = []
        new_pts = []
        for g in range(2):
            lo, hi = groups[g]
            res = kernel_call(
                functools.partial(key_part_body, groups[g], first),
                [sds(rows, width), sds(rows, width)]
                + ([sds(heads, rows, wide[g])] if first else []),
                got[lo:hi] + got[blocks + lo : blocks + hi] + [pts[g]] + static + grads,
                scratch=[pltpu.VMEM((wide[g], width), BF16)],
            )
            grads = list(res[:2])
            new_pts += list(res[2:])
        halved = last and tps == 2
        span = cols if halved else full
        lo, hi = groups[2]
        if folded:
            own, send, gk, gv = kernel_call(
                functools.partial(key_fold_body, groups[2]),
                [sds(rows, width), sds(rows, width, dtype=BF16)]
                + [sds(rows, width, dtype=BF16)] * 2,
                got[lo:hi]
                + got[blocks + lo : blocks + hi]
                + [pts[2]]
                + static
                + grads
                + [folds]
                + list(part_q),
                scratch=[pltpu.VMEM((wide[2], width), BF16)],
            )
            recv = tp_blocks(send)[1]
            (packed,) = kernel_call(
                combine_fold_body,
                [sds(rows + PAD, width, dtype=BF16)],
                [own, recv, inv, att],
            )
            side = kernel_call(
                side_body,
                [sds(rows, cols), sds(rows, cols, dtype=BF16)],
                [gq, gk, gv, w_query, w_key, w_value],
                scratch=[pltpu.VMEM((rows, full), F32)],
            )
            continue
        res = kernel_call(
            functools.partial(key_last_body, groups[2], first, halved),
            [sds(rows, span), sds(rows, span, dtype=BF16)]
            + ([sds(heads, rows, wide[2])] if first else []),
            got[lo:hi]
            + got[blocks + lo : blocks + hi]
            + [pts[2]]
            + static
            + grads
            + [w_key, w_value]
            + list(part_q),
            scratch=[pltpu.VMEM((wide[2], width), BF16), pltpu.VMEM((rows, full), F32)],
        )
        part, send = res[:2]
        if first:
            pts = new_pts + list(res[2:])
        k = 1
        while True:
            recv = lax.ppermute(send, "tp", [(i, i ^ k) for i in range(tps)])
            k *= 2
            if k >= tps:
                break
            part = part + recv.astype(F32)
            send = part.astype(BF16)
        if fold and first:
            wo_other = swap_core(wo_mine)
            (folds,) = kernel_call(
                fold_body,
                [sds(2, 3, width, width, dtype=BF16)],
                [w_out, wo_mine, wo_other, gain, w_query, w_key, w_value],
                scratch=[pltpu.VMEM((width, full), BF16)],
                limit=16 << 20,
            )
        if not last:
            kry, packed = kernel_call(
                combine_body,
                [sds(rows, cols), sds(rows + PAD, width, dtype=BF16)],
                [part, recv, inv, gain, w_out, att],
                scratch=[pltpu.VMEM((rows, full), F32)],
            )
        else:
            kry, sums = kernel_call(
                gram_body,
                [sds(rows, cols), sds(ranks, 1, HD)],
                [part, recv, inv, gain] + krylov,
                scratch=[pltpu.VMEM((rows, full), F32)],
            )
        krylov.append(kry)
    sums = lax.all_to_all(sums, ("seq", "tp"), 0, 0)
    adjoint, residual = kernel_call(
        finish_body,
        [sds(rows, cols), sds(rows, cols)],
        [sums] + krylov,
    )
    return (adjoint, residual)


def solution(mesh):
    in_specs = (
        P("seq", "tp"),
        P("seq", "tp"),
        P(),
        P(None, "tp"),
        P(None, "tp"),
        P(None, "tp"),
        P("tp", None),
    )
    out_specs = (P("seq", "tp"), P("seq", "tp"))
    return jax.shard_map(
        on_device, mesh=mesh, in_specs=in_specs, out_specs=out_specs, check_vma=False
    )
```
